128 devices in a mesh: gx: 8 (over x, core), gy: 16 (over z, y).
Axes of the slice: x: 4, y: 4, z: 4, core: 2. Of those that a mesh axis runs over, the one named last changes fastest.
Arguments:
- blade_state: float32 [5, 8, 524288], P(None, 'gx', 'gy'), may hold values from -6 to 6
- back_state: float32 [5, 128, 8192], P(None, 'gx', 'gy'), may hold values from -6 to 6
- blade_cotangent: float32 [5, 8, 524288], P(None, 'gx', 'gy'), may hold values from -6 to 6
- back_cotangent: float32 [5, 128, 8192], P(None, 'gx', 'gy'), may hold values from -6 to 6
- blade_flux: float32 [3, 5, 5], replicated, may hold values from -3 to 3
- back_flux: float32 [3, 5, 5], replicated, may hold values from -3 to 3
- blade_owner: int32 [2, 131072, 1], P(None, ('gx', 'gy')), may hold values from 0 to 127; in each aligned block of 1024 rows (0 to 1023, 1024 to 2047, ..., all dimensions but the last counted through in order) at most 16 rows name the same one
- back_donor_cell: int32 [2, 262144], P(None, ('gx', 'gy')), may hold values from 32 to 7614, as said below
- back_donor_weight: float32 [2, 8, 262144], P(None, None, ('gx', 'gy')), may hold values from 0 to 1, as said below
- hole_cell: int32 [2, 262144], P(None, ('gx', 'gy')), may hold values from 0 to 8159, as said below
- hole_owner: int32 [2, 262144, 1], P(None, ('gx', 'gy')), may hold values from 0 to 127; in each aligned block of 2048 rows (0 to 2047, 2048 to 4095, ..., all dimensions but the last counted through in order) at most 32 rows name the same one
- blade_donor_cell: int32 [2, 524288], P(None, ('gx', 'gy')), may hold values from 0 to 24190, as said below
- blade_donor_weight: float32 [2, 8, 524288], P(None, None, ('gx', 'gy')), may hold values from 0 to 1, as said below
Outputs:
- blade_adjoint: float32 [5, 8, 524288], P(None, 'gx', 'gy')
- back_adjoint: float32 [5, 128, 8192], P(None, 'gx', 'gy')
The draws below stay inside these ranges and needn't reach their ends.
Inputs may be any that keep to these rules, and one draw needn't show every extreme that they name: `blade_owner`: in each step, at most 16 rim receivers of one device name the same owner. `hole_owner`: in each step, at most 32 hole receivers of one device name the same owner. `back_donor_cell`: local cell number (x * 8 + y) * 64 + z of the owner's block with x < 15, y < 7 and 32 <= z < 63. `blade_donor_cell`: local cell number (j * 64 + k) * 128 + i of the owner's blade block with j < 3, k < 61 and i < 127. `hole_cell`: in each step the 2048 cells of one device are distinct local cell numbers (x * 8 + y) * 64 + z of that device with z < 32. `back_donor_weight`: trilinear weights: products of three fractions, nonnegative, summing to one over the 8 corners of each slot. `blade_donor_weight`: trilinear weights: products of three fractions, nonnegative, summing to one over the 8 corners of each slot.
All inputs are finite; a program needn't handle non-finite values.
Results may differ from the reference program's by a relative error of at most 0.0003.
Values sent between devices are 32-bit elements; how exact they have to be, the bound alone decides.
No kernel may reach another device: no remote copies, remote signals or barrier semaphores. Data moves between devices by JAX's collectives and lax.ppermute only.
A program may use at most 384 MiB of HBM per device.

```python
import math
import jax
import jax.numpy as jnp
import numpy as np
from jax import lax

WRAP_DEV = 4
WALL_CELLS = 64
CHORD_CELLS = 128
EAST_DEV = 16
NORTH_DEV = 8
VERT_CELLS = 64
HOLE_DEV = 2048
REVERSE_STEPS = 2
BLADES = 8
WRAP_CELLS = 64
EAST_CELLS = 128
NORTH_CELLS = 128
RIM_DEV = 1024
CAP_RIM = 16
CAP_HOLE = 32
RIM_ALL = 131072
HOLE_ALL = 262144
RIM_SLOTS = 262144
HOLE_SLOTS = 524288
N_GX = 8
N_GY = 16


def trilinear(key, slot_count):
    fractions = jax.random.uniform(key, (REVERSE_STEPS, 3, slot_count), jnp.float32)
    corners = []
    for corner in range(8):
        factor = jnp.ones((REVERSE_STEPS, slot_count), jnp.float32)
        for position in range(3):
            picked = corner >> 2 - position & 1
            if picked == 1:
                factor = factor * fractions[:, position]
            else:
                factor = factor * (1.0 - fractions[:, position])
        corners.append(factor)
    return jnp.stack(corners, axis=1)


def draw_back_donor_weight(key, part):
    return trilinear(jax.random.fold_in(key, 11), RIM_SLOTS)


def draw_blade_donor_weight(key, part):
    return trilinear(jax.random.fold_in(key, 12), HOLE_SLOTS)


def draw_back_donor_cell(key, part):
    sub_keys = jax.random.split(jax.random.fold_in(key, 21), 3)
    shape_out = (REVERSE_STEPS, RIM_SLOTS)
    east_pos = jax.random.randint(sub_keys[0], shape_out, 0, EAST_DEV - 1)
    north_pos = jax.random.randint(sub_keys[1], shape_out, 0, NORTH_DEV - 1)
    vert_pos = jax.random.randint(sub_keys[2], shape_out, VERT_CELLS // 2, VERT_CELLS - 1)
    return ((east_pos * NORTH_DEV + north_pos) * VERT_CELLS + vert_pos).astype(jnp.int32)


def draw_blade_donor_cell(key, part):
    sub_keys = jax.random.split(jax.random.fold_in(key, 22), 3)
    shape_out = (REVERSE_STEPS, HOLE_SLOTS)
    wrap_pos = jax.random.randint(sub_keys[0], shape_out, 0, WRAP_DEV - 1)
    wall_pos = jax.random.randint(sub_keys[1], shape_out, 0, WALL_CELLS - 3)
    chord_pos = jax.random.randint(sub_keys[2], shape_out, 0, CHORD_CELLS - 1)
    return ((wrap_pos * WALL_CELLS + wall_pos) * CHORD_CELLS + chord_pos).astype(jnp.int32)


def draw_hole_cell(key, part):
    device_count = HOLE_ALL // HOLE_DEV
    half_vert = VERT_CELLS // 2
    region = EAST_DEV * NORTH_DEV * half_vert
    sub_keys = jax.random.split(jax.random.fold_in(key, 31), REVERSE_STEPS * device_count)
    chosen = jax.vmap(lambda sub_key: jax.random.permutation(sub_key, region)[:HOLE_DEV])(sub_keys)
    chosen = chosen.astype(jnp.int32)
    east_pos = chosen // (NORTH_DEV * half_vert)
    remainder = chosen % (NORTH_DEV * half_vert)
    north_pos = remainder // half_vert
    vert_pos = remainder % half_vert
    cell_list = (east_pos * NORTH_DEV + north_pos) * VERT_CELLS + vert_pos
    return cell_list.reshape(REVERSE_STEPS, HOLE_ALL).astype(jnp.int32)


def shard_levels(stream_key, shape, cuts, least, high):
    level = 1.0
    for dim, blocks in cuts:
        draws = jax.random.uniform(jax.random.fold_in(jax.random.fold_in(stream_key, 6), dim), (blocks,), jnp.float32, least / len(cuts), high / len(cuts))
        level = level * jnp.repeat(jnp.exp(draws), shape[dim] // blocks).reshape((-1,) + (1,) * (len(shape) - 1 - dim))
    return level


def assign_block(key, own, number, rows, count, top, limit, lean):
    sequence = jax.random.permutation(key, count)
    packed, common = load_shares(count, rows * top, limit, lean, True), load_shares(count, rows * top, limit, lean, False)
    places = jnp.arange(count)

    def named(lengths, rotation):
        used = int((lengths > 0).sum())
        fixed = max(1, used // 4)
        passed = fixed + (places - fixed + rotation * (used - fixed)) % max(1, count - fixed)
        return jnp.zeros((count,), jnp.int32).at[sequence[jnp.where(places < fixed, places, passed)]].set(jnp.asarray(lengths, jnp.int32))

    lengths = jnp.where(number % 4 == 0, named(packed, number // 4), named(common, number - number // 4 - 1))
    mixed = jax.random.permutation(jax.random.fold_in(own, 3), count)
    source_of, sink = mixed[0:count // 2 * 2:2], mixed[1:count // 2 * 2:2]
    slack = jnp.minimum(lengths[source_of] - 1, limit - lengths[sink]) // 2
    slack = jnp.where((source_of == sequence[0]) | (sink == sequence[0]) | (lengths[sink] == 0), 0, jnp.maximum(slack, 0))
    passed = jax.random.randint(jax.random.fold_in(own, 4), (count // 2,), 0, 1 << 20) % (slack + 1)
    lengths = lengths.at[source_of].add(-passed).at[sink].add(passed)
    items = jnp.searchsorted(jnp.cumsum(lengths), jnp.arange(rows * top), side="right").astype(jnp.int32)
    table = items.reshape(top, rows).T
    table = table[jax.random.permutation(jax.random.fold_in(own, 1), rows)]
    rotation = jax.random.randint(jax.random.fold_in(own, 2), (rows, 1), 0, top)
    return jnp.take_along_axis(table, (jnp.arange(top)[None, :] + rotation) % top, axis=1)


def load_shares(amount, total, limit, lean, full):
    weights = [(1 << 20) // math.isqrt(standing ** lean) + 1 for standing in range(1, amount + 1)]
    largest = limit if full else min(limit, max(-(-total // amount), total * weights[0] // sum(weights)))
    least = 1 if total - largest >= amount - 1 else 0
    counts, surplus = [largest] + [least] * (amount - 1), total - largest - least * (amount - 1)
    while surplus > 0:
        candidates = [i for i in range(1, amount) if counts[i] < largest] or [i for i in range(1, amount) if counts[i] < limit]
        mass, left = sum([weights[i] for i in candidates]), surplus
        for i in candidates:
            extra = min(limit - counts[i], max(1, left * weights[i] // mass), surplus)
            counts[i] = counts[i] + extra
            surplus = surplus - extra
    return np.array(counts)


def noise(key, dims, width, most, cuts=(), kind=jnp.bfloat16):
    values = jax.random.normal(key, dims, jnp.float32) * width
    if len(cuts) > 0:
        values = shard_levels(key, dims, cuts, -0.22, 0.18) * values
    return jnp.clip(values, min=-most, max=most).astype(kind)


def setup_inputs(seed: int = 0) -> dict:
    arg_keys = jax.random.split(jax.random.key(seed), 14)
    blade_state = noise(arg_keys[0], (5, BLADES, WRAP_CELLS * WALL_CELLS * CHORD_CELLS), 1.0, 6.0, ((1, 8), (2, 16)), jnp.float32)
    back_state = noise(arg_keys[1], (5, EAST_CELLS, NORTH_CELLS * VERT_CELLS), 1.0, 6.0, ((1, 8), (2, 16)), jnp.float32)
    blade_cotangent = noise(arg_keys[2], (5, BLADES, WRAP_CELLS * WALL_CELLS * CHORD_CELLS), 1.0, 6.0, ((1, 8), (2, 16)), jnp.float32)
    back_cotangent = noise(arg_keys[3], (5, EAST_CELLS, NORTH_CELLS * VERT_CELLS), 1.0, 6.0, ((1, 8), (2, 16)), jnp.float32)
    blade_flux = noise(arg_keys[4], (3, 5, 5), 0.5, 3.0, (), jnp.float32)
    back_flux = noise(arg_keys[5], (3, 5, 5), 0.5, 3.0, (), jnp.float32)
    blade_owner_keys = jax.random.split(jax.random.fold_in(arg_keys[6], 1), REVERSE_STEPS * RIM_ALL // RIM_DEV)
    blade_owner_turns = jax.random.permutation(jax.random.fold_in(arg_keys[6], 3), REVERSE_STEPS * RIM_ALL // RIM_DEV)
    blade_owner = jax.vmap(lambda own, number: assign_block(jax.random.fold_in(arg_keys[6], 2), own, number, RIM_DEV, N_GX * N_GY, 1, CAP_RIM, 2))(blade_owner_keys, blade_owner_turns).reshape((REVERSE_STEPS, RIM_ALL, 1))
    back_donor_cell = draw_back_donor_cell(jax.random.fold_in(arg_keys[13], 71), 0)
    back_donor_weight = draw_back_donor_weight(jax.random.fold_in(arg_keys[13], 71), 0)
    hole_cell = draw_hole_cell(jax.random.fold_in(arg_keys[13], 71), 0)
    hole_owner_keys = jax.random.split(jax.random.fold_in(arg_keys[10], 1), REVERSE_STEPS * HOLE_ALL // HOLE_DEV)
    hole_owner_turns = jax.random.permutation(jax.random.fold_in(arg_keys[10], 3), REVERSE_STEPS * HOLE_ALL // HOLE_DEV)
    hole_owner = jax.vmap(lambda own, number: assign_block(jax.random.fold_in(arg_keys[10], 2), own, number, HOLE_DEV, N_GX * N_GY, 1, CAP_HOLE, 2))(hole_owner_keys, hole_owner_turns).reshape((REVERSE_STEPS, HOLE_ALL, 1))
    blade_donor_cell = draw_blade_donor_cell(jax.random.fold_in(arg_keys[13], 71), 0)
    blade_donor_weight = draw_blade_donor_weight(jax.random.fold_in(arg_keys[13], 71), 0)
    return {"blade_state": blade_state, "back_state": back_state, "blade_cotangent": blade_cotangent, "back_cotangent": back_cotangent, "blade_flux": blade_flux, "back_flux": back_flux, "blade_owner": blade_owner, "back_donor_cell": back_donor_cell, "back_donor_weight": back_donor_weight, "hole_cell": hole_cell, "hole_owner": hole_owner, "blade_donor_cell": blade_donor_cell, "blade_donor_weight": blade_donor_weight}


exact_mode = lax.Precision.HIGHEST
time_step = 0.2
damping = 0.1


def face_slice(padded, axis_pos, shift):
    pieces = [slice(None)] * (padded.ndim - 3)
    for position in range(3):
        if position == axis_pos:
            length = padded.shape[padded.ndim - 3 + position] - 2
            pieces.append(slice(shift, shift + length))
        else:
            pieces.append(slice(1, -1))
    return padded[tuple(pieces)]


def flux_apply(matrices, direction, states):
    linear = jnp.einsum("ce,e...->c...", matrices[direction], states, precision=exact_mode)
    return linear + states[1 + direction] * states


def residual_of(padded, matrices):
    center = face_slice(padded, 0, 1)
    summed = jnp.zeros_like(center)
    for direction in range(3):
        upper_side = face_slice(padded, direction, 2)
        lower_side = face_slice(padded, direction, 0)
        summed = summed + 0.5 * (flux_apply(matrices, direction, upper_side) - flux_apply(matrices, direction, lower_side))
        summed = summed - damping * (upper_side - 2.0 * center + lower_side)
    return summed


def adjoint_of(states, padded, matrices):
    center = face_slice(padded, 0, 1)
    summed = jnp.zeros_like(center)
    for direction in range(3):
        upper_side = face_slice(padded, direction, 2)
        lower_side = face_slice(padded, direction, 0)
        jump_half = 0.5 * (lower_side - upper_side)
        turned = jnp.einsum("ec,e...->c...", matrices[direction], jump_half, precision=exact_mode)
        turned = turned + states[1 + direction] * jump_half
        contracted = jnp.sum(states * jump_half, axis=0)
        turned = turned.at[1 + direction].add(contracted)
        summed = summed + turned - damping * (upper_side - 2.0 * center + lower_side)
    return summed


def blade_grid(field_in):
    shaped = field_in.reshape(5, BLADES, WRAP_CELLS, WALL_CELLS, CHORD_CELLS)
    shaped = jnp.pad(shaped, ((0, 0), (0, 0), (1, 1), (0, 0), (0, 0)), mode="wrap")
    return jnp.pad(shaped, ((0, 0), (0, 0), (0, 0), (1, 1), (1, 1)))


def back_grid(field_in):
    shaped = field_in.reshape(5, EAST_CELLS, NORTH_CELLS, VERT_CELLS)
    return jnp.pad(shaped, ((0, 0), (1, 1), (1, 1), (1, 1)))


def blade_split(field_in):
    shaped = field_in.reshape(5, BLADES, N_GY, -1)
    return shaped.transpose(1, 2, 0, 3).reshape(BLADES * N_GY, 5, -1)


def blade_join(blocks):
    shaped = blocks.reshape(BLADES, N_GY, 5, -1)
    return shaped.transpose(2, 0, 1, 3).reshape(5, BLADES, -1)


def back_split(field_in):
    shaped = field_in.reshape(5, N_GX, EAST_DEV, N_GY, NORTH_DEV * VERT_CELLS)
    return shaped.transpose(1, 3, 0, 2, 4).reshape(N_GX * N_GY, 5, -1)


def back_join(blocks):
    shaped = blocks.reshape(N_GX, N_GY, 5, EAST_DEV, NORTH_DEV * VERT_CELLS)
    return shaped.transpose(2, 0, 3, 1, 4).reshape(5, EAST_CELLS, NORTH_CELLS * VERT_CELLS)


def slot_address(owner_rows, capacity):
    def one_device(owner_row):
        ordering = jnp.argsort(owner_row, stable=True).astype(jnp.int32)
        ordered = owner_row[ordering]
        starts = jnp.searchsorted(ordered, ordered, side="left").astype(jnp.int32)
        rank_sorted = jnp.arange(owner_row.shape[0], dtype=jnp.int32) - starts
        rank_list = jnp.zeros_like(owner_row).at[ordering].set(rank_sorted)
        return owner_row * capacity + rank_list
    return jax.vmap(one_device)(owner_rows)


def corner_offset(corner, strides):
    return (corner // 4) * strides[0] + (corner // 2 % 2) * strides[1] + (corner % 2) * strides[2]


def interpolate(blocks, base_cell, weights, strides):
    def one_device(values, base_rows, weight_rows):
        summed = jnp.zeros((values.shape[0], base_rows.shape[0]), jnp.float32)
        for corner in range(8):
            summed = summed + weight_rows[corner][None, :] * values[:, base_rows + corner_offset(corner, strides)]
        return summed
    return jax.vmap(one_device)(blocks, base_cell, weights)


def spread(blocks, base_cell, weights, strides, arrived):
    def one_device(values, base_rows, weight_rows, incoming):
        for corner in range(8):
            values = values.at[:, base_rows + corner_offset(corner, strides)].add(weight_rows[corner][None, :] * incoming)
        return values
    return jax.vmap(one_device)(blocks, base_cell, weights, arrived)


def transfer(sent):
    devices = sent.shape[0]
    return sent.reshape(devices, 5, devices, -1).transpose(2, 1, 0, 3).reshape(devices, 5, -1)


def fill_fringe(blade_blocks, back_blocks, step_table, strides_pair):
    rim_address, hole_address, hole_list, back_base, back_weight, blade_base, blade_weight = step_table
    devices = blade_blocks.shape[0]
    rim_values = transfer(interpolate(back_blocks, back_base, back_weight, strides_pair[1]))
    hole_values = transfer(interpolate(blade_blocks, blade_base, blade_weight, strides_pair[0]))
    rim_fill = jax.vmap(lambda arrived, address: arrived[:, address])(rim_values, rim_address)
    hole_fill = jax.vmap(lambda arrived, address: arrived[:, address])(hole_values, hole_address)
    shaped = blade_blocks.reshape(devices, 5, WRAP_DEV, WALL_CELLS, CHORD_CELLS)
    shaped = shaped.at[:, :, :, WALL_CELLS - 2:, :].set(rim_fill.reshape(devices, 5, WRAP_DEV, 2, CHORD_CELLS))
    back_filled = jax.vmap(lambda values, cell_list, fill_values: values.at[:, cell_list].set(fill_values))(back_blocks, hole_list, hole_fill)
    return shaped.reshape(devices, 5, -1), back_filled


def transpose_fringe(blade_blocks, back_blocks, step_table, strides_pair):
    rim_address, hole_address, hole_list, back_base, back_weight, blade_base, blade_weight = step_table
    devices = blade_blocks.shape[0]
    shaped = blade_blocks.reshape(devices, 5, WRAP_DEV, WALL_CELLS, CHORD_CELLS)
    rim_cot = shaped[:, :, :, WALL_CELLS - 2:, :].reshape(devices, 5, -1)
    blade_kept = shaped.at[:, :, :, WALL_CELLS - 2:, :].set(0.0).reshape(devices, 5, -1)
    rim_sent = jax.vmap(lambda values, address: jnp.zeros((5, 2 * RIM_DEV), jnp.float32).at[:, address].set(values))(rim_cot, rim_address)
    hole_cot = jax.vmap(lambda values, cell_list: values[:, cell_list])(back_blocks, hole_list)
    back_kept = jax.vmap(lambda values, cell_list: values.at[:, cell_list].set(0.0))(back_blocks, hole_list)
    hole_sent = jax.vmap(lambda values, address: jnp.zeros((5, 2 * HOLE_DEV), jnp.float32).at[:, address].set(values))(hole_cot, hole_address)
    rim_arrived = transfer(rim_sent)
    hole_arrived = transfer(hole_sent)
    back_out = spread(back_kept, back_base, back_weight, strides_pair[1], rim_arrived)
    blade_out = spread(blade_kept, blade_base, blade_weight, strides_pair[0], hole_arrived)
    return blade_out, back_out


def reference(blade_state, back_state, blade_cotangent, back_cotangent, blade_flux, back_flux, blade_owner, back_donor_cell, back_donor_weight, hole_cell, hole_owner, blade_donor_cell, blade_donor_weight):
    devices = N_GX * N_GY
    strides_pair = ((WALL_CELLS * CHORD_CELLS, CHORD_CELLS, 1), (NORTH_DEV * VERT_CELLS, VERT_CELLS, 1))
    tables = []
    for step_index in range(REVERSE_STEPS):
        tables.append((
            slot_address(blade_owner[step_index, :, 0].reshape(devices, RIM_DEV), CAP_RIM),
            slot_address(hole_owner[step_index, :, 0].reshape(devices, HOLE_DEV), CAP_HOLE),
            hole_cell[step_index].reshape(devices, HOLE_DEV),
            back_donor_cell[step_index].reshape(devices, 2 * RIM_DEV),
            back_donor_weight[step_index].reshape(8, devices, 2 * RIM_DEV).transpose(1, 0, 2),
            blade_donor_cell[step_index].reshape(devices, 2 * HOLE_DEV),
            blade_donor_weight[step_index].reshape(8, devices, 2 * HOLE_DEV).transpose(1, 0, 2)))
    blade_shape = (5, BLADES, WRAP_CELLS, WALL_CELLS, CHORD_CELLS)
    back_shape = (5, EAST_CELLS, NORTH_CELLS, VERT_CELLS)
    blade_blocks, back_blocks = fill_fringe(blade_split(blade_state), back_split(back_state), tables[0], strides_pair)
    blade_first = blade_join(blade_blocks)
    back_first = back_join(back_blocks)
    blade_next = blade_first - time_step * residual_of(blade_grid(blade_first), blade_flux).reshape(blade_first.shape)
    back_next = back_first - time_step * residual_of(back_grid(back_first), back_flux).reshape(back_first.shape)
    blade_blocks, back_blocks = fill_fringe(blade_split(blade_next), back_split(back_next), tables[1], strides_pair)
    blade_second = blade_join(blade_blocks)
    back_second = back_join(back_blocks)
    blade_mu = blade_cotangent - time_step * adjoint_of(blade_second.reshape(blade_shape), blade_grid(blade_cotangent), blade_flux).reshape(blade_cotangent.shape)
    back_mu = back_cotangent - time_step * adjoint_of(back_second.reshape(back_shape), back_grid(back_cotangent), back_flux).reshape(back_cotangent.shape)
    blade_blocks, back_blocks = transpose_fringe(blade_split(blade_mu), back_split(back_mu), tables[1], strides_pair)
    blade_mid = blade_join(blade_blocks)
    back_mid = back_join(back_blocks)
    blade_mu = blade_mid - time_step * adjoint_of(blade_first.reshape(blade_shape), blade_grid(blade_mid), blade_flux).reshape(blade_mid.shape)
    back_mu = back_mid - time_step * adjoint_of(back_first.reshape(back_shape), back_grid(back_mid), back_flux).reshape(back_mid.shape)
    blade_blocks, back_blocks = transpose_fringe(blade_split(blade_mu), back_split(back_mu), tables[0], strides_pair)
    return blade_join(blade_blocks), back_join(back_blocks)
```

```python
import functools

import jax
import jax.numpy as jnp
from jax import lax
from jax.experimental import pallas as pl
from jax.experimental.pallas import tpu as pltpu
from jax.sharding import PartitionSpec as P

DEVS = 128
WRAP = 4
WALL = 64
CHORD = 128
EAST = 16
NORTH = 8
VERT = 64
HALF = VERT // 2
RIMS = 1024
HOLES = 2048
QR = 2 * RIMS // DEVS
QH = 2 * HOLES // DEVS
FIELDS = 17

time_step = 0.2
damping = 0.1

F32 = jnp.float32
BF16 = jnp.bfloat16


def split(x):
    hi = x.astype(BF16)
    return hi, (x - hi.astype(F32)).astype(BF16)


def dot_nn(a, b):
    return lax.dot_general(a, b, (((1,), (0,)), ((), ())), preferred_element_type=F32)


def dot_nt(a, b):
    return lax.dot_general(a, b, (((1,), (1,)), ((), ())), preferred_element_type=F32)


def iota(shape, dim):
    return lax.broadcasted_iota(jnp.int32, shape, dim)


def one_hot(rows, index):
    return jnp.where(iota((rows, index.shape[1]), 0) == index, 1.0, 0.0)


def pair_hot(rows, index, first, second):
    position = iota((rows, index.shape[1]), 0)
    return jnp.where(position == index, first, jnp.where(position == index + 1, second, 0.0))


def lane_roll(x, amount):
    amount = amount % x.shape[-1]
    return pltpu.roll(x, amount, x.ndim - 1) if amount else x


def to_planes(block):
    rows = [block[:, y * VERT : (y + 1) * VERT] for y in range(NORTH)]
    return jnp.concatenate(rows, axis=0).T


def from_planes(field):
    turned = field.T
    return [turned[y * EAST : (y + 1) * EAST, :] for y in range(NORTH)]


def donor_parts(weights):
    w = [weights[corner : corner + 1, :] for corner in range(8)]
    x0 = (w[0] + w[1]) + (w[2] + w[3])
    x1 = (w[4] + w[5]) + (w[6] + w[7])
    y0 = (w[0] + w[1]) + (w[4] + w[5])
    y1 = (w[2] + w[3]) + (w[6] + w[7])
    z0 = (w[0] + w[2]) + (w[4] + w[6])
    z1 = (w[1] + w[3]) + (w[5] + w[7])
    return x0, x1, y0, y1, z0, z1


def blade_donors(base, weights):
    x0, x1, y0, y1, z0, z1 = donor_parts(weights)
    wrap = pair_hot(WRAP, base >> 13, x0, x1)
    wall = pair_hot(WALL, (base >> 7) & (WALL - 1), y0, y1)
    rows = jnp.concatenate([wrap[j : j + 1, :] * wall for j in range(WRAP)], axis=0)
    return split(rows), pair_hot(CHORD, base & (CHORD - 1), z0, z1)


def back_donors(base, weights):
    x0, x1, y0, y1, z0, z1 = donor_parts(weights)
    east = pair_hot(EAST, base >> 9, x0, x1)
    north = pair_hot(NORTH, (base >> 6) & (NORTH - 1), y0, y1)
    rows = jnp.concatenate([north[y : y + 1, :] * east for y in range(NORTH)], axis=0)
    return split(rows), pair_hot(HALF, (base & (VERT - 1)) - HALF, z0, z1)


def picked(parts, rows, cols):
    (hi, lo), (row_hi, row_lo) = parts, rows
    table = dot_nn(hi, row_hi) + (dot_nn(hi, row_lo) + dot_nn(lo, row_hi))
    return jnp.sum(table * cols, axis=0, keepdims=True)


def spread_terms(rows, terms):
    (row_hi, row_lo), (hi, lo) = rows, split(terms)
    return dot_nt(row_hi, hi) + (dot_nt(row_hi, lo) + dot_nt(row_lo, hi))


def wall_shift(v, up):
    position = iota(v.shape, 0)
    if up:
        return jnp.where(position == v.shape[0] - 1, 0.0, pltpu.roll(v, v.shape[0] - 1, 0))
    return jnp.where(position == 0, 0.0, pltpu.roll(v, 1, 0))


def lane_shift(v, up, width, period, fill):
    place = (iota(v.shape, 1) // width) % period
    if up:
        return jnp.where(place == period - 1, fill, lane_roll(v, -width))
    return jnp.where(place == 0, fill, lane_roll(v, width))


def flux_of(m_ref, t, v):
    out = []
    for c in range(5):
        total = m_ref[t, c * 5] * v[0]
        for e in range(1, 5):
            total = total + m_ref[t, c * 5 + e] * v[e]
        out.append(total + v[1 + t] * v[c])
    return out


def turned_of(m_ref, t, w):
    out = []
    for c in range(5):
        total = m_ref[t, c] * w[0]
        for e in range(1, 5):
            total = total + m_ref[t, e * 5 + c] * w[e]
        out.append(total)
    return out


PAIRS = [(0, 1), (0, 2), (0, 3), (4, 1), (4, 2), (4, 3), (1, 1), (1, 2), (1, 3), (2, 2), (2, 3), (3, 3)]


def linear_fields(m_ref, center, sides):
    base = [center[c] * (1.0 - 6.0 * damping * time_step) for c in range(5)]
    jumps = []
    for t, (upper, lower) in enumerate(sides):
        jump = [0.5 * (lower[c] - upper[c]) for c in range(5)]
        turned = turned_of(m_ref, t, jump)
        for c in range(5):
            base[c] = base[c] - time_step * (turned[c] - damping * (upper[c] + lower[c]))
        jumps.append(jump)
    out = list(base)
    for a, b in PAIRS:
        if a in (0, 4):
            out.append(jumps[b - 1][a])
        else:
            out.append(jumps[a - 1][b] + jumps[b - 1][a])
    return out


def apply_fields(fields, v):
    out = []
    table = {pair: 5 + n for n, pair in enumerate(PAIRS)}
    for c in range(5):
        total = None
        for e in range(5):
            key = (c, e) if (c, e) in table else (e, c)
            if key in table:
                term = fields[table[key]] * v[e]
                total = term if total is None else total + term
        out.append(fields[c] - time_step * total)
    return out


def adjoint_at(m_ref, v, center, sides):
    out = [center[c] * (1.0 - 6.0 * damping * time_step) for c in range(5)]
    for t, (upper, lower) in enumerate(sides):
        jump = [0.5 * (lower[c] - upper[c]) for c in range(5)]
        turned = turned_of(m_ref, t, jump)
        inner = v[0] * jump[0]
        for e in range(1, 5):
            inner = inner + v[e] * jump[e]
        for c in range(5):
            total = turned[c] + v[1 + t] * jump[c]
            if c == 1 + t:
                total = total + inner
            out[c] = out[c] - time_step * (total - damping * (upper[c] + lower[c]))
    return out


def blade_sides(ref, low, high, j):
    center = [ref[c, j * WALL : (j + 1) * WALL, :] for c in range(5)]
    above = [
        ref[c, (j + 1) * WALL : (j + 2) * WALL, :] if j < WRAP - 1 else high[c] for c in range(5)
    ]
    below = [ref[c, (j - 1) * WALL : j * WALL, :] if j > 0 else low[c] for c in range(5)]
    wall = ([wall_shift(v, True) for v in center], [wall_shift(v, False) for v in center])
    span = (
        [lane_shift(v, True, 1, CHORD, 0.0) for v in center],
        [lane_shift(v, False, 1, CHORD, 0.0) for v in center],
    )
    return center, [(above, below), wall, span]


def back_sides(center, halo):
    east = (
        [lane_shift(v, True, 1, EAST, halo[1][c]) for c, v in enumerate(center)],
        [lane_shift(v, False, 1, EAST, halo[0][c]) for c, v in enumerate(center)],
    )
    north = (
        [lane_shift(v, True, EAST, NORTH, halo[3][c]) for c, v in enumerate(center)],
        [lane_shift(v, False, EAST, NORTH, halo[2][c]) for c, v in enumerate(center)],
    )
    vert = ([wall_shift(v, True) for v in center], [wall_shift(v, False) for v in center])
    return [east, north, vert]


def pack_east(v, x):
    lane = iota((8, DEVS), 1)
    out = jnp.zeros((8, DEVS), F32)
    for g in range(8):
        out = jnp.where(lane % EAST == g, lane_roll(v[g * 8 : g * 8 + 8, :], g - x), out)
    return out


def unpack_east(v, x):
    return jnp.concatenate([lane_roll(v, x - g) for g in range(8)], axis=0)


def pack_north(v, y):
    lane = iota((8, DEVS), 1)
    out = jnp.zeros((8, DEVS), F32)
    for g in range(8):
        out = jnp.where(lane // EAST == g, lane_roll(v[g * 8 : g * 8 + 8, :], (g - y) * EAST), out)
    return out


def unpack_north(v, y):
    return jnp.concatenate([lane_roll(v, (y - g) * EAST) for g in range(8)], axis=0)


def store_edges(blade_at, back, edges):
    to_high, to_low, to_east, to_west = edges
    for c in range(5):
        to_high[c, :WALL, :] = blade_at(c, (WRAP - 1) * WALL)
        to_low[c, :WALL, :] = blade_at(c, 0)
        to_high[c, WALL:, :] = pack_north(back[c], NORTH - 1)
        to_low[c, WALL:, :] = pack_north(back[c], 0)
        to_east[c] = pack_east(back[c], EAST - 1)
        to_west[c] = pack_east(back[c], 0)


EDGE_SHAPES = [
    jax.ShapeDtypeStruct((5, WALL + 8, CHORD), F32),
    jax.ShapeDtypeStruct((5, WALL + 8, CHORD), F32),
    jax.ShapeDtypeStruct((5, 8, DEVS), F32),
    jax.ShapeDtypeStruct((5, 8, DEVS), F32),
]


def read_halo(place_ref, from_low, from_high, from_west, from_east):
    north = place_ref[0]
    keep_low = jnp.where(north > 0, 1.0, 0.0)
    keep_high = jnp.where(north < DEVS // 8 - 1, 1.0, 0.0)
    low = [from_low[c, :WALL, :] for c in range(5)]
    high = [from_high[c, :WALL, :] for c in range(5)]
    west = [unpack_east(from_west[c], 0) for c in range(5)]
    east = [unpack_east(from_east[c], EAST - 1) for c in range(5)]
    south = [unpack_north(from_low[c, WALL:, :] * keep_low, 0) for c in range(5)]
    upper = [unpack_north(from_high[c, WALL:, :] * keep_high, NORTH - 1) for c in range(5)]
    return low, high, [west, east, south, upper]


def exchange(edges):
    gx, gy = lax.axis_size("gx"), lax.axis_size("gy")
    ring = [(i, (i + 1) % gy) for i in range(gy)]
    line = [(i, i + 1) for i in range(gx - 1)]
    to_high, to_low, to_east, to_west = edges
    return (
        lax.ppermute(to_high, "gy", ring),
        lax.ppermute(to_low, "gy", [(b, a) for a, b in ring]),
        lax.ppermute(to_east, "gx", line),
        lax.ppermute(to_west, "gx", [(b, a) for a, b in line]),
    )


def regroup(pieces, width):
    count = DEVS // width
    shape = next(piece.shape for piece in pieces if piece is not None)
    block = iota(shape, 1) // width
    out = []
    for b in range(count):
        total = jnp.zeros(shape, F32)
        for a in range(count):
            if pieces[a] is not None:
                total = jnp.where(block == a, lane_roll(pieces[a], (a - b) * width), total)
        out.append(total)
    return out


def ranks_of(owner_ref, out_ref):
    count = owner_ref.shape[1]
    earlier = jnp.where(iota((256, 256), 0) < iota((256, 256), 1), 1.0, 0.0).astype(BF16)
    carry = jnp.zeros((DEVS, 1), F32)
    for start in range(0, count, 256):
        marks = one_hot(DEVS, owner_ref[:, start : start + 256])
        before = dot_nn(marks.astype(BF16), earlier) + carry
        out_ref[:, start : start + 256] = jnp.sum(marks * before, axis=0, keepdims=True).astype(
            jnp.int32
        )
        carry = carry + jnp.sum(marks, axis=1, keepdims=True)


def send_rows(values, owner, rank, slots, pad_rows):
    marks = one_hot(DEVS, owner).astype(BF16)
    seats = one_hot(slots, rank)
    terms = jnp.concatenate([seats * v for v in values], axis=0)
    before, after = pad_rows
    parts = [terms]
    if before:
        parts.insert(0, jnp.zeros((before, terms.shape[1]), F32))
    if after:
        parts.append(jnp.zeros((after, terms.shape[1]), F32))
    if len(parts) > 1:
        terms = jnp.concatenate(parts, axis=0)
    hi, lo = split(terms)
    return dot_nt(marks, hi) + dot_nt(marks, lo)


def hole_parts(cell):
    row = ((cell >> 6) & (NORTH - 1)) * EAST + (cell >> 9)
    return row, cell & (VERT - 1)


def hole_values(low_half, cell):
    row, vert = hole_parts(cell)
    marks = one_hot(DEVS, row).astype(BF16)
    seats = one_hot(HALF, vert)
    out = []
    for field in low_half:
        hi, lo = split(field)
        table = dot_nn(hi, marks) + dot_nn(lo, marks)
        out.append(jnp.sum(table * seats, axis=0, keepdims=True))
    return out


def hole_mask(cell_ref):
    total = jnp.zeros((HALF, DEVS), F32)
    for start in range(0, HOLES, 512):
        row, vert = hole_parts(cell_ref[:, start : start + 512])
        total = total + dot_nt(one_hot(HALF, vert).astype(BF16), one_hot(DEVS, row).astype(BF16))
    return total


CHUNK = 512


def interpolate_all(blade_parts, back_parts, tables, blade_out, back_out):
    back_base, back_weight, blade_base, blade_weight = tables

    def blade_step(n, carry):
        lanes = pl.ds(pl.multiple_of(n * CHUNK, CHUNK), CHUNK)
        rows, cols = blade_donors(blade_base[:, lanes], blade_weight[0, :, lanes])
        for c in range(5):
            value = picked((blade_parts[0][c], blade_parts[1][c]), rows, cols)
            for m in range(CHUNK // DEVS):
                blade_out[c, pl.ds(n * (CHUNK // DEVS) + m, 1), :] = value[
                    :, m * DEVS : (m + 1) * DEVS
                ]
        return carry

    lax.fori_loop(0, 2 * HOLES // CHUNK, blade_step, 0)

    def back_step(n, carry):
        lanes = pl.ds(pl.multiple_of(n * CHUNK, CHUNK), CHUNK)
        rows, cols = back_donors(back_base[:, lanes], back_weight[0, :, lanes])
        for c in range(5):
            value = picked((back_parts[0][c], back_parts[1][c]), rows, cols)
            for m in range(CHUNK // DEVS):
                back_out[c, pl.ds(n * (CHUNK // DEVS) + m, 1), :] = value[
                    :, m * DEVS : (m + 1) * DEVS
                ]
        return carry

    lax.fori_loop(0, 2 * RIMS // CHUNK, back_step, 0)


def start_kernel(
    blade, back, cot, back_cot, back_base, back_weight, blade_base, blade_weight,
    send, back_planes, cot_planes, to_high, to_low, to_east, to_west,
    blade_hi, blade_lo, back_hi, back_lo, hole_vals, rim_vals,
):
    cots = []
    for c in range(5):
        turned = to_planes(back_cot[c])
        cot_planes[c] = turned
        cots.append(turned)
    store_edges(lambda c, r: cot[c, r : r + WALL, :], cots, (to_high, to_low, to_east, to_west))
    for c in range(5):
        hi, lo = split(blade[c].T)
        blade_hi[c] = hi
        blade_lo[c] = lo
        field = to_planes(back[c])
        back_planes[c] = field
        hi, lo = split(field[HALF:, :])
        back_hi[c] = hi
        back_lo[c] = lo
    interpolate_all(
        (blade_hi, blade_lo), (back_hi, back_lo),
        (back_base, back_weight, blade_base, blade_weight), hole_vals, rim_vals,
    )
    store_slots(hole_vals, rim_vals, send)


def store_slots(hole_vals, rim_vals, send):
    first = regroup([hole_vals[c] for c in range(4)], QH)
    fifth = hole_vals[4]
    tail = regroup([fifth, None, None, None], QH)
    for d in range(DEVS // QH):
        send[pl.ds(d, QH, stride=DEVS // QH), 0, :] = first[d]
        send[pl.ds(d, QH, stride=DEVS // QH), 1, :] = tail[d]
    rims = regroup([None, None] + [rim_vals[c] for c in range(5)] + [None], QR)
    lane = iota((QR, DEVS), 1)
    for d in range(DEVS // QR):
        rows = pl.ds(d, QR, stride=DEVS // QR)
        send[rows, 1, :] = jnp.where(lane < QH, send[rows, 1, :], rims[d])


def cot_kernel(
    place, blade_m, back_m, cot, cot_planes, from_low, from_high, from_west, from_east,
    rim_owner, hole_owner, hole_cell,
    send, blade_fields, back_fields, rim_rank, hole_rank,
):
    low, high, halo = read_halo(place, from_low, from_high, from_west, from_east)
    for j in range(WRAP):
        center, sides = blade_sides(cot, low, high, j)
        fields = linear_fields(blade_m, center, sides)
        for n in range(FIELDS):
            blade_fields[n, j * WALL : (j + 1) * WALL, :] = fields[n]
    center = [cot_planes[c] for c in range(5)]
    fields = linear_fields(back_m, center, back_sides(center, halo))
    for n in range(FIELDS):
        back_fields[n] = fields[n]
    for step in range(2):
        ranks_of(rim_owner.at[step], rim_rank.at[step])
        ranks_of(hole_owner.at[step], hole_rank.at[step])

    total = jnp.zeros((DEVS, FIELDS * QR + 112), F32)
    for j in range(WRAP):
        lanes = slice(j * 256, j * 256 + 256)
        values = [
            jnp.concatenate(
                [
                    blade_fields[n, j * WALL + WALL - 2 + k : j * WALL + WALL - 1 + k, :]
                    for k in range(2)
                ],
                axis=1,
            )
            for n in range(FIELDS)
        ]
        total = total + send_rows(
            values, rim_owner[1, :, lanes], rim_rank[1, :, lanes], QR, (0, 112)
        )
    for m in range(3):
        send[:, 5 + m, :] = total[:, m * DEVS : (m + 1) * DEVS]
    total = jnp.zeros((DEVS, FIELDS * QH + 96), F32)
    low_half = [back_fields[n, :HALF, :] for n in range(FIELDS)]
    for start in range(0, HOLES, 512):
        lanes = slice(start, start + 512)
        values = hole_values(low_half, hole_cell[1:2, lanes])
        total = total + send_rows(
            values, hole_owner[1, :, lanes], hole_rank[1, :, lanes], QH, (0, 96)
        )
    for m in range(5):
        send[:, m, :] = total[:, m * DEVS : (m + 1) * DEVS]


def fill_kernel(
    blade, back_planes, recv, rim_owner, hole_owner, rim_rank, hole_rank, hole_cell,
    blade_first, back_first, to_high, to_low, to_east, to_west,
):
    arrived = jnp.concatenate([recv[:, 0, :].T, recv[:, 1, :].T], axis=0)
    hi, lo = split(arrived)
    for c in range(5):
        for j in range(WRAP):
            rows = slice(j * WALL, (j + 1) * WALL)
            blade_first[c, rows, :] = blade[c, rows, :]
    base = 5 * QH
    for j in range(WRAP):
        lanes = slice(j * 256, j * 256 + 256)
        marks = one_hot(DEVS, rim_owner[0, :, lanes]).astype(BF16)
        seats = one_hot(QR, rim_rank[0, :, lanes])
        table = dot_nn(hi[base : base + 5 * QR], marks) + dot_nn(lo[base : base + 5 * QR], marks)
        for c in range(5):
            value = jnp.sum(table[c * QR : (c + 1) * QR] * seats, axis=0, keepdims=True)
            for k in range(2):
                row = j * WALL + WALL - 2 + k
                blade_first[c, row : row + 1, :] = value[:, k * CHORD : (k + 1) * CHORD]
    filled = [jnp.zeros((HALF, DEVS), F32) for _ in range(5)]
    mask = jnp.zeros((HALF, DEVS), F32)
    for start in range(0, HOLES, 512):
        lanes = slice(start, start + 512)
        marks = one_hot(DEVS, hole_owner[0, :, lanes]).astype(BF16)
        seats = one_hot(QH, hole_rank[0, :, lanes])
        row, vert = hole_parts(hole_cell[0:1, lanes])
        row_marks = one_hot(DEVS, row).astype(BF16)
        vert_marks = one_hot(HALF, vert)
        table = dot_nn(hi[: 5 * QH], marks) + dot_nn(lo[: 5 * QH], marks)
        mask = mask + dot_nt(vert_marks.astype(BF16), row_marks)
        for c in range(5):
            value = jnp.sum(table[c * QH : (c + 1) * QH] * seats, axis=0, keepdims=True)
            value_hi, value_lo = split(vert_marks * value)
            filled[c] = filled[c] + (dot_nt(value_hi, row_marks) + dot_nt(value_lo, row_marks))
    backs = []
    for c in range(5):
        top = jnp.where(mask > 0.5, filled[c], back_planes[c, :HALF, :])
        field = jnp.concatenate([top, back_planes[c, HALF:, :]], axis=0)
        back_first[c] = field
        backs.append(field)
    store_edges(
        lambda c, r: blade_first[c, r : r + WALL, :], backs, (to_high, to_low, to_east, to_west)
    )


def residual_step(m_ref, center, halo_flux):
    out = [center[c] * (1.0 - 6.0 * damping * time_step) for c in range(5)]
    for t in range(3):
        upper, lower = halo_flux(t)
        for c in range(5):
            out[c] = out[c] - time_step * (upper[c] - lower[c])
    return out


def side_terms(m_ref, t, v):
    flux = flux_of(m_ref, t, v)
    upper = [0.5 * flux[c] - damping * v[c] for c in range(5)]
    lower = [0.5 * flux[c] + damping * v[c] for c in range(5)]
    return upper, lower


def middle_kernel(
    place, blade_m, back_m, blade_first, back_first, from_low, from_high, from_west, from_east,
    blade_fields, back_fields, recv, back_base, back_weight, blade_base, blade_weight, hole_cell,
    blade_mid, back_mid, to_high, to_low, to_east, to_west,
    blade_next, back_next, blade_hi, blade_lo, back_hi, back_lo, hole_lin, rim_lin,
):
    low, high, halo = read_halo(place, from_low, from_high, from_west, from_east)

    for j in range(WRAP):
        center, sides = blade_sides(blade_first, low, high, j)

        def around(t, center=center, sides=sides):
            if t == 0:
                return side_terms(blade_m, 0, sides[0][0])[0], side_terms(blade_m, 0, sides[0][1])[1]
            upper, lower = side_terms(blade_m, t, center)
            if t == 1:
                return [wall_shift(v, True) for v in upper], [wall_shift(v, False) for v in lower]
            return (
                [lane_shift(v, True, 1, CHORD, 0.0) for v in upper],
                [lane_shift(v, False, 1, CHORD, 0.0) for v in lower],
            )

        out = residual_step(blade_m, center, around)
        for c in range(5):
            blade_next[c, j * WALL : (j + 1) * WALL, :] = out[c]
    center = [back_first[c] for c in range(5)]

    def across(t):
        upper, lower = side_terms(back_m, t, center)
        if t == 2:
            return [wall_shift(v, True) for v in upper], [wall_shift(v, False) for v in lower]
        width, period = ((1, EAST), (EAST, NORTH))[t]
        below = side_terms(back_m, t, halo[2 * t])[1]
        above = side_terms(back_m, t, halo[2 * t + 1])[0]
        return (
            [lane_shift(upper[c], True, width, period, above[c]) for c in range(5)],
            [lane_shift(lower[c], False, width, period, below[c]) for c in range(5)],
        )

    out = residual_step(back_m, center, across)
    for c in range(5):
        back_next[c] = out[c]
        hi, lo = split(out[c][HALF:, :])
        back_hi[c] = hi
        back_lo[c] = lo
        hi, lo = split(blade_next[c].T)
        blade_hi[c] = hi
        blade_lo[c] = lo

    for j in range(WRAP):
        rows = slice(j * WALL, (j + 1) * WALL)
        v = [blade_next[c, rows, :] for c in range(5)]
        own = apply_fields([blade_fields[n, rows, :] for n in range(FIELDS)], v)
        inside = iota((WALL, CHORD), 0) < WALL - 2
        for c in range(5):
            blade_mid[c, rows, :] = jnp.where(inside, own[c], 0.0)
    mask = hole_mask(hole_cell)
    own = apply_fields([back_fields[n] for n in range(FIELDS)], [back_next[c] for c in range(5)])
    for c in range(5):
        back_mid[c, :HALF, :] = jnp.where(mask > 0.5, 0.0, own[c][:HALF, :])
        back_mid[c, HALF:, :] = own[c][HALF:, :]

    for m in range(5):
        pieces = [recv[pl.ds(d, QH, stride=DEVS // QH), m, :] for d in range(DEVS // QH)]
        for b, piece in enumerate(regroup(pieces, QH)):
            if m * 4 + b < FIELDS:
                hole_lin[m * 4 + b] = piece
    for m in range(3):
        pieces = [recv[pl.ds(d, QR, stride=DEVS // QR), 5 + m, :] for d in range(DEVS // QR)]
        for b, piece in enumerate(regroup(pieces, QR)):
            if m * 8 + b < FIELDS:
                rim_lin[m * 8 + b] = piece

    def lanes_of(ref, n, k):
        count = CHUNK // DEVS
        return jnp.concatenate([ref[k, pl.ds(n * count + m, 1), :] for m in range(count)], axis=1)

    def blade_step(n, carry):
        lanes = pl.ds(pl.multiple_of(n * CHUNK, CHUNK), CHUNK)
        rows, cols = blade_donors(blade_base[:, lanes], blade_weight[0, :, lanes])
        value = [picked((blade_hi[c], blade_lo[c]), rows, cols) for c in range(5)]
        mu = apply_fields([lanes_of(hole_lin, n, k) for k in range(FIELDS)], value)
        for c in range(5):
            blade_mid[c] = blade_mid[c] + spread_terms(rows, cols * mu[c])
        return carry

    lax.fori_loop(0, 2 * HOLES // CHUNK, blade_step, 0)

    def back_step(n, carry):
        lanes = pl.ds(pl.multiple_of(n * CHUNK, CHUNK), CHUNK)
        rows, cols = back_donors(back_base[:, lanes], back_weight[0, :, lanes])
        value = [picked((back_hi[c], back_lo[c]), rows, cols) for c in range(5)]
        mu = apply_fields([lanes_of(rim_lin, n, k) for k in range(FIELDS)], value)
        spread_back(back_mid, rows, cols, mu)
        return carry

    lax.fori_loop(0, 2 * RIMS // CHUNK, back_step, 0)
    store_edges(
        lambda c, r: blade_mid[c, r : r + WALL, :],
        [back_mid[c] for c in range(5)],
        (to_high, to_low, to_east, to_west),
    )


def spread_back(target, rows, cols, mu):
    row_hi, row_lo = rows
    for c in range(5):
        hi, lo = split(cols * mu[c])
        target[c, HALF:, :] = target[c, HALF:, :] + (
            dot_nt(hi, row_hi) + (dot_nt(lo, row_hi) + dot_nt(hi, row_lo))
        )


def last_kernel(
    place, blade_m, back_m, blade_first, back_first, blade_mid, back_mid,
    from_low, from_high, from_west, from_east,
    rim_owner, hole_owner, rim_rank, hole_rank, hole_cell,
    send, blade_kept, back_kept,
):
    low, high, halo = read_halo(place, from_low, from_high, from_west, from_east)
    rims = jnp.zeros((DEVS, DEVS), F32)
    for j in range(WRAP):
        rows = slice(j * WALL, (j + 1) * WALL)
        center, sides = blade_sides(blade_mid, low, high, j)
        out = adjoint_at(blade_m, [blade_first[c, rows, :] for c in range(5)], center, sides)
        inside = iota((WALL, CHORD), 0) < WALL - 2
        values = []
        for c in range(5):
            blade_kept[c, rows, :] = jnp.where(inside, out[c], 0.0)
            values.append(
                jnp.concatenate([out[c][WALL - 2 : WALL - 1, :], out[c][WALL - 1 :, :]], axis=1)
            )
        lanes = slice(j * 256, j * 256 + 256)
        rims = rims + send_rows(
            values, rim_owner[0, :, lanes], rim_rank[0, :, lanes], QR, (QH, DEVS - QH - 5 * QR)
        )
    center = [back_mid[c] for c in range(5)]
    out = adjoint_at(back_m, [back_first[c] for c in range(5)], center, back_sides(center, halo))
    mask = hole_mask(hole_cell)
    low_half = []
    for c in range(5):
        back_kept[c, :HALF, :] = jnp.where(mask > 0.5, 0.0, out[c][:HALF, :])
        back_kept[c, HALF:, :] = out[c][HALF:, :]
        low_half.append(out[c][:HALF, :])
    holes = jnp.zeros((DEVS, 2 * DEVS), F32)
    for start in range(0, HOLES, 512):
        lanes = slice(start, start + 512)
        values = hole_values(low_half, hole_cell[0:1, lanes])
        holes = holes + send_rows(
            values, hole_owner[0, :, lanes], hole_rank[0, :, lanes], QH, (0, 2 * DEVS - 5 * QH)
        )
    send[:, 0, :] = holes[:, :DEVS]
    send[:, 1, :] = holes[:, DEVS:] + rims


def end_kernel(
    blade_kept, back_kept, recv, back_base, back_weight, blade_base, blade_weight,
    blade_out, back_out, hole_mu, rim_mu, back_acc,
):
    count = DEVS // QH
    pieces = [recv[pl.ds(d, QH, stride=count), 0, :] for d in range(count)]
    for c, piece in enumerate(regroup(pieces, QH)):
        hole_mu[c] = piece
    pieces = [recv[pl.ds(d, QH, stride=count), 1, :] for d in range(count)]
    hole_mu[4] = regroup(pieces, QH)[0]
    count = DEVS // QR
    pieces = [recv[pl.ds(d, QR, stride=count), 1, :] for d in range(count)]
    groups = regroup(pieces, QR)
    for c in range(5):
        rim_mu[c] = groups[QH // QR + c]
        blade_out[c] = blade_kept[c]
        back_acc[c] = back_kept[c]

    def lanes_of(ref, n, k):
        count = CHUNK // DEVS
        return jnp.concatenate([ref[k, pl.ds(n * count + m, 1), :] for m in range(count)], axis=1)

    def blade_step(n, carry):
        lanes = pl.ds(pl.multiple_of(n * CHUNK, CHUNK), CHUNK)
        rows, cols = blade_donors(blade_base[:, lanes], blade_weight[0, :, lanes])
        for c in range(5):
            blade_out[c] = blade_out[c] + spread_terms(rows, cols * lanes_of(hole_mu, n, c))
        return carry

    lax.fori_loop(0, 2 * HOLES // CHUNK, blade_step, 0)

    def back_step(n, carry):
        lanes = pl.ds(pl.multiple_of(n * CHUNK, CHUNK), CHUNK)
        rows, cols = back_donors(back_base[:, lanes], back_weight[0, :, lanes])
        spread_back(back_acc, rows, cols, [lanes_of(rim_mu, n, c) for c in range(5)])
        return carry

    lax.fori_loop(0, 2 * RIMS // CHUNK, back_step, 0)
    for c in range(5):
        parts = from_planes(back_acc[c])
        for y in range(0, NORTH, 2):
            back_out[c, :, y * VERT : (y + 2) * VERT] = jnp.concatenate(parts[y : y + 2], axis=1)


VMEM = pl.BlockSpec(memory_space=pltpu.VMEM)
SMEM = pl.BlockSpec(memory_space=pltpu.SMEM)
BLADE = jax.ShapeDtypeStruct((5, WRAP * WALL, CHORD), F32)
PLANES = jax.ShapeDtypeStruct((5, VERT, DEVS), F32)
DONOR_PARTS = [
    pltpu.VMEM((5, CHORD, WRAP * WALL), BF16),
    pltpu.VMEM((5, CHORD, WRAP * WALL), BF16),
    pltpu.VMEM((5, HALF, DEVS), BF16),
    pltpu.VMEM((5, HALF, DEVS), BF16),
]


def run(kernel, name, args, out_shape, scratch=(), scalars=0, flops=0):
    size = sum(4 * a.size for a in args) + sum(4 * o.size for o in out_shape)
    return pl.pallas_call(
        kernel,
        name=name,
        out_shape=list(out_shape),
        in_specs=[SMEM] * scalars + [VMEM] * (len(args) - scalars),
        out_specs=[VMEM] * len(out_shape),
        scratch_shapes=list(scratch),
        cost_estimate=pl.CostEstimate(flops=flops, bytes_accessed=size, transcendentals=0),
    )(*args)


def swap(rows):
    return lax.all_to_all(rows, ("gx", "gy"), split_axis=0, concat_axis=0, tiled=True)


def body(
    blade_state,
    back_state,
    blade_cotangent,
    back_cotangent,
    blade_flux,
    back_flux,
    blade_owner,
    back_donor_cell,
    back_donor_weight,
    hole_cell,
    hole_owner,
    blade_donor_cell,
    blade_donor_weight,
):
    shape = jax.ShapeDtypeStruct
    place = lax.axis_index("gy").astype(jnp.int32).reshape(1)
    blade = blade_state.reshape(5, WRAP * WALL, CHORD)
    cot = blade_cotangent.reshape(5, WRAP * WALL, CHORD)
    blade_m = blade_flux.reshape(3, 25)
    back_m = back_flux.reshape(3, 25)
    rim_owner = blade_owner.reshape(2, 1, RIMS)
    holes_owner = hole_owner.reshape(2, 1, HOLES)
    tables = [
        (
            back_donor_cell[s : s + 1],
            back_donor_weight[s : s + 1],
            blade_donor_cell[s : s + 1],
            blade_donor_weight[s : s + 1],
        )
        for s in range(2)
    ]

    send, back_planes, cot_planes, *edges = run(
        start_kernel,
        "start",
        (blade, back_state, cot, back_cotangent) + tables[0],
        [shape((DEVS, 2, DEVS), F32), PLANES, PLANES] + EDGE_SHAPES,
        DONOR_PARTS + [pltpu.VMEM((5, QH, DEVS), F32), pltpu.VMEM((5, QR, DEVS), F32)],
        flops=5 * 10**9,
    )
    recv = swap(send)
    cot_halo = exchange(edges)
    lin_send, blade_fields, back_fields, rim_rank, hole_rank = run(
        cot_kernel,
        "cotangent",
        (place, blade_m, back_m, cot, cot_planes, *cot_halo, rim_owner, holes_owner, hole_cell),
        [
            shape((DEVS, 8, DEVS), F32),
            shape((FIELDS, WRAP * WALL, CHORD), F32),
            shape((FIELDS, VERT, DEVS), F32),
            shape((2, 1, RIMS), jnp.int32),
            shape((2, 1, HOLES), jnp.int32),
        ],
        scalars=3,
        flops=2 * 10**9,
    )
    lin_recv = swap(lin_send)
    slots = (rim_owner, holes_owner, rim_rank, hole_rank)
    blade_first, back_first, *edges = run(
        fill_kernel,
        "fill",
        (blade, back_planes, recv) + slots + (hole_cell[0:1],),
        [BLADE, PLANES] + EDGE_SHAPES,
        flops=10**9,
    )
    first_halo = exchange(edges)
    blade_mid, back_mid, *edges = run(
        middle_kernel,
        "middle",
        (place, blade_m, back_m, blade_first, back_first, *first_halo, blade_fields, back_fields)
        + (lin_recv,)
        + tables[1]
        + (hole_cell[1:2],),
        [BLADE, PLANES] + EDGE_SHAPES,
        [pltpu.VMEM(BLADE.shape, F32), pltpu.VMEM(PLANES.shape, F32)]
        + DONOR_PARTS
        + [pltpu.VMEM((FIELDS, QH, DEVS), F32), pltpu.VMEM((FIELDS, QR, DEVS), F32)],
        scalars=3,
        flops=10**10,
    )
    mid_halo = exchange(edges)
    send, blade_kept, back_kept = run(
        last_kernel,
        "last",
        (place, blade_m, back_m, blade_first, back_first, blade_mid, back_mid, *mid_halo)
        + slots
        + (hole_cell[0:1],),
        [shape((DEVS, 2, DEVS), F32), BLADE, PLANES],
        scalars=3,
        flops=10**9,
    )
    recv = swap(send)
    blade_last, back_last = run(
        end_kernel,
        "end",
        (blade_kept, back_kept, recv) + tables[0],
        [BLADE, shape((5, EAST, NORTH * VERT), F32)],
        [
            pltpu.VMEM((5, QH, DEVS), F32),
            pltpu.VMEM((5, QR, DEVS), F32),
            pltpu.VMEM(PLANES.shape, F32),
        ],
        flops=5 * 10**9,
    )
    return (blade_last.reshape(blade_state.shape), back_last)


def solution(mesh):
    return jax.shard_map(
        body,
        mesh=mesh,
        in_specs=(
            P(None, "gx", "gy"),
            P(None, "gx", "gy"),
            P(None, "gx", "gy"),
            P(None, "gx", "gy"),
            P(),
            P(),
            P(None, ("gx", "gy"), None),
            P(None, ("gx", "gy")),
            P(None, None, ("gx", "gy")),
            P(None, ("gx", "gy")),
            P(None, ("gx", "gy"), None),
            P(None, ("gx", "gy")),
            P(None, None, ("gx", "gy")),
        ),
        out_specs=(P(None, "gx", "gy"), P(None, "gx", "gy")),
        check_vma=False,
    )
```

```python
import jax
import jax.numpy as jnp
from jax import lax
from jax.experimental import pallas as pl
from jax.experimental.pallas import tpu as pltpu
from jax.sharding import PartitionSpec as P


DEVS = 128
WRAP = 4
WALL = 64
CHORD = 128
EAST = 16
NORTH = 8
VERT = 64
HALF = VERT // 2
RIMS = 1024
HOLES = 2048
QR = 2 * RIMS // DEVS
QH = 2 * HOLES // DEVS
FIELDS = 17

time_step = 0.2
damping = 0.1

F32 = jnp.float32
BF16 = jnp.bfloat16


def split(x):
    hi = x.astype(BF16)
    return hi, (x - hi.astype(F32)).astype(BF16)


def dot_nn(a, b):
    return lax.dot_general(a, b, (((1,), (0,)), ((), ())), preferred_element_type=F32)


def dot_nt(a, b):
    return lax.dot_general(a, b, (((1,), (1,)), ((), ())), preferred_element_type=F32)


def iota(shape, dim):
    return lax.broadcasted_iota(jnp.int32, shape, dim)


def one_hot(rows, index):
    return jnp.where(iota((rows, index.shape[1]), 0) == index, 1.0, 0.0)


def pair_hot(rows, index, first, second):
    position = iota((rows, index.shape[1]), 0)
    return jnp.where(position == index, first, jnp.where(position == index + 1, second, 0.0))


def lane_roll(x, amount):
    amount = amount % x.shape[-1]
    return pltpu.roll(x, amount, x.ndim - 1) if amount else x


def to_planes(block):
    rows = [block[:, y * VERT : (y + 1) * VERT] for y in range(NORTH)]
    return jnp.concatenate(rows, axis=0).T


def from_planes(field):
    turned = field.T
    return [turned[y * EAST : (y + 1) * EAST, :] for y in range(NORTH)]


def donor_parts(weights):
    w = [weights[corner : corner + 1, :] for corner in range(8)]
    x0 = (w[0] + w[1]) + (w[2] + w[3])
    x1 = (w[4] + w[5]) + (w[6] + w[7])
    y0 = (w[0] + w[1]) + (w[4] + w[5])
    y1 = (w[2] + w[3]) + (w[6] + w[7])
    z0 = (w[0] + w[2]) + (w[4] + w[6])
    z1 = (w[1] + w[3]) + (w[5] + w[7])
    return x0, x1, y0, y1, z0, z1


def short_marks(size, index):
    position = iota((size, index.shape[1]), 0).astype(jnp.int16)
    return position == index.astype(jnp.int16), position == (index + 1).astype(jnp.int16)


def pair_split(marks, first, second):
    (first_hi, first_lo), (second_hi, second_lo) = split(first), split(second)
    zero = jnp.zeros((), BF16)

    def place(a, b):
        return jnp.where(marks[0], a, jnp.where(marks[1], b, zero))

    return place(first_hi, second_hi), place(first_lo, second_lo)


def donor_rows(outer, outer_index, outer_pair, inner, inner_index, inner_pair):
    hot = pair_hot(outer, outer_index, *outer_pair)
    marks = short_marks(inner, inner_index)
    parts = [
        pair_split(marks, hot[n : n + 1, :] * inner_pair[0], hot[n : n + 1, :] * inner_pair[1])
        for n in range(outer)
    ]
    return tuple(jnp.concatenate([p[k] for p in parts], axis=0) for k in range(2))


def blade_donors(base, weights):
    x0, x1, y0, y1, z0, z1 = donor_parts(weights)
    wall = (base >> 7) & (WALL - 1)
    rows = donor_rows(WRAP, base >> 13, (x0, x1), WALL, wall, (y0, y1))
    return rows, (CHORD, base & (CHORD - 1), z0, z1)


def back_donors(base, weights):
    x0, x1, y0, y1, z0, z1 = donor_parts(weights)
    north = (base >> 6) & (NORTH - 1)
    rows = donor_rows(NORTH, north, (y0, y1), EAST, base >> 9, (x0, x1))
    return rows, (HALF, (base & (VERT - 1)) - HALF, z0, z1)


def triple_rows(rows):
    hi, lo = rows
    return jnp.concatenate([hi, lo, hi], axis=0)


def triple_lanes(rows):
    hi, lo = rows
    return jnp.concatenate([hi, hi, lo], axis=1)


def store_parts(target, place, size, field):
    hi, lo = split(field)
    rows = slice(place, place + size)
    target[rows, :] = jnp.concatenate([hi, hi, lo], axis=1)


def picked(parts, rows, cols):
    size = cols[0]
    hot = pair_hot(*cols)
    table = dot_nn(parts[...], triple_rows(rows))
    return [
        jnp.sum(table[c * size : (c + 1) * size] * hot, axis=0, keepdims=True) for c in range(5)
    ]


def spread_terms(rows, cols, mu):
    size, index, first, second = cols
    pairs = [(first * mu[c], second * mu[c]) for c in range(5)]
    tiles = {c: [] for c in range(5)}
    for start in range(0, size, 16):
        marks = short_marks(16, index - start)
        for c in range(5):
            tiles[c].append(pair_split(marks, *pairs[c]))
    hi, lo = (
        jnp.concatenate([t[k] for c in range(5) for t in tiles[c]], axis=0) for k in range(2)
    )
    return dot_nt(jnp.concatenate([hi, lo, hi], axis=1), triple_lanes(rows))


def exact_nt(terms, marks):
    hi, lo = split(terms)
    return dot_nt(jnp.concatenate([hi, lo], axis=1), jnp.concatenate([marks, marks], axis=1))


def doubled(field):
    hi, lo = split(field)
    return jnp.concatenate([hi, lo], axis=1)


def twice(marks):
    return jnp.concatenate([marks, marks], axis=0)


def wall_shift(v, up):
    position = iota(v.shape, 0)
    if up:
        return jnp.where(position == v.shape[0] - 1, 0.0, pltpu.roll(v, v.shape[0] - 1, 0))
    return jnp.where(position == 0, 0.0, pltpu.roll(v, 1, 0))


def lane_shift(v, up, width, period, fill):
    place = (iota(v.shape, 1) // width) % period
    if up:
        return jnp.where(place == period - 1, fill, lane_roll(v, -width))
    return jnp.where(place == 0, fill, lane_roll(v, width))


def flux_of(m_ref, t, v):
    out = []
    half = 0.5 * time_step * v[1 + t]
    for c in range(5):
        total = half * v[c]
        for e in range(5):
            total = total + m_ref[t, c * 5 + e] * v[e]
        out.append(total)
    return out


def turned_of(m_ref, t, w):
    out = []
    for c in range(5):
        total = m_ref[t, c] * w[0]
        for e in range(1, 5):
            total = total + m_ref[t, e * 5 + c] * w[e]
        out.append(total)
    return out


PAIRS = [(0, 1), (0, 2), (0, 3), (4, 1), (4, 2), (4, 3), (1, 1), (1, 2), (1, 3), (2, 2), (2, 3), (3, 3)]


def linear_fields(m_ref, center, sides):
    base = [center[c] * (1.0 - 6.0 * damping * time_step) for c in range(5)]
    jumps = []
    for t, (upper, lower) in enumerate(sides):
        jump = [0.5 * time_step * (lower[c] - upper[c]) for c in range(5)]
        turned = turned_of(m_ref, t, jump)
        for c in range(5):
            base[c] = base[c] - turned[c] + damping * time_step * (upper[c] + lower[c])
        jumps.append(jump)
    out = list(base)
    for a, b in PAIRS:
        if a in (0, 4):
            out.append(jumps[b - 1][a])
        else:
            out.append(jumps[a - 1][b] + jumps[b - 1][a])
    return out


def apply_fields(fields, v):
    out = []
    table = {pair: 5 + n for n, pair in enumerate(PAIRS)}
    for c in range(5):
        total = fields[c]
        for e in range(5):
            key = (c, e) if (c, e) in table else (e, c)
            if key in table:
                total = total - fields[table[key]] * v[e]
        out.append(total)
    return out


def adjoint_at(m_ref, v, center, sides):
    out = [center[c] * (1.0 - 6.0 * damping * time_step) for c in range(5)]
    for t, (upper, lower) in enumerate(sides):
        jump = [0.5 * time_step * (lower[c] - upper[c]) for c in range(5)]
        turned = turned_of(m_ref, t, jump)
        inner = v[0] * jump[0]
        for e in range(1, 5):
            inner = inner + v[e] * jump[e]
        for c in range(5):
            total = turned[c] + v[1 + t] * jump[c]
            if c == 1 + t:
                total = total + inner
            out[c] = out[c] - total + damping * time_step * (upper[c] + lower[c])
    return out


def blade_sides(ref, low, high, j, part=slice(0, WALL)):
    def plane(n):
        if n < 0 or n >= WRAP:
            return [v[part, :] for v in (low if n < 0 else high)]
        rows = slice(n * WALL + part.start, n * WALL + part.stop)
        return [ref[c, rows, :] for c in range(5)]

    center, above, below = plane(j), plane(j + 1), plane(j - 1)
    wall = ([wall_shift(v, True) for v in center], [wall_shift(v, False) for v in center])
    span = (
        [lane_shift(v, True, 1, CHORD, 0.0) for v in center],
        [lane_shift(v, False, 1, CHORD, 0.0) for v in center],
    )
    return center, [(above, below), wall, span]


def back_sides(center, halo):
    east = (
        [lane_shift(v, True, 1, EAST, halo[1][c]) for c, v in enumerate(center)],
        [lane_shift(v, False, 1, EAST, halo[0][c]) for c, v in enumerate(center)],
    )
    north = (
        [lane_shift(v, True, EAST, NORTH, halo[3][c]) for c, v in enumerate(center)],
        [lane_shift(v, False, EAST, NORTH, halo[2][c]) for c, v in enumerate(center)],
    )
    vert = ([wall_shift(v, True) for v in center], [wall_shift(v, False) for v in center])
    return [east, north, vert]


def pack_east(v, x):
    lane = iota((8, DEVS), 1)
    out = jnp.zeros((8, DEVS), F32)
    for g in range(8):
        out = jnp.where(lane % EAST == g, lane_roll(v[g * 8 : g * 8 + 8, :], g - x), out)
    return out


def unpack_east(v, x):
    return jnp.concatenate([lane_roll(v, x - g) for g in range(8)], axis=0)


def pack_north(v, y):
    lane = iota((8, DEVS), 1)
    out = jnp.zeros((8, DEVS), F32)
    for g in range(8):
        out = jnp.where(lane // EAST == g, lane_roll(v[g * 8 : g * 8 + 8, :], (g - y) * EAST), out)
    return out


def unpack_north(v, y):
    return jnp.concatenate([lane_roll(v, (y - g) * EAST) for g in range(8)], axis=0)


def store_edges(place_ref, blade_at, back, edges):
    first_y, second_y, first_x, second_x = edges
    even_y = place_ref[0] % 2 == 0
    even_x = place_ref[1] % 2 == 0
    for c in range(5):
        high, low = blade_at(c, (WRAP - 1) * WALL), blade_at(c, 0)
        first_y[c, :WALL, :] = jnp.where(even_y, high, low)
        second_y[c, :WALL, :] = jnp.where(even_y, low, high)
        high, low = pack_north(back[c], NORTH - 1), pack_north(back[c], 0)
        first_y[c, WALL:, :] = jnp.where(even_y, high, low)
        second_y[c, WALL:, :] = jnp.where(even_y, low, high)
        high, low = pack_east(back[c], EAST - 1), pack_east(back[c], 0)
        first_x[c] = jnp.where(even_x, high, low)
        second_x[c] = jnp.where(even_x, low, high)


EDGE_SHAPES = [
    jax.ShapeDtypeStruct((5, WALL + 8, CHORD), F32),
    jax.ShapeDtypeStruct((5, WALL + 8, CHORD), F32),
    jax.ShapeDtypeStruct((5, 8, DEVS), F32),
    jax.ShapeDtypeStruct((5, 8, DEVS), F32),
]


def read_halo(place_ref, first_y, second_y, first_x, second_x):
    north = place_ref[0]
    even_y = north % 2 == 0
    even_x = place_ref[1] % 2 == 0
    keep_low = jnp.where(north > 0, 1.0, 0.0)
    keep_high = jnp.where(north < DEVS // 8 - 1, 1.0, 0.0)
    both = [(first_y[c], second_y[c]) for c in range(5)]
    above = [jnp.where(even_y, a, b) for a, b in both]
    below = [jnp.where(even_y, b, a) for a, b in both]
    both = [(first_x[c], second_x[c]) for c in range(5)]
    east = [unpack_east(jnp.where(even_x, a, b), EAST - 1) for a, b in both]
    west = [unpack_east(jnp.where(even_x, b, a), 0) for a, b in both]
    south = [unpack_north(v[WALL:, :] * keep_low, 0) for v in below]
    upper = [unpack_north(v[WALL:, :] * keep_high, NORTH - 1) for v in above]
    return [v[:WALL, :] for v in below], [v[:WALL, :] for v in above], [west, east, south, upper]


def exchange(edges):
    gx, gy = lax.axis_size("gx"), lax.axis_size("gy")

    def pairs(start, stop, count):
        there = [(i, (i + 1) % count) for i in range(start, stop, 2)]
        return there + [(b, a) for a, b in there]

    first_y, second_y, first_x, second_x = edges
    got_y = lax.ppermute(first_y, "gy", pairs(0, gy, gy))
    got_x = lax.ppermute(first_x, "gx", pairs(0, gx, gx))
    got_x2 = lax.ppermute(second_x, "gx", pairs(1, gx - 1, gx))
    got_y2 = lax.ppermute(second_y, "gy", pairs(1, gy, gy))
    return got_y, got_y2, got_x, got_x2


def regroup(pieces, width):
    count = DEVS // width
    shape = next(piece.shape for piece in pieces if piece is not None)
    block = iota(shape, 1) // width
    out = []
    for b in range(count):
        total = jnp.zeros(shape, F32)
        for a in range(count):
            if pieces[a] is not None:
                total = jnp.where(block == a, lane_roll(pieces[a], (a - b) * width), total)
        out.append(total)
    return out


def ranks_of(owner_ref, out_ref):
    count = owner_ref.shape[1]
    earlier = jnp.where(iota((256, 256), 0) < iota((256, 256), 1), 1.0, 0.0).astype(BF16)
    carry = jnp.zeros((DEVS, 1), F32)
    for start in range(0, count, 256):
        marks = one_hot(DEVS, owner_ref[:, start : start + 256])
        before = dot_nn(marks.astype(BF16), earlier) + carry
        out_ref[:, start : start + 256] = jnp.sum(marks * before, axis=0, keepdims=True).astype(
            jnp.int32
        )
        carry = carry + jnp.sum(marks, axis=1, keepdims=True)


def send_rows(values, owner, rank, slots):
    seats = one_hot(slots, rank)
    terms = jnp.concatenate([seats * v for v in values], axis=0)
    return exact_nt(terms, one_hot(DEVS, owner).astype(BF16))


def hole_parts(cell):
    row = ((cell >> 6) & (NORTH - 1)) * EAST + (cell >> 9)
    return row, cell & (VERT - 1)


def hole_values(low_half, cell):
    row, vert = hole_parts(cell)
    seats = one_hot(HALF, vert)
    table = dot_nn(low_half, twice(one_hot(DEVS, row).astype(BF16)))
    return [
        jnp.sum(table[n : n + HALF] * seats, axis=0, keepdims=True)
        for n in range(0, table.shape[0], HALF)
    ]


def hole_mask(cell_ref):
    total = jnp.zeros((HALF, DEVS), F32)
    for start in range(0, HOLES, 512):
        row, vert = hole_parts(cell_ref[:, start : start + 512])
        total = total + dot_nt(one_hot(HALF, vert).astype(BF16), one_hot(DEVS, row).astype(BF16))
    return total


CHUNK = 512


def chunk_lanes(n):
    return pl.ds(pl.multiple_of(n * CHUNK, CHUNK), CHUNK)


def lanes_of(ref, n, k):
    count = CHUNK // DEVS
    return jnp.concatenate([ref[k, pl.ds(n * count + m, 1), :] for m in range(count)], axis=1)


def store_chunk(out, n, values):
    for c in range(5):
        for m in range(CHUNK // DEVS):
            row = pl.ds(n * (CHUNK // DEVS) + m, 1)
            out[c, row, :] = values[c][:, m * DEVS : (m + 1) * DEVS]


def edge_kernel(place, cot, back_cot, cot_planes, first_y, second_y, first_x, second_x):
    cots = []
    for c in range(5):
        turned = to_planes(back_cot[c])
        cot_planes[c] = turned
        cots.append(turned)
    store_edges(
        place, lambda c, r: cot[c, r : r + WALL, :], cots, (first_y, second_y, first_x, second_x)
    )


def start_kernel(
    blade, back, back_base, back_weight, blade_base, blade_weight,
    send, back_planes,
    blade_parts, back_parts, hole_vals, rim_vals,
):
    for c in range(5):
        store_parts(blade_parts, c * CHORD, CHORD, blade[c].T)
        field = to_planes(back[c])
        back_planes[c] = field
        store_parts(back_parts, c * HALF, HALF, field[HALF:, :])

    def blade_step(n, carry):
        lanes = chunk_lanes(n)
        rows, cols = blade_donors(blade_base[0:1, lanes], blade_weight[0, :, lanes])
        store_chunk(hole_vals, n, picked(blade_parts, rows, cols))
        return carry

    lax.fori_loop(0, 2 * HOLES // CHUNK, blade_step, 0, unroll=2)

    def back_step(n, carry):
        lanes = chunk_lanes(n)
        rows, cols = back_donors(back_base[0:1, lanes], back_weight[0, :, lanes])
        store_chunk(rim_vals, n, picked(back_parts, rows, cols))
        return carry

    lax.fori_loop(0, 2 * RIMS // CHUNK, back_step, 0)
    store_slots(hole_vals, rim_vals, send)


def store_slots(hole_vals, rim_vals, send):
    first = regroup([hole_vals[c] for c in range(4)], QH)
    fifth = hole_vals[4]
    tail = regroup([fifth, None, None, None], QH)
    for d in range(DEVS // QH):
        send[pl.ds(d, QH, stride=DEVS // QH), 0, :] = first[d]
        send[pl.ds(d, QH, stride=DEVS // QH), 1, :] = tail[d]
    rims = regroup([None, None] + [rim_vals[c] for c in range(5)] + [None], QR)
    lane = iota((QR, DEVS), 1)
    for d in range(DEVS // QR):
        rows = pl.ds(d, QR, stride=DEVS // QR)
        send[rows, 1, :] = jnp.where(lane < QH, send[rows, 1, :], rims[d])


def cot_kernel(
    place, blade_m, back_m, cot, cot_planes, got_y, got_y2, got_x, got_x2,
    rim_owner, hole_owner, hole_cell,
    send, blade_fields, back_fields, rim_rank, hole_rank,
):
    low, high, halo = read_halo(place, got_y, got_y2, got_x, got_x2)
    for j in range(WRAP):
        center, sides = blade_sides(cot, low, high, j)
        fields = linear_fields(blade_m, center, sides)
        for n in range(FIELDS):
            blade_fields[n, j * WALL : (j + 1) * WALL, :] = fields[n]
    center = [cot_planes[c] for c in range(5)]
    fields = linear_fields(back_m, center, back_sides(center, halo))
    for n in range(FIELDS):
        back_fields[n] = fields[n]
    for step in range(2):
        ranks_of(rim_owner.at[step], rim_rank.at[step])
        ranks_of(hole_owner.at[step], hole_rank.at[step])

    total = jnp.zeros((FIELDS * QR, DEVS), F32)
    for j in range(WRAP):
        lanes = slice(j * 256, j * 256 + 256)
        top = j * WALL + WALL - 2
        values = [
            jnp.concatenate(
                [blade_fields[n, top + k : top + k + 1, :] for k in range(2)], axis=1
            )
            for n in range(FIELDS)
        ]
        total = total + send_rows(values, rim_owner[1, :, lanes], rim_rank[1, :, lanes], QR)
    total = jnp.concatenate([total, jnp.zeros((112, DEVS), F32)], axis=0)
    for m in range(3):
        send[:, 5 + m, :] = total[m * DEVS : (m + 1) * DEVS].T
    total = jnp.zeros((FIELDS * QH, DEVS), F32)
    low_half = doubled(jnp.concatenate([back_fields[n, :HALF, :] for n in range(FIELDS)], axis=0))
    for start in range(0, HOLES, 512):
        lanes = slice(start, start + 512)
        values = hole_values(low_half, hole_cell[1:2, lanes])
        total = total + send_rows(values, hole_owner[1, :, lanes], hole_rank[1, :, lanes], QH)
    total = jnp.concatenate([total, jnp.zeros((96, DEVS), F32)], axis=0)
    for m in range(5):
        send[:, m, :] = total[m * DEVS : (m + 1) * DEVS].T


def fill_kernel(
    place, blade, back_planes, recv, rim_owner, hole_owner, rim_rank, hole_rank, hole_cell,
    blade_first, back_first, first_y, second_y, first_x, second_x,
):
    arrived = doubled(jnp.concatenate([recv[:, 0, :].T, recv[:, 1, :].T], axis=0))
    for c in range(5):
        for j in range(WRAP):
            rows = slice(j * WALL, (j + 1) * WALL)
            blade_first[c, rows, :] = blade[c, rows, :]
    base = 5 * QH
    for j in range(WRAP):
        lanes = slice(j * 256, j * 256 + 256)
        marks = one_hot(DEVS, rim_owner[0, :, lanes]).astype(BF16)
        seats = one_hot(QR, rim_rank[0, :, lanes])
        table = dot_nn(arrived[base : base + 5 * QR], twice(marks))
        for c in range(5):
            value = jnp.sum(table[c * QR : (c + 1) * QR] * seats, axis=0, keepdims=True)
            for k in range(2):
                row = j * WALL + WALL - 2 + k
                blade_first[c, row : row + 1, :] = value[:, k * CHORD : (k + 1) * CHORD]
    filled = jnp.zeros((6 * HALF, DEVS), F32)
    for start in range(0, HOLES, 512):
        lanes = slice(start, start + 512)
        marks = one_hot(DEVS, hole_owner[0, :, lanes]).astype(BF16)
        seats = one_hot(QH, hole_rank[0, :, lanes])
        row, vert = hole_parts(hole_cell[0:1, lanes])
        vert_marks = one_hot(HALF, vert)
        table = dot_nn(arrived[:base], twice(marks))
        terms = [
            vert_marks * jnp.sum(table[c * QH : (c + 1) * QH] * seats, axis=0, keepdims=True)
            for c in range(5)
        ]
        terms = jnp.concatenate(terms + [vert_marks], axis=0)
        filled = filled + exact_nt(terms, one_hot(DEVS, row).astype(BF16))
    mask = filled[5 * HALF :]
    backs = []
    for c in range(5):
        top = jnp.where(mask > 0.5, filled[c * HALF : (c + 1) * HALF], back_planes[c, :HALF, :])
        field = jnp.concatenate([top, back_planes[c, HALF:, :]], axis=0)
        back_first[c] = field
        backs.append(field)
    store_edges(
        place,
        lambda c, r: blade_first[c, r : r + WALL, :],
        backs,
        (first_y, second_y, first_x, second_x),
    )


def residual_step(center, halo_flux):
    out = [center[c] * (1.0 - 6.0 * damping * time_step) for c in range(5)]
    for t in range(3):
        upper, lower = halo_flux(t)
        for c in range(5):
            out[c] = out[c] - upper[c] + lower[c]
    return out


def side_terms(m_ref, t, v):
    flux = flux_of(m_ref, t, v)
    damped = [damping * time_step * v[c] for c in range(5)]
    upper = [flux[c] - damped[c] for c in range(5)]
    lower = [flux[c] + damped[c] for c in range(5)]
    return upper, lower


def middle_kernel(
    place, blade_m, back_m, blade_first, back_first, got_y, got_y2, got_x, got_x2,
    blade_fields, back_fields, recv, back_base, back_weight, blade_base, blade_weight, hole_cell,
    blade_mid, back_mid, first_y, second_y, first_x, second_x,
    blade_next, back_next, blade_parts, back_parts, hole_lin, rim_lin, blade_acc, back_acc,
):
    low, high, halo = read_halo(place, got_y, got_y2, got_x, got_x2)

    planes = [low]
    for j in range(WRAP):
        planes.append([blade_first[c, j * WALL : (j + 1) * WALL, :] for c in range(5)])
    planes.append(high)
    turns = [side_terms(blade_m, 0, plane) for plane in planes]
    for j in range(WRAP):
        center = planes[j + 1]

        def around(t, j=j, center=center):
            if t == 0:
                return turns[j + 2][0], turns[j][1]
            upper, lower = side_terms(blade_m, t, center)
            if t == 1:
                return [wall_shift(v, True) for v in upper], [wall_shift(v, False) for v in lower]
            return (
                [lane_shift(v, True, 1, CHORD, 0.0) for v in upper],
                [lane_shift(v, False, 1, CHORD, 0.0) for v in lower],
            )

        out = residual_step(center, around)
        for c in range(5):
            blade_next[c, j * WALL : (j + 1) * WALL, :] = out[c]
    center = [back_first[c] for c in range(5)]

    def across(t):
        upper, lower = side_terms(back_m, t, center)
        if t == 2:
            return [wall_shift(v, True) for v in upper], [wall_shift(v, False) for v in lower]
        width, period = ((1, EAST), (EAST, NORTH))[t]
        below = side_terms(back_m, t, halo[2 * t])[1]
        above = side_terms(back_m, t, halo[2 * t + 1])[0]
        return (
            [lane_shift(upper[c], True, width, period, above[c]) for c in range(5)],
            [lane_shift(lower[c], False, width, period, below[c]) for c in range(5)],
        )

    out = residual_step(center, across)
    for c in range(5):
        back_next[c] = out[c]
        store_parts(back_parts, c * HALF, HALF, out[c][HALF:, :])
        store_parts(blade_parts, c * CHORD, CHORD, blade_next[c].T)

    for j in range(WRAP):
        rows = slice(j * WALL, (j + 1) * WALL)
        v = [blade_next[c, rows, :] for c in range(5)]
        own = apply_fields([blade_fields[n, rows, :] for n in range(FIELDS)], v)
        inside = iota((WALL, CHORD), 0) < WALL - 2
        for c in range(5):
            blade_mid[c, rows, :] = jnp.where(inside, own[c], 0.0)
    mask = hole_mask(hole_cell.at[1:2])
    own = apply_fields([back_fields[n] for n in range(FIELDS)], [back_next[c] for c in range(5)])
    for c in range(5):
        back_mid[c, :HALF, :] = jnp.where(mask > 0.5, 0.0, own[c][:HALF, :])
        back_mid[c, HALF:, :] = own[c][HALF:, :]

    for m in range(5):
        pieces = [recv[pl.ds(d, QH, stride=DEVS // QH), m, :] for d in range(DEVS // QH)]
        for b, piece in enumerate(regroup(pieces, QH)):
            if m * 4 + b < FIELDS:
                hole_lin[m * 4 + b] = piece
    for m in range(3):
        pieces = [recv[pl.ds(d, QR, stride=DEVS // QR), 5 + m, :] for d in range(DEVS // QR)]
        for b, piece in enumerate(regroup(pieces, QR)):
            if m * 8 + b < FIELDS:
                rim_lin[m * 8 + b] = piece

    blade_acc[...] = jnp.zeros(blade_acc.shape, F32)
    back_acc[...] = jnp.zeros(back_acc.shape, F32)

    def blade_step(n, carry):
        lanes = chunk_lanes(n)
        rows, cols = blade_donors(blade_base[1:2, lanes], blade_weight[1, :, lanes])
        value = picked(blade_parts, rows, cols)
        mu = apply_fields([lanes_of(hole_lin, n, k) for k in range(FIELDS)], value)
        blade_acc[...] += spread_terms(rows, cols, mu)
        return carry

    lax.fori_loop(0, 2 * HOLES // CHUNK, blade_step, 0, unroll=2)

    def back_step(n, carry):
        lanes = chunk_lanes(n)
        rows, cols = back_donors(back_base[1:2, lanes], back_weight[1, :, lanes])
        value = picked(back_parts, rows, cols)
        mu = apply_fields([lanes_of(rim_lin, n, k) for k in range(FIELDS)], value)
        back_acc[...] += spread_terms(rows, cols, mu)
        return carry

    lax.fori_loop(0, 2 * RIMS // CHUNK, back_step, 0)
    for c in range(5):
        blade_mid[c] = blade_mid[c] + blade_acc[c * CHORD : (c + 1) * CHORD, :].T
        back_mid[c, HALF:, :] = back_mid[c, HALF:, :] + back_acc[c * HALF : (c + 1) * HALF, :]
    store_edges(
        place,
        lambda c, r: blade_mid[c, r : r + WALL, :],
        [back_mid[c] for c in range(5)],
        (first_y, second_y, first_x, second_x),
    )


def give_kernel(
    place, blade_m, back_m, blade_first, back_first, blade_mid, back_mid,
    got_y, got_y2, got_x, got_x2,
    rim_owner, hole_owner, rim_rank, hole_rank, hole_cell,
    send,
):
    low, high, halo = read_halo(place, got_y, got_y2, got_x, got_x2)
    rims = jnp.zeros((5 * QR, DEVS), F32)
    for j in range(WRAP):
        outer = slice(WALL - 8, WALL)
        rows = slice(j * WALL + WALL - 8, (j + 1) * WALL)
        center, sides = blade_sides(blade_mid, low, high, j, outer)
        out = adjoint_at(blade_m, [blade_first[c, rows, :] for c in range(5)], center, sides)
        values = [jnp.concatenate([out[c][6:7, :], out[c][7:8, :]], axis=1) for c in range(5)]
        lanes = slice(j * 256, j * 256 + 256)
        rims = rims + send_rows(values, rim_owner[0, :, lanes], rim_rank[0, :, lanes], QR)
    part = HALF + 8
    center = [back_mid[c, :part, :] for c in range(5)]
    halo = [[v[:part, :] for v in side] for side in halo]
    out = adjoint_at(
        back_m, [back_first[c, :part, :] for c in range(5)], center, back_sides(center, halo)
    )
    holes = jnp.zeros((5 * QH, DEVS), F32)
    low_half = doubled(jnp.concatenate([out[c][:HALF, :] for c in range(5)], axis=0))
    for start in range(0, HOLES, 512):
        lanes = slice(start, start + 512)
        values = hole_values(low_half, hole_cell[0:1, lanes])
        holes = holes + send_rows(values, hole_owner[0, :, lanes], hole_rank[0, :, lanes], QH)
    rest = jnp.zeros((2 * DEVS - 5 * QH - 5 * QR, DEVS), F32)
    total = jnp.concatenate([holes, rims, rest], axis=0)
    send[:, 0, :] = total[:DEVS].T
    send[:, 1, :] = total[DEVS:].T


def keep_kernel(
    place, blade_m, back_m, blade_first, back_first, blade_mid, back_mid,
    got_y, got_y2, got_x, got_x2, hole_cell,
    blade_kept, back_kept,
):
    low, high, halo = read_halo(place, got_y, got_y2, got_x, got_x2)
    for j in range(WRAP):
        rows = slice(j * WALL, (j + 1) * WALL)
        center, sides = blade_sides(blade_mid, low, high, j)
        out = adjoint_at(blade_m, [blade_first[c, rows, :] for c in range(5)], center, sides)
        inside = iota((WALL, CHORD), 0) < WALL - 2
        for c in range(5):
            blade_kept[c, rows, :] = jnp.where(inside, out[c], 0.0)
    center = [back_mid[c] for c in range(5)]
    out = adjoint_at(back_m, [back_first[c] for c in range(5)], center, back_sides(center, halo))
    mask = hole_mask(hole_cell.at[0:1])
    for c in range(5):
        back_kept[c, :HALF, :] = jnp.where(mask > 0.5, 0.0, out[c][:HALF, :])
        back_kept[c, HALF:, :] = out[c][HALF:, :]


def end_kernel(
    blade_kept, back_kept, recv, back_base, back_weight, blade_base, blade_weight,
    blade_out, back_out, hole_mu, rim_mu, blade_acc, back_acc,
):
    count = DEVS // QH
    pieces = [recv[pl.ds(d, QH, stride=count), 0, :] for d in range(count)]
    for c, piece in enumerate(regroup(pieces, QH)):
        hole_mu[c] = piece
    pieces = [recv[pl.ds(d, QH, stride=count), 1, :] for d in range(count)]
    hole_mu[4] = regroup(pieces, QH)[0]
    count = DEVS // QR
    pieces = [recv[pl.ds(d, QR, stride=count), 1, :] for d in range(count)]
    groups = regroup(pieces, QR)
    for c in range(5):
        rim_mu[c] = groups[QH // QR + c]
    blade_acc[...] = jnp.zeros(blade_acc.shape, F32)
    back_acc[...] = jnp.zeros(back_acc.shape, F32)

    def blade_step(n, carry):
        lanes = chunk_lanes(n)
        rows, cols = blade_donors(blade_base[0:1, lanes], blade_weight[0, :, lanes])
        blade_acc[...] += spread_terms(rows, cols, [lanes_of(hole_mu, n, c) for c in range(5)])
        return carry

    lax.fori_loop(0, 2 * HOLES // CHUNK, blade_step, 0, unroll=2)

    def back_step(n, carry):
        lanes = chunk_lanes(n)
        rows, cols = back_donors(back_base[0:1, lanes], back_weight[0, :, lanes])
        back_acc[...] += spread_terms(rows, cols, [lanes_of(rim_mu, n, c) for c in range(5)])
        return carry

    lax.fori_loop(0, 2 * RIMS // CHUNK, back_step, 0)
    for c in range(5):
        blade_out[c] = blade_kept[c] + blade_acc[c * CHORD : (c + 1) * CHORD, :].T
        top = back_kept[c, HALF:, :] + back_acc[c * HALF : (c + 1) * HALF, :]
        parts = from_planes(jnp.concatenate([back_kept[c, :HALF, :], top], axis=0))
        for y in range(0, NORTH, 2):
            back_out[c, :, y * VERT : (y + 2) * VERT] = jnp.concatenate(parts[y : y + 2], axis=1)


VMEM = pl.BlockSpec(memory_space=pltpu.VMEM)
SMEM = pl.BlockSpec(memory_space=pltpu.SMEM)
BLADE = jax.ShapeDtypeStruct((5, WRAP * WALL, CHORD), F32)
PLANES = jax.ShapeDtypeStruct((5, VERT, DEVS), F32)
DONOR_PARTS = [
    pltpu.VMEM((5 * CHORD, 3 * WRAP * WALL), BF16),
    pltpu.VMEM((5 * HALF, 3 * DEVS), BF16),
]
SUMS = [pltpu.VMEM((5 * CHORD, WRAP * WALL), F32), pltpu.VMEM((5 * HALF, DEVS), F32)]


def run(kernel, args, out_shape, scratch=(), scalars=0, flops=0):
    size = sum(4 * a.size for a in args) + sum(4 * o.size for o in out_shape)
    return pl.pallas_call(
        kernel,
        out_shape=list(out_shape),
        in_specs=[SMEM] * scalars + [VMEM] * (len(args) - scalars),
        out_specs=[VMEM] * len(out_shape),
        scratch_shapes=list(scratch),
        cost_estimate=pl.CostEstimate(flops=flops, bytes_accessed=size, transcendentals=0),
    )(*args)


def swap(rows):
    return lax.all_to_all(rows, ("gx", "gy"), split_axis=0, concat_axis=0, tiled=True)


def body(
    blade_state,
    back_state,
    blade_cotangent,
    back_cotangent,
    blade_flux,
    back_flux,
    blade_owner,
    back_donor_cell,
    back_donor_weight,
    hole_cell,
    hole_owner,
    blade_donor_cell,
    blade_donor_weight,
):
    shape = jax.ShapeDtypeStruct
    place = jnp.stack([lax.axis_index("gy"), lax.axis_index("gx")]).astype(jnp.int32)
    blade = blade_state.reshape(5, WRAP * WALL, CHORD)
    cot = blade_cotangent.reshape(5, WRAP * WALL, CHORD)
    matrices = (blade_flux.reshape(3, 25), back_flux.reshape(3, 25))
    scaled = tuple(0.5 * time_step * m for m in matrices)
    owners = (blade_owner.reshape(2, 1, RIMS), hole_owner.reshape(2, 1, HOLES))
    tables = (back_donor_cell, back_donor_weight, blade_donor_cell, blade_donor_weight)

    cot_planes, *edges = run(
        edge_kernel, (place, cot, back_cotangent), [PLANES] + EDGE_SHAPES, scalars=1
    )
    cot_halo = exchange(edges)
    send, back_planes = run(
        start_kernel,
        (blade, back_state) + tables,
        [shape((DEVS, 2, DEVS), F32), PLANES],
        DONOR_PARTS + [pltpu.VMEM((5, QH, DEVS), F32), pltpu.VMEM((5, QR, DEVS), F32)],
        flops=5 * 10**9,
    )
    recv = swap(send)
    lin_send, blade_fields, back_fields, rim_rank, hole_rank = run(
        cot_kernel,
        (place, *matrices, cot, cot_planes, *cot_halo, *owners, hole_cell),
        [
            shape((DEVS, 8, DEVS), F32),
            shape((FIELDS, WRAP * WALL, CHORD), F32),
            shape((FIELDS, VERT, DEVS), F32),
            shape((2, 1, RIMS), jnp.int32),
            shape((2, 1, HOLES), jnp.int32),
        ],
        scalars=3,
        flops=2 * 10**9,
    )
    lin_recv = swap(lin_send)
    slots = (*owners, rim_rank, hole_rank, hole_cell)
    blade_first, back_first, *edges = run(
        fill_kernel,
        (place, blade, back_planes, recv) + slots,
        [BLADE, PLANES] + EDGE_SHAPES,
        scalars=1,
        flops=10**9,
    )
    first_halo = exchange(edges)
    blade_mid, back_mid, *edges = run(
        middle_kernel,
        (place, *scaled, blade_first, back_first, *first_halo, blade_fields, back_fields)
        + (lin_recv,)
        + tables
        + (hole_cell,),
        [BLADE, PLANES] + EDGE_SHAPES,
        [pltpu.VMEM(BLADE.shape, F32), pltpu.VMEM(PLANES.shape, F32)]
        + DONOR_PARTS
        + [pltpu.VMEM((FIELDS, QH, DEVS), F32), pltpu.VMEM((FIELDS, QR, DEVS), F32)]
        + SUMS,
        scalars=3,
        flops=10**10,
    )
    mid_halo = exchange(edges)
    both = (place, *matrices, blade_first, back_first, blade_mid, back_mid, *mid_halo)
    (send,) = run(give_kernel, both + slots, [shape((DEVS, 2, DEVS), F32)], scalars=3, flops=10**9)
    recv = swap(send)
    blade_kept, back_kept = run(
        keep_kernel, both + (hole_cell,), [BLADE, PLANES], scalars=3, flops=10**9
    )
    blade_last, back_last = run(
        end_kernel,
        (blade_kept, back_kept, recv) + tables,
        [BLADE, shape((5, EAST, NORTH * VERT), F32)],
        [pltpu.VMEM((5, QH, DEVS), F32), pltpu.VMEM((5, QR, DEVS), F32)] + SUMS,
        flops=5 * 10**9,
    )
    return (blade_last.reshape(blade_state.shape), back_last)


def solution(mesh):
    return jax.shard_map(
        body,
        mesh=mesh,
        in_specs=(
            P(None, "gx", "gy"),
            P(None, "gx", "gy"),
            P(None, "gx", "gy"),
            P(None, "gx", "gy"),
            P(),
            P(),
            P(None, ("gx", "gy"), None),
            P(None, ("gx", "gy")),
            P(None, None, ("gx", "gy")),
            P(None, ("gx", "gy")),
            P(None, ("gx", "gy"), None),
            P(None, ("gx", "gy")),
            P(None, None, ("gx", "gy")),
        ),
        out_specs=(P(None, "gx", "gy"), P(None, "gx", "gy")),
        check_vma=False,
    )
```

```python
import jax
import jax.numpy as jnp
from jax import lax
from jax.experimental import pallas as pl
from jax.experimental.pallas import tpu as pltpu
from jax.sharding import PartitionSpec as P


DEVS = 128
WRAP = 4
WALL = 64
CHORD = 128
EAST = 16
NORTH = 8
VERT = 64
HALF = VERT // 2
RIMS = 1024
HOLES = 2048
QR = 2 * RIMS // DEVS
QH = 2 * HOLES // DEVS
FIELDS = 17

time_step = 0.2
damping = 0.1

F32 = jnp.float32
BF16 = jnp.bfloat16


def split(x):
    hi = x.astype(BF16)
    return hi, (x - hi.astype(F32)).astype(BF16)


def dot_nn(a, b):
    return lax.dot_general(a, b, (((1,), (0,)), ((), ())), preferred_element_type=F32)


def dot_nt(a, b):
    return lax.dot_general(a, b, (((1,), (1,)), ((), ())), preferred_element_type=F32)


def iota(shape, dim):
    return lax.broadcasted_iota(jnp.int32, shape, dim)


def one_hot(rows, index):
    return jnp.where(iota((rows, index.shape[1]), 0) == index, 1.0, 0.0)


def pair_hot(rows, index, first, second):
    position = iota((rows, index.shape[1]), 0)
    return jnp.where(position == index, first, jnp.where(position == index + 1, second, 0.0))


def lane_roll(x, amount):
    amount = amount % x.shape[-1]
    return pltpu.roll(x, amount, x.ndim - 1) if amount else x


def to_planes(block):
    rows = [block[:, y * VERT : (y + 1) * VERT] for y in range(NORTH)]
    return jnp.concatenate(rows, axis=0).T


def from_planes(field):
    turned = field.T
    return [turned[y * EAST : (y + 1) * EAST, :] for y in range(NORTH)]


def donor_parts(weights):
    w = [weights[corner : corner + 1, :] for corner in range(8)]
    x0 = (w[0] + w[1]) + (w[2] + w[3])
    x1 = (w[4] + w[5]) + (w[6] + w[7])
    y0 = (w[0] + w[1]) + (w[4] + w[5])
    y1 = (w[2] + w[3]) + (w[6] + w[7])
    z0 = (w[0] + w[2]) + (w[4] + w[6])
    z1 = (w[1] + w[3]) + (w[5] + w[7])
    return x0, x1, y0, y1, z0, z1


def short_marks(size, index):
    position = iota((size, index.shape[1]), 0).astype(jnp.int16)
    return position == index.astype(jnp.int16), position == (index + 1).astype(jnp.int16)


def pair_split(marks, first, second):
    (first_hi, first_lo), (second_hi, second_lo) = split(first), split(second)
    zero = jnp.zeros((), BF16)

    def place(a, b):
        return jnp.where(marks[0], a, jnp.where(marks[1], b, zero))

    return place(first_hi, second_hi), place(first_lo, second_lo)


def donor_rows(outer, outer_index, outer_pair, inner, inner_index, inner_pair):
    hot = pair_hot(outer, outer_index, *outer_pair)
    marks = short_marks(inner, inner_index)
    parts = [
        pair_split(marks, hot[n : n + 1, :] * inner_pair[0], hot[n : n + 1, :] * inner_pair[1])
        for n in range(outer)
    ]
    return tuple(jnp.concatenate([p[k] for p in parts], axis=0) for k in range(2))


def blade_donors(base, weights):
    x0, x1, y0, y1, z0, z1 = donor_parts(weights)
    wall = (base >> 7) & (WALL - 1)
    rows = donor_rows(WRAP, base >> 13, (x0, x1), WALL, wall, (y0, y1))
    return rows, (CHORD, base & (CHORD - 1), z0, z1)


def back_donors(base, weights):
    x0, x1, y0, y1, z0, z1 = donor_parts(weights)
    north = (base >> 6) & (NORTH - 1)
    rows = donor_rows(NORTH, north, (y0, y1), EAST, base >> 9, (x0, x1))
    return rows, (HALF, (base & (VERT - 1)) - HALF, z0, z1)


def triple_rows(rows):
    hi, lo = rows
    return jnp.concatenate([hi, lo, hi], axis=0)


def triple_lanes(rows):
    hi, lo = rows
    return jnp.concatenate([hi, hi, lo], axis=1)


def store_parts(target, place, size, field):
    hi, lo = split(field)
    rows = slice(place, place + size)
    target[rows, :] = jnp.concatenate([hi, hi, lo], axis=1)


def picked(parts, rows, cols):
    size = cols[0]
    hot = pair_hot(*cols)
    table = dot_nn(parts[...], triple_rows(rows))
    return [
        jnp.sum(table[c * size : (c + 1) * size] * hot, axis=0, keepdims=True) for c in range(5)
    ]


def spread_terms(rows, cols, mu):
    size, index, first, second = cols
    pairs = [(first * mu[c], second * mu[c]) for c in range(5)]
    tiles = {c: [] for c in range(5)}
    for start in range(0, size, 16):
        marks = short_marks(16, index - start)
        for c in range(5):
            tiles[c].append(pair_split(marks, *pairs[c]))
    hi, lo = (
        jnp.concatenate([t[k] for c in range(5) for t in tiles[c]], axis=0) for k in range(2)
    )
    return dot_nt(jnp.concatenate([hi, lo, hi], axis=1), triple_lanes(rows))


def exact_nt(terms, marks):
    hi, lo = split(terms)
    return dot_nt(jnp.concatenate([hi, lo], axis=1), jnp.concatenate([marks, marks], axis=1))


def doubled(field):
    hi, lo = split(field)
    return jnp.concatenate([hi, lo], axis=1)


def twice(marks):
    return jnp.concatenate([marks, marks], axis=0)


def wall_shift(v, up):
    position = iota(v.shape, 0)
    if up:
        return jnp.where(position == v.shape[0] - 1, 0.0, pltpu.roll(v, v.shape[0] - 1, 0))
    return jnp.where(position == 0, 0.0, pltpu.roll(v, 1, 0))


def lane_shift(v, up, width, period, fill):
    place = (iota(v.shape, 1) // width) % period
    if up:
        return jnp.where(place == period - 1, fill, lane_roll(v, -width))
    return jnp.where(place == 0, fill, lane_roll(v, width))


class Matrices:
    def __init__(self, ref, start):
        self.ref, self.start = ref, start

    def __getitem__(self, place):
        return self.ref[self.start + place[0], place[1]]


def flux_of(m_ref, t, v, scaled):
    out = []
    for c in range(5):
        total = v[1 + t] * scaled[c]
        for e in range(5):
            total = total + m_ref[t, c * 5 + e] * scaled[e]
        out.append(total)
    return out


def turned_of(m_ref, t, w):
    out = []
    for c in range(5):
        total = m_ref[t, c] * w[0]
        for e in range(1, 5):
            total = total + m_ref[t, e * 5 + c] * w[e]
        out.append(total)
    return out


PAIRS = [(0, 1), (0, 2), (0, 3), (4, 1), (4, 2), (4, 3), (1, 1), (1, 2), (1, 3), (2, 2), (2, 3), (3, 3)]


def linear_fields(m_ref, center, sides):
    base = [center[c] * (1.0 - 6.0 * damping * time_step) for c in range(5)]
    jumps = []
    for t, (upper, lower) in enumerate(sides):
        jump = [0.5 * time_step * (lower[c] - upper[c]) for c in range(5)]
        turned = turned_of(m_ref, t, jump)
        for c in range(5):
            base[c] = base[c] - turned[c] + damping * time_step * (upper[c] + lower[c])
        jumps.append(jump)
    out = list(base)
    for a, b in PAIRS:
        if a in (0, 4):
            out.append(jumps[b - 1][a])
        else:
            out.append(jumps[a - 1][b] + jumps[b - 1][a])
    return out


def apply_fields(fields, v):
    out = []
    table = {pair: 5 + n for n, pair in enumerate(PAIRS)}
    for c in range(5):
        total = fields[c]
        for e in range(5):
            key = (c, e) if (c, e) in table else (e, c)
            if key in table:
                total = total - fields[table[key]] * v[e]
        out.append(total)
    return out


def adjoint_at(m_ref, v, center, sides):
    out = [center[c] * (1.0 - 6.0 * damping * time_step) for c in range(5)]
    for t, (upper, lower) in enumerate(sides):
        jump = [0.5 * time_step * (lower[c] - upper[c]) for c in range(5)]
        turned = turned_of(m_ref, t, jump)
        inner = v[0] * jump[0]
        for e in range(1, 5):
            inner = inner + v[e] * jump[e]
        for c in range(5):
            total = turned[c] + v[1 + t] * jump[c]
            if c == 1 + t:
                total = total + inner
            out[c] = out[c] - total + damping * time_step * (upper[c] + lower[c])
    return out


def blade_sides(ref, low, high, j):
    def plane(n):
        if n < 0 or n >= WRAP:
            return low if n < 0 else high
        return [ref[c, n * WALL : (n + 1) * WALL, :] for c in range(5)]

    center, above, below = plane(j), plane(j + 1), plane(j - 1)
    wall = ([wall_shift(v, True) for v in center], [wall_shift(v, False) for v in center])
    span = (
        [lane_shift(v, True, 1, CHORD, 0.0) for v in center],
        [lane_shift(v, False, 1, CHORD, 0.0) for v in center],
    )
    return center, [(above, below), wall, span]


def back_sides(center, halo):
    east = (
        [lane_shift(v, True, 1, EAST, halo[1][c]) for c, v in enumerate(center)],
        [lane_shift(v, False, 1, EAST, halo[0][c]) for c, v in enumerate(center)],
    )
    north = (
        [lane_shift(v, True, EAST, NORTH, halo[3][c]) for c, v in enumerate(center)],
        [lane_shift(v, False, EAST, NORTH, halo[2][c]) for c, v in enumerate(center)],
    )
    vert = ([wall_shift(v, True) for v in center], [wall_shift(v, False) for v in center])
    return [east, north, vert]


def pack_east(v, x):
    lane = iota((8, DEVS), 1)
    out = jnp.zeros((8, DEVS), F32)
    for g in range(8):
        out = jnp.where(lane % EAST == g, lane_roll(v[g * 8 : g * 8 + 8, :], g - x), out)
    return out


def unpack_east(v, x):
    return jnp.concatenate([lane_roll(v, x - g) for g in range(8)], axis=0)


def pack_north(v, y):
    lane = iota((8, DEVS), 1)
    out = jnp.zeros((8, DEVS), F32)
    for g in range(8):
        out = jnp.where(lane // EAST == g, lane_roll(v[g * 8 : g * 8 + 8, :], (g - y) * EAST), out)
    return out


def unpack_north(v, y):
    return jnp.concatenate([lane_roll(v, (y - g) * EAST) for g in range(8)], axis=0)


def store_blade_edges(ref, rows, edges, at=0):
    even_y = lax.axis_index("gy") % 2 == 0
    first_y, second_y = edges
    count = rows.stop - rows.start
    top = (WRAP - 1) * WALL
    for c in range(5):
        high, low = ref[c, top + rows.start : top + rows.stop, :], ref[c, rows, :]
        first_y[c, at : at + count, :] = jnp.where(even_y, high, low)
        second_y[c, at : at + count, :] = jnp.where(even_y, low, high)


def store_back_edges(back, edges, at):
    first_y, second_y, first_x, second_x = edges
    even_y = lax.axis_index("gy") % 2 == 0
    even_x = lax.axis_index("gx") % 2 == 0
    for c in range(5):
        high, low = pack_north(back[c], NORTH - 1), pack_north(back[c], 0)
        first_y[c, at : at + 8, :] = jnp.where(even_y, high, low)
        second_y[c, at : at + 8, :] = jnp.where(even_y, low, high)
        high, low = pack_east(back[c], EAST - 1), pack_east(back[c], 0)
        first_x[c] = jnp.where(even_x, high, low)
        second_x[c] = jnp.where(even_x, low, high)


def edge_shapes(rows):
    ends = jax.ShapeDtypeStruct((5, rows, CHORD), F32)
    sides = jax.ShapeDtypeStruct((5, 8, DEVS), F32)
    return [ends, ends, sides, sides]


def read_ends(first_y, second_y, rows):
    even_y = lax.axis_index("gy") % 2 == 0
    both = [(first_y[c, rows, :], second_y[c, rows, :]) for c in range(5)]
    return [jnp.where(even_y, b, a) for a, b in both], [jnp.where(even_y, a, b) for a, b in both]


def read_back(first_y, second_y, first_x, second_x, at):
    north = lax.axis_index("gy")
    even_x = lax.axis_index("gx") % 2 == 0
    keep_low = jnp.where(north > 0, 1.0, 0.0)
    keep_high = jnp.where(north < DEVS // 8 - 1, 1.0, 0.0)
    below, above = read_ends(first_y, second_y, slice(at, at + 8))
    both = [(first_x[c], second_x[c]) for c in range(5)]
    east = [unpack_east(jnp.where(even_x, a, b), EAST - 1) for a, b in both]
    west = [unpack_east(jnp.where(even_x, b, a), 0) for a, b in both]
    south = [unpack_north(v * keep_low, 0) for v in below]
    upper = [unpack_north(v * keep_high, NORTH - 1) for v in above]
    return [west, east, south, upper]


def exchange(edges):
    gx, gy = lax.axis_size("gx"), lax.axis_size("gy")

    def pairs(start, stop, count):
        there = [(i, (i + 1) % count) for i in range(start, stop, 2)]
        return there + [(b, a) for a, b in there]

    first_y, second_y, first_x, second_x = edges
    got_y = lax.ppermute(first_y, "gy", pairs(0, gy, gy))
    got_x = lax.ppermute(first_x, "gx", pairs(0, gx, gx))
    got_x2 = lax.ppermute(second_x, "gx", pairs(1, gx - 1, gx))
    got_y2 = lax.ppermute(second_y, "gy", pairs(1, gy, gy))
    return got_y, got_y2, got_x, got_x2


def regroup(pieces, width):
    count = DEVS // width
    shape = next(piece.shape for piece in pieces if piece is not None)
    block = iota(shape, 1) // width
    out = []
    for b in range(count):
        total = jnp.zeros(shape, F32)
        for a in range(count):
            if pieces[a] is not None:
                total = jnp.where(block == a, lane_roll(pieces[a], (a - b) * width), total)
        out.append(total)
    return out


def ranks_of(owner_ref, out_ref):
    count = owner_ref.shape[1]
    earlier = jnp.where(iota((256, 256), 0) < iota((256, 256), 1), 1.0, 0.0).astype(BF16)
    carry = jnp.zeros((DEVS, 1), F32)
    for start in range(0, count, 256):
        marks = one_hot(DEVS, owner_ref[:, start : start + 256])
        before = dot_nn(marks.astype(BF16), earlier) + carry
        out_ref[:, start : start + 256] = jnp.sum(marks * before, axis=0, keepdims=True).astype(
            jnp.int32
        )
        carry = carry + jnp.sum(marks, axis=1, keepdims=True)


def send_rows(values, owner, rank, slots):
    seats = one_hot(slots, rank)
    terms = jnp.concatenate([seats * v for v in values], axis=0)
    return exact_nt(terms, one_hot(DEVS, owner).astype(BF16))


def hole_parts(cell):
    row = ((cell >> 6) & (NORTH - 1)) * EAST + (cell >> 9)
    return row, cell & (VERT - 1)


def hole_values(low_half, cell):
    row, vert = hole_parts(cell)
    seats = one_hot(HALF, vert)
    table = dot_nn(low_half, twice(one_hot(DEVS, row).astype(BF16)))
    return [
        jnp.sum(table[n : n + HALF] * seats, axis=0, keepdims=True)
        for n in range(0, table.shape[0], HALF)
    ]


def hole_mask(cell_ref):
    total = jnp.zeros((HALF, DEVS), F32)
    for start in range(0, HOLES, 512):
        row, vert = hole_parts(cell_ref[:, start : start + 512])
        total = total + dot_nt(one_hot(HALF, vert).astype(BF16), one_hot(DEVS, row).astype(BF16))
    return total


CHUNK = 512


def chunk_lanes(n):
    return pl.ds(pl.multiple_of(n * CHUNK, CHUNK), CHUNK)


def lanes_of(ref, n, k):
    count = CHUNK // DEVS
    return jnp.concatenate([ref[k, pl.ds(n * count + m, 1), :] for m in range(count)], axis=1)


def store_chunk(out, n, values):
    for c in range(5):
        for m in range(CHUNK // DEVS):
            row = pl.ds(n * (CHUNK // DEVS) + m, 1)
            out[c, row, :] = values[c][:, m * DEVS : (m + 1) * DEVS]


def edge_kernel(blade, cot, back_cot, cot_planes, first_y, second_y, first_x, second_x):
    cots = []
    for c in range(5):
        turned = to_planes(back_cot[c])
        cot_planes[c] = turned
        cots.append(turned)
    store_blade_edges(cot, slice(0, WALL), (first_y, second_y))
    store_blade_edges(blade, slice(0, WALL - 8), (first_y, second_y), WALL + 8)
    store_back_edges(cots, (first_y, second_y, first_x, second_x), WALL)


def start_kernel(
    blade, back, back_base, back_weight, blade_base, blade_weight,
    send, back_planes,
    blade_parts, back_parts, hole_vals, rim_vals,
):
    for c in range(5):
        store_parts(blade_parts, c * CHORD, CHORD, blade[c].T)
        field = to_planes(back[c])
        back_planes[c] = field
        store_parts(back_parts, c * HALF, HALF, field[HALF:, :])

    def blade_step(n, carry):
        lanes = chunk_lanes(n)
        rows, cols = blade_donors(blade_base[0:1, lanes], blade_weight[0, :, lanes])
        store_chunk(hole_vals, n, picked(blade_parts, rows, cols))
        return carry

    lax.fori_loop(0, 2 * HOLES // CHUNK, blade_step, 0, unroll=4)

    def back_step(n, carry):
        lanes = chunk_lanes(n)
        rows, cols = back_donors(back_base[0:1, lanes], back_weight[0, :, lanes])
        store_chunk(rim_vals, n, picked(back_parts, rows, cols))
        return carry

    lax.fori_loop(0, 2 * RIMS // CHUNK, back_step, 0)
    store_slots(hole_vals, rim_vals, send)


def store_slots(hole_vals, rim_vals, send):
    first = regroup([hole_vals[c] for c in range(4)], QH)
    fifth = hole_vals[4]
    tail = regroup([fifth, None, None, None], QH)
    for d in range(DEVS // QH):
        send[pl.ds(d, QH, stride=DEVS // QH), 0, :] = first[d]
        send[pl.ds(d, QH, stride=DEVS // QH), 1, :] = tail[d]
    rims = regroup([None, None] + [rim_vals[c] for c in range(5)] + [None], QR)
    lane = iota((QR, DEVS), 1)
    for d in range(DEVS // QR):
        rows = pl.ds(d, QR, stride=DEVS // QR)
        send[rows, 1, :] = jnp.where(lane < QH, send[rows, 1, :], rims[d])


def cot_kernel(
    matrices, cot, cot_planes, got_y, got_y2, got_x, got_x2, rim_owner, hole_owner, hole_cell,
    send, blade_fields, back_fields, rim_rank, hole_rank,
):
    blade_m, back_m = Matrices(matrices, 0), Matrices(matrices, 3)
    low, high = read_ends(got_y, got_y2, slice(0, WALL))
    halo = read_back(got_y, got_y2, got_x, got_x2, WALL)
    for j in range(WRAP):
        center, sides = blade_sides(cot, low, high, j)
        fields = linear_fields(blade_m, center, sides)
        for n in range(FIELDS):
            blade_fields[n, j * WALL : (j + 1) * WALL, :] = fields[n]
    center = [cot_planes[c] for c in range(5)]
    fields = linear_fields(back_m, center, back_sides(center, halo))
    for n in range(FIELDS):
        back_fields[n] = fields[n]
    for step in range(2):
        ranks_of(rim_owner.at[step], rim_rank.at[step])
        ranks_of(hole_owner.at[step], hole_rank.at[step])

    total = jnp.zeros((FIELDS * QR, DEVS), F32)
    for j in range(WRAP):
        lanes = slice(j * 256, j * 256 + 256)
        top = j * WALL + WALL - 2
        values = [
            jnp.concatenate(
                [blade_fields[n, top + k : top + k + 1, :] for k in range(2)], axis=1
            )
            for n in range(FIELDS)
        ]
        total = total + send_rows(values, rim_owner[1, :, lanes], rim_rank[1, :, lanes], QR)
    total = jnp.concatenate([total, jnp.zeros((112, DEVS), F32)], axis=0)
    for m in range(3):
        send[:, 5 + m, :] = total[m * DEVS : (m + 1) * DEVS].T
    total = jnp.zeros((FIELDS * QH, DEVS), F32)
    low_half = doubled(jnp.concatenate([back_fields[n, :HALF, :] for n in range(FIELDS)], axis=0))
    for start in range(0, HOLES, 512):
        lanes = slice(start, start + 512)
        values = hole_values(low_half, hole_cell[1:2, lanes])
        total = total + send_rows(values, hole_owner[1, :, lanes], hole_rank[1, :, lanes], QH)
    total = jnp.concatenate([total, jnp.zeros((96, DEVS), F32)], axis=0)
    for m in range(5):
        send[:, m, :] = total[m * DEVS : (m + 1) * DEVS].T


def fill_kernel(
    blade, back_planes, recv, rim_owner, hole_owner, rim_rank, hole_rank, hole_cell,
    blade_first, back_first, first_y, second_y, first_x, second_x,
):
    arrived = doubled(jnp.concatenate([recv[:, 0, :].T, recv[:, 1, :].T], axis=0))
    for c in range(5):
        for j in range(WRAP):
            rows = slice(j * WALL, (j + 1) * WALL)
            blade_first[c, rows, :] = blade[c, rows, :]
    base = 5 * QH
    for j in range(WRAP):
        lanes = slice(j * 256, j * 256 + 256)
        marks = one_hot(DEVS, rim_owner[0, :, lanes]).astype(BF16)
        seats = one_hot(QR, rim_rank[0, :, lanes])
        table = dot_nn(arrived[base : base + 5 * QR], twice(marks))
        for c in range(5):
            value = jnp.sum(table[c * QR : (c + 1) * QR] * seats, axis=0, keepdims=True)
            for k in range(2):
                row = j * WALL + WALL - 2 + k
                blade_first[c, row : row + 1, :] = value[:, k * CHORD : (k + 1) * CHORD]
    filled = jnp.zeros((6 * HALF, DEVS), F32)
    for start in range(0, HOLES, 512):
        lanes = slice(start, start + 512)
        marks = one_hot(DEVS, hole_owner[0, :, lanes]).astype(BF16)
        seats = one_hot(QH, hole_rank[0, :, lanes])
        row, vert = hole_parts(hole_cell[0:1, lanes])
        vert_marks = one_hot(HALF, vert)
        table = dot_nn(arrived[:base], twice(marks))
        terms = [
            vert_marks * jnp.sum(table[c * QH : (c + 1) * QH] * seats, axis=0, keepdims=True)
            for c in range(5)
        ]
        terms = jnp.concatenate(terms + [vert_marks], axis=0)
        filled = filled + exact_nt(terms, one_hot(DEVS, row).astype(BF16))
    mask = filled[5 * HALF :]
    backs = []
    for c in range(5):
        top = jnp.where(mask > 0.5, filled[c * HALF : (c + 1) * HALF], back_planes[c, :HALF, :])
        field = jnp.concatenate([top, back_planes[c, HALF:, :]], axis=0)
        back_first[c] = field
        backs.append(field)
    store_blade_edges(blade_first, slice(WALL - 8, WALL), (first_y, second_y))
    store_back_edges(backs, (first_y, second_y, first_x, second_x), 8)


def residual_step(center, halo_flux):
    out = [center[c] * (1.0 - 6.0 * damping * time_step) for c in range(5)]
    for t in range(3):
        upper, lower = halo_flux(t)
        for c in range(5):
            out[c] = out[c] - upper[c] + lower[c]
    return out


def side_terms(m_ref, t, v):
    flux = flux_of(m_ref, t, v, [0.5 * time_step * v[c] for c in range(5)])
    damped = [damping * time_step * v[c] for c in range(5)]
    upper = [flux[c] - damped[c] for c in range(5)]
    lower = [flux[c] + damped[c] for c in range(5)]
    return upper, lower


def middle_kernel(
    matrices, blade_first, back_first, old_y, old_y2, got_y, got_y2, got_x, got_x2,
    blade_fields, back_fields, recv, back_base, back_weight, blade_base, blade_weight, hole_cell,
    blade_mid, back_mid, first_y, second_y, first_x, second_x,
    blade_next, back_next, blade_parts, back_parts, hole_lin, rim_lin, blade_acc, back_acc,
):
    blade_m, back_m = Matrices(matrices, 0), Matrices(matrices, 3)
    planes = zip(
        read_ends(old_y, old_y2, slice(WALL + 8, 2 * WALL)), read_ends(got_y, got_y2, slice(0, 8))
    )
    low, high = (
        [jnp.concatenate([a, b], axis=0) for a, b in zip(inner, outer)] for inner, outer in planes
    )
    halo = read_back(got_y, got_y2, got_x, got_x2, 8)

    sections = [low]
    for j in range(WRAP):
        sections.append([blade_first[c, j * WALL : (j + 1) * WALL, :] for c in range(5)])
    sections.append(high)
    turns = [side_terms(blade_m, 0, plane) for plane in sections]
    for j in range(WRAP):
        center = sections[j + 1]

        def around(t, j=j, center=center):
            if t == 0:
                return turns[j + 2][0], turns[j][1]
            upper, lower = side_terms(blade_m, t, center)
            if t == 1:
                return [wall_shift(v, True) for v in upper], [wall_shift(v, False) for v in lower]
            return (
                [lane_shift(v, True, 1, CHORD, 0.0) for v in upper],
                [lane_shift(v, False, 1, CHORD, 0.0) for v in lower],
            )

        out = residual_step(center, around)
        for c in range(5):
            blade_next[c, j * WALL : (j + 1) * WALL, :] = out[c]
    center = [back_first[c] for c in range(5)]

    def across(t):
        upper, lower = side_terms(back_m, t, center)
        if t == 2:
            return [wall_shift(v, True) for v in upper], [wall_shift(v, False) for v in lower]
        width, period = ((1, EAST), (EAST, NORTH))[t]
        below = side_terms(back_m, t, halo[2 * t])[1]
        above = side_terms(back_m, t, halo[2 * t + 1])[0]
        return (
            [lane_shift(upper[c], True, width, period, above[c]) for c in range(5)],
            [lane_shift(lower[c], False, width, period, below[c]) for c in range(5)],
        )

    out = residual_step(center, across)
    for c in range(5):
        back_next[c] = out[c]
        store_parts(back_parts, c * HALF, HALF, out[c][HALF:, :])
        store_parts(blade_parts, c * CHORD, CHORD, blade_next[c].T)

    for j in range(WRAP):
        rows = slice(j * WALL, (j + 1) * WALL)
        v = [blade_next[c, rows, :] for c in range(5)]
        own = apply_fields([blade_fields[n, rows, :] for n in range(FIELDS)], v)
        inside = iota((WALL, CHORD), 0) < WALL - 2
        for c in range(5):
            blade_mid[c, rows, :] = jnp.where(inside, own[c], 0.0)
    mask = hole_mask(hole_cell.at[1:2])
    own = apply_fields([back_fields[n] for n in range(FIELDS)], [back_next[c] for c in range(5)])
    for c in range(5):
        back_mid[c, :HALF, :] = jnp.where(mask > 0.5, 0.0, own[c][:HALF, :])
        back_mid[c, HALF:, :] = own[c][HALF:, :]

    for m in range(5):
        pieces = [recv[pl.ds(d, QH, stride=DEVS // QH), m, :] for d in range(DEVS // QH)]
        for b, piece in enumerate(regroup(pieces, QH)):
            if m * 4 + b < FIELDS:
                hole_lin[m * 4 + b] = piece
    for m in range(3):
        pieces = [recv[pl.ds(d, QR, stride=DEVS // QR), 5 + m, :] for d in range(DEVS // QR)]
        for b, piece in enumerate(regroup(pieces, QR)):
            if m * 8 + b < FIELDS:
                rim_lin[m * 8 + b] = piece

    blade_acc[...] = jnp.zeros(blade_acc.shape, F32)
    back_acc[...] = jnp.zeros(back_acc.shape, F32)

    def blade_step(n, carry):
        lanes = chunk_lanes(n)
        rows, cols = blade_donors(blade_base[1:2, lanes], blade_weight[1, :, lanes])
        value = picked(blade_parts, rows, cols)
        mu = apply_fields([lanes_of(hole_lin, n, k) for k in range(FIELDS)], value)
        blade_acc[...] += spread_terms(rows, cols, mu)
        return carry

    lax.fori_loop(0, 2 * HOLES // CHUNK, blade_step, 0, unroll=4)

    def back_step(n, carry):
        lanes = chunk_lanes(n)
        rows, cols = back_donors(back_base[1:2, lanes], back_weight[1, :, lanes])
        value = picked(back_parts, rows, cols)
        mu = apply_fields([lanes_of(rim_lin, n, k) for k in range(FIELDS)], value)
        back_acc[...] += spread_terms(rows, cols, mu)
        return carry

    lax.fori_loop(0, 2 * RIMS // CHUNK, back_step, 0)
    for c in range(5):
        blade_mid[c] = blade_mid[c] + blade_acc[c * CHORD : (c + 1) * CHORD, :].T
        back_mid[c, HALF:, :] = back_mid[c, HALF:, :] + back_acc[c * HALF : (c + 1) * HALF, :]
    store_blade_edges(blade_mid, slice(0, WALL), (first_y, second_y))
    store_back_edges(
        [back_mid[c] for c in range(5)], (first_y, second_y, first_x, second_x), WALL
    )


def inner_kernel(
    matrices, blade_first, back_first, blade_mid, back_mid, hole_cell, blade_part, back_part, mask
):
    blade_m, back_m = Matrices(matrices, 0), Matrices(matrices, 3)
    nothing = [jnp.zeros((WALL, CHORD), F32)] * 5
    for j in range(WRAP):
        rows = slice(j * WALL, (j + 1) * WALL)
        center, sides = blade_sides(blade_mid, nothing, nothing, j)
        out = adjoint_at(blade_m, [blade_first[c, rows, :] for c in range(5)], center, sides)
        for c in range(5):
            blade_part[c, rows, :] = out[c]
    nothing = [jnp.zeros((VERT, DEVS), F32)] * 5
    center = [back_mid[c] for c in range(5)]
    sides = back_sides(center, [nothing] * 4)
    out = adjoint_at(back_m, [back_first[c] for c in range(5)], center, sides)
    for c in range(5):
        back_part[c] = out[c]
    mask[...] = hole_mask(hole_cell.at[0:1])


def outside_terms(m_ref, t, v, beyond, sign):
    jump = [-sign * 0.5 * time_step * beyond[c] for c in range(5)]
    turned = turned_of(m_ref, t, jump)
    inner = v[0] * jump[0]
    for e in range(1, 5):
        inner = inner + v[e] * jump[e]
    out = []
    for c in range(5):
        total = turned[c] + v[1 + t] * jump[c]
        if c == 1 + t:
            total = total + inner
        out.append(damping * time_step * beyond[c] - total)
    return out


def last_kernel(
    matrices, blade_first, back_first, blade_part, back_part, mask,
    got_y, got_y2, got_x, got_x2,
    rim_owner, hole_owner, rim_rank, hole_rank, hole_cell,
    send, blade_kept, back_kept,
):
    blade_m, back_m = Matrices(matrices, 0), Matrices(matrices, 3)
    low, high = read_ends(got_y, got_y2, slice(0, WALL))
    halo = read_back(got_y, got_y2, got_x, got_x2, WALL)
    rims = jnp.zeros((5 * QR, DEVS), F32)
    for j in range(WRAP):
        rows = slice(j * WALL, (j + 1) * WALL)
        out = [blade_part[c, rows, :] for c in range(5)]
        if j in (0, WRAP - 1):
            v = [blade_first[c, rows, :] for c in range(5)]
            beyond, sign = (high, 1.0) if j else (low, -1.0)
            more = outside_terms(blade_m, 0, v, beyond, sign)
            out = [out[c] + more[c] for c in range(5)]
        inside = iota((WALL, CHORD), 0) < WALL - 2
        values = []
        for c in range(5):
            blade_kept[c, rows, :] = jnp.where(inside, out[c], 0.0)
            outer = [out[c][WALL - 2 + k : WALL - 1 + k, :] for k in range(2)]
            values.append(jnp.concatenate(outer, axis=1))
        lanes = slice(j * 256, j * 256 + 256)
        rims = rims + send_rows(values, rim_owner[0, :, lanes], rim_rank[0, :, lanes], QR)
    v = [back_first[c] for c in range(5)]
    out = [back_part[c] for c in range(5)]
    place = iota((VERT, DEVS), 1)
    east, north = place % EAST, place // EAST
    for t, beyond, sign, at in (
        (0, halo[0], -1.0, east == 0),
        (0, halo[1], 1.0, east == EAST - 1),
        (1, halo[2], -1.0, north == 0),
        (1, halo[3], 1.0, north == NORTH - 1),
    ):
        more = outside_terms(back_m, t, v, [jnp.where(at, x, 0.0) for x in beyond], sign)
        out = [out[c] + more[c] for c in range(5)]
    holes_here = mask[...] > 0.5
    for c in range(5):
        back_kept[c, :HALF, :] = jnp.where(holes_here, 0.0, out[c][:HALF, :])
        back_kept[c, HALF:, :] = out[c][HALF:, :]
    holes = jnp.zeros((5 * QH, DEVS), F32)
    low_half = doubled(jnp.concatenate([out[c][:HALF, :] for c in range(5)], axis=0))
    for start in range(0, HOLES, 512):
        lanes = slice(start, start + 512)
        values = hole_values(low_half, hole_cell[0:1, lanes])
        holes = holes + send_rows(values, hole_owner[0, :, lanes], hole_rank[0, :, lanes], QH)
    rest = jnp.zeros((2 * DEVS - 5 * QH - 5 * QR, DEVS), F32)
    total = jnp.concatenate([holes, rims, rest], axis=0)
    send[:, 0, :] = total[:DEVS].T
    send[:, 1, :] = total[DEVS:].T


def end_kernel(
    blade_kept, back_kept, recv, back_base, back_weight, blade_base, blade_weight,
    blade_out, back_out, hole_mu, rim_mu, blade_acc, back_acc,
):
    count = DEVS // QH
    pieces = [recv[pl.ds(d, QH, stride=count), 0, :] for d in range(count)]
    for c, piece in enumerate(regroup(pieces, QH)):
        hole_mu[c] = piece
    pieces = [recv[pl.ds(d, QH, stride=count), 1, :] for d in range(count)]
    hole_mu[4] = regroup(pieces, QH)[0]
    count = DEVS // QR
    pieces = [recv[pl.ds(d, QR, stride=count), 1, :] for d in range(count)]
    groups = regroup(pieces, QR)
    for c in range(5):
        rim_mu[c] = groups[QH // QR + c]
    blade_acc[...] = jnp.zeros(blade_acc.shape, F32)
    back_acc[...] = jnp.zeros(back_acc.shape, F32)

    def blade_step(n, carry):
        lanes = chunk_lanes(n)
        rows, cols = blade_donors(blade_base[0:1, lanes], blade_weight[0, :, lanes])
        blade_acc[...] += spread_terms(rows, cols, [lanes_of(hole_mu, n, c) for c in range(5)])
        return carry

    lax.fori_loop(0, 2 * HOLES // CHUNK, blade_step, 0, unroll=4)

    def back_step(n, carry):
        lanes = chunk_lanes(n)
        rows, cols = back_donors(back_base[0:1, lanes], back_weight[0, :, lanes])
        back_acc[...] += spread_terms(rows, cols, [lanes_of(rim_mu, n, c) for c in range(5)])
        return carry

    lax.fori_loop(0, 2 * RIMS // CHUNK, back_step, 0)
    for c in range(5):
        blade_out[c] = blade_kept[c] + blade_acc[c * CHORD : (c + 1) * CHORD, :].T
        top = back_kept[c, HALF:, :] + back_acc[c * HALF : (c + 1) * HALF, :]
        parts = from_planes(jnp.concatenate([back_kept[c, :HALF, :], top], axis=0))
        for y in range(0, NORTH, 2):
            back_out[c, :, y * VERT : (y + 2) * VERT] = jnp.concatenate(parts[y : y + 2], axis=1)


VMEM = pl.BlockSpec(memory_space=pltpu.VMEM)
SMEM = pl.BlockSpec(memory_space=pltpu.SMEM)
BLADE = jax.ShapeDtypeStruct((5, WRAP * WALL, CHORD), F32)
PLANES = jax.ShapeDtypeStruct((5, VERT, DEVS), F32)
DONOR_PARTS = [
    pltpu.VMEM((5 * CHORD, 3 * WRAP * WALL), BF16),
    pltpu.VMEM((5 * HALF, 3 * DEVS), BF16),
]
SUMS = [pltpu.VMEM((5 * CHORD, WRAP * WALL), F32), pltpu.VMEM((5 * HALF, DEVS), F32)]


def run(kernel, args, out_shape, scratch=(), scalars=0, flops=0):
    size = sum(4 * a.size for a in args) + sum(4 * o.size for o in out_shape)
    return pl.pallas_call(
        kernel,
        out_shape=list(out_shape),
        in_specs=[SMEM] * scalars + [VMEM] * (len(args) - scalars),
        out_specs=[VMEM] * len(out_shape),
        scratch_shapes=list(scratch),
        cost_estimate=pl.CostEstimate(flops=flops, bytes_accessed=size, transcendentals=0),
    )(*args)


def swap(rows):
    return lax.all_to_all(rows, ("gx", "gy"), split_axis=0, concat_axis=0, tiled=True)


def body(
    blade_state,
    back_state,
    blade_cotangent,
    back_cotangent,
    blade_flux,
    back_flux,
    blade_owner,
    back_donor_cell,
    back_donor_weight,
    hole_cell,
    hole_owner,
    blade_donor_cell,
    blade_donor_weight,
):
    shape = jax.ShapeDtypeStruct
    blade = blade_state.reshape(5, WRAP * WALL, CHORD)
    cot = blade_cotangent.reshape(5, WRAP * WALL, CHORD)
    matrices = jnp.concatenate([blade_flux, back_flux]).reshape(6, 25)
    owners = (blade_owner.reshape(2, 1, RIMS), hole_owner.reshape(2, 1, HOLES))
    tables = (back_donor_cell, back_donor_weight, blade_donor_cell, blade_donor_weight)

    cot_planes, *edges = run(
        edge_kernel, (blade, cot, back_cotangent), [PLANES] + edge_shapes(2 * WALL)
    )
    cot_halo = exchange(edges)
    send, back_planes = run(
        start_kernel,
        (blade, back_state) + tables,
        [shape((DEVS, 2, DEVS), F32), PLANES],
        DONOR_PARTS + [pltpu.VMEM((5, QH, DEVS), F32), pltpu.VMEM((5, QR, DEVS), F32)],
        flops=5 * 10**9,
    )
    recv = swap(send)
    lin_send, blade_fields, back_fields, rim_rank, hole_rank = run(
        cot_kernel,
        (matrices, cot, cot_planes, *cot_halo, *owners, hole_cell),
        [
            shape((DEVS, 8, DEVS), F32),
            shape((FIELDS, WRAP * WALL, CHORD), F32),
            shape((FIELDS, VERT, DEVS), F32),
            shape((2, 1, RIMS), jnp.int32),
            shape((2, 1, HOLES), jnp.int32),
        ],
        scalars=1,
        flops=2 * 10**9,
    )
    lin_recv = swap(lin_send)
    slots = (*owners, rim_rank, hole_rank, hole_cell)
    blade_first, back_first, *edges = run(
        fill_kernel,
        (blade, back_planes, recv) + slots,
        [BLADE, PLANES] + edge_shapes(16),
        flops=10**9,
    )
    first_halo = exchange(edges)
    blade_mid, back_mid, *edges = run(
        middle_kernel,
        (matrices, blade_first, back_first, *cot_halo[:2], *first_halo, blade_fields, back_fields)
        + (lin_recv,)
        + tables
        + (hole_cell,),
        [BLADE, PLANES] + edge_shapes(WALL + 8),
        [pltpu.VMEM(BLADE.shape, F32), pltpu.VMEM(PLANES.shape, F32)]
        + DONOR_PARTS
        + [pltpu.VMEM((FIELDS, QH, DEVS), F32), pltpu.VMEM((FIELDS, QR, DEVS), F32)]
        + SUMS,
        scalars=1,
        flops=10**10,
    )
    mid_halo = exchange(edges)
    parts = run(
        inner_kernel,
        (matrices, blade_first, back_first, blade_mid, back_mid, hole_cell),
        [BLADE, PLANES, shape((HALF, DEVS), F32)],
        scalars=1,
        flops=10**9,
    )
    send, blade_kept, back_kept = run(
        last_kernel,
        (matrices, blade_first, back_first, *parts, *mid_halo) + slots,
        [shape((DEVS, 2, DEVS), F32), BLADE, PLANES],
        scalars=1,
        flops=10**9,
    )
    recv = swap(send)
    blade_last, back_last = run(
        end_kernel,
        (blade_kept, back_kept, recv) + tables,
        [BLADE, shape((5, EAST, NORTH * VERT), F32)],
        [pltpu.VMEM((5, QH, DEVS), F32), pltpu.VMEM((5, QR, DEVS), F32)] + SUMS,
        flops=5 * 10**9,
    )
    return (blade_last.reshape(blade_state.shape), back_last)


def solution(mesh):
    return jax.shard_map(
        body,
        mesh=mesh,
        in_specs=(
            P(None, "gx", "gy"),
            P(None, "gx", "gy"),
            P(None, "gx", "gy"),
            P(None, "gx", "gy"),
            P(),
            P(),
            P(None, ("gx", "gy"), None),
            P(None, ("gx", "gy")),
            P(None, None, ("gx", "gy")),
            P(None, ("gx", "gy")),
            P(None, ("gx", "gy"), None),
            P(None, ("gx", "gy")),
            P(None, None, ("gx", "gy")),
        ),
        out_specs=(P(None, "gx", "gy"), P(None, "gx", "gy")),
        check_vma=False,
    )
```

```python
import jax
import jax.numpy as jnp
from jax import lax
from jax.experimental import pallas as pl
from jax.experimental.pallas import tpu as pltpu
from jax.sharding import PartitionSpec as P


DEVS = 128
WRAP = 4
WALL = 64
CHORD = 128
EAST = 16
NORTH = 8
VERT = 64
HALF = VERT // 2
RIMS = 1024
HOLES = 2048
QR = 2 * RIMS // DEVS
QH = 2 * HOLES // DEVS
FIELDS = 17

time_step = 0.2
damping = 0.1

F32 = jnp.float32
BF16 = jnp.bfloat16


def split(x):
    hi = x.astype(BF16)
    return hi, (x - hi.astype(F32)).astype(BF16)


def dot_nn(a, b):
    return lax.dot_general(a, b, (((1,), (0,)), ((), ())), preferred_element_type=F32)


def dot_nt(a, b):
    return lax.dot_general(a, b, (((1,), (1,)), ((), ())), preferred_element_type=F32)


def iota(shape, dim):
    return lax.broadcasted_iota(jnp.int32, shape, dim)


def one_hot(rows, index):
    return jnp.where(iota((rows, index.shape[1]), 0) == index, 1.0, 0.0)


def pair_hot(rows, index, first, second):
    position = iota((rows, index.shape[1]), 0)
    return jnp.where(position == index, first, jnp.where(position == index + 1, second, 0.0))


def lane_roll(x, amount):
    amount = amount % x.shape[-1]
    return pltpu.roll(x, amount, x.ndim - 1) if amount else x


def to_planes(block):
    rows = [block[:, y * VERT : (y + 1) * VERT] for y in range(NORTH)]
    return jnp.concatenate(rows, axis=0).T


def from_planes(field):
    turned = field.T
    return [turned[y * EAST : (y + 1) * EAST, :] for y in range(NORTH)]


def donor_parts(weights):
    w = [weights[corner : corner + 1, :] for corner in range(8)]
    x0 = (w[0] + w[1]) + (w[2] + w[3])
    x1 = (w[4] + w[5]) + (w[6] + w[7])
    y0 = (w[0] + w[1]) + (w[4] + w[5])
    y1 = (w[2] + w[3]) + (w[6] + w[7])
    z0 = (w[0] + w[2]) + (w[4] + w[6])
    z1 = (w[1] + w[3]) + (w[5] + w[7])
    return x0, x1, y0, y1, z0, z1


def short_marks(size, index):
    position = iota((size, index.shape[1]), 0).astype(jnp.int16)
    return position == index.astype(jnp.int16), position == (index + 1).astype(jnp.int16)


def pair_split(marks, first, second):
    (first_hi, first_lo), (second_hi, second_lo) = split(first), split(second)
    zero = jnp.zeros((), BF16)

    def place(a, b):
        return jnp.where(marks[0], a, jnp.where(marks[1], b, zero))

    return place(first_hi, second_hi), place(first_lo, second_lo)


def donor_rows(outer, outer_index, outer_pair, inner, inner_index, inner_pair):
    hot = pair_hot(outer, outer_index, *outer_pair)
    marks = short_marks(inner, inner_index)
    parts = [
        pair_split(marks, hot[n : n + 1, :] * inner_pair[0], hot[n : n + 1, :] * inner_pair[1])
        for n in range(outer)
    ]
    return tuple(jnp.concatenate([p[k] for p in parts], axis=0) for k in range(2))


def blade_donors(base, weights):
    x0, x1, y0, y1, z0, z1 = donor_parts(weights)
    wall = (base >> 7) & (WALL - 1)
    rows = donor_rows(WRAP, base >> 13, (x0, x1), WALL, wall, (y0, y1))
    return rows, (CHORD, base & (CHORD - 1), z0, z1)


def back_donors(base, weights):
    x0, x1, y0, y1, z0, z1 = donor_parts(weights)
    north = (base >> 6) & (NORTH - 1)
    rows = donor_rows(NORTH, north, (y0, y1), EAST, base >> 9, (x0, x1))
    return rows, (HALF, (base & (VERT - 1)) - HALF, z0, z1)


def triple_rows(rows):
    hi, lo = rows
    return jnp.concatenate([hi, lo, hi], axis=0)


def triple_lanes(rows):
    hi, lo = rows
    return jnp.concatenate([hi, hi, lo], axis=1)


def store_parts(target, place, size, field):
    hi, lo = split(field)
    rows = slice(place, place + size)
    target[rows, :] = jnp.concatenate([hi, hi, lo], axis=1)


def picked(parts, rows, cols):
    size = cols[0]
    hot = pair_hot(*cols)
    table = dot_nn(parts[...], triple_rows(rows))
    return [
        jnp.sum(table[c * size : (c + 1) * size] * hot, axis=0, keepdims=True) for c in range(5)
    ]


def spread_terms(rows, cols, mu):
    size, index, first, second = cols
    pairs = [(first * mu[c], second * mu[c]) for c in range(5)]
    tiles = {c: [] for c in range(5)}
    for start in range(0, size, 16):
        marks = short_marks(16, index - start)
        for c in range(5):
            tiles[c].append(pair_split(marks, *pairs[c]))
    hi, lo = (
        jnp.concatenate([t[k] for c in range(5) for t in tiles[c]], axis=0) for k in range(2)
    )
    return dot_nt(jnp.concatenate([hi, lo, hi], axis=1), triple_lanes(rows))


def doubled(field):
    hi, lo = split(field)
    return jnp.concatenate([hi, lo], axis=1)


def twice(marks):
    return jnp.concatenate([marks, marks], axis=0)


def wall_shift(v, up):
    position = iota(v.shape, 0)
    if up:
        return jnp.where(position == v.shape[0] - 1, 0.0, pltpu.roll(v, v.shape[0] - 1, 0))
    return jnp.where(position == 0, 0.0, pltpu.roll(v, 1, 0))


def lane_shift(v, up, width, period, fill):
    place = (iota(v.shape, 1) // width) % period
    if up:
        return jnp.where(place == period - 1, fill, lane_roll(v, -width))
    return jnp.where(place == 0, fill, lane_roll(v, width))


class Matrices:
    def __init__(self, ref, start):
        self.ref, self.start = ref, start

    def __getitem__(self, place):
        return self.ref[self.start + place[0], place[1]]


def flux_of(m_ref, t, v, scaled):
    out = []
    for c in range(5):
        total = v[1 + t] * scaled[c]
        for e in range(5):
            total = total + m_ref[t, c * 5 + e] * scaled[e]
        out.append(total)
    return out


def turned_of(m_ref, t, w):
    out = []
    for c in range(5):
        total = m_ref[t, c] * w[0]
        for e in range(1, 5):
            total = total + m_ref[t, e * 5 + c] * w[e]
        out.append(total)
    return out


PAIRS = [(0, 1), (0, 2), (0, 3), (4, 1), (4, 2), (4, 3), (1, 1), (1, 2), (1, 3), (2, 2), (2, 3), (3, 3)]


def linear_fields(m_ref, center, sides):
    base = [center[c] * (1.0 - 6.0 * damping * time_step) for c in range(5)]
    jumps = []
    for t, (upper, lower) in enumerate(sides):
        jump = [0.5 * time_step * (lower[c] - upper[c]) for c in range(5)]
        turned = turned_of(m_ref, t, jump)
        for c in range(5):
            base[c] = base[c] - turned[c] + damping * time_step * (upper[c] + lower[c])
        jumps.append(jump)
    out = list(base)
    for a, b in PAIRS:
        if a in (0, 4):
            out.append(jumps[b - 1][a])
        else:
            out.append(jumps[a - 1][b] + jumps[b - 1][a])
    return out


def apply_fields(fields, v):
    out = []
    table = {pair: 5 + n for n, pair in enumerate(PAIRS)}
    for c in range(5):
        total = fields[c]
        for e in range(5):
            key = (c, e) if (c, e) in table else (e, c)
            if key in table:
                total = total - fields[table[key]] * v[e]
        out.append(total)
    return out


def adjoint_at(m_ref, v, center, sides):
    out = [center[c] * (1.0 - 6.0 * damping * time_step) for c in range(5)]
    for t, (upper, lower) in enumerate(sides):
        jump = [0.5 * time_step * (lower[c] - upper[c]) for c in range(5)]
        turned = turned_of(m_ref, t, jump)
        inner = v[0] * jump[0]
        for e in range(1, 5):
            inner = inner + v[e] * jump[e]
        for c in range(5):
            total = turned[c] + v[1 + t] * jump[c]
            if c == 1 + t:
                total = total + inner
            out[c] = out[c] - total + damping * time_step * (upper[c] + lower[c])
    return out


def blade_sides(ref, low, high, j):
    def plane(n):
        if n < 0 or n >= WRAP:
            return low if n < 0 else high
        return [ref[c, n * WALL : (n + 1) * WALL, :] for c in range(5)]

    center, above, below = plane(j), plane(j + 1), plane(j - 1)
    wall = ([wall_shift(v, True) for v in center], [wall_shift(v, False) for v in center])
    span = (
        [lane_shift(v, True, 1, CHORD, 0.0) for v in center],
        [lane_shift(v, False, 1, CHORD, 0.0) for v in center],
    )
    return center, [(above, below), wall, span]


def back_sides(center, halo):
    east = (
        [lane_shift(v, True, 1, EAST, halo[1][c]) for c, v in enumerate(center)],
        [lane_shift(v, False, 1, EAST, halo[0][c]) for c, v in enumerate(center)],
    )
    north = (
        [lane_shift(v, True, EAST, NORTH, halo[3][c]) for c, v in enumerate(center)],
        [lane_shift(v, False, EAST, NORTH, halo[2][c]) for c, v in enumerate(center)],
    )
    vert = ([wall_shift(v, True) for v in center], [wall_shift(v, False) for v in center])
    return [east, north, vert]


def pack_east(v, x):
    lane = iota((8, DEVS), 1)
    out = jnp.zeros((8, DEVS), F32)
    for g in range(8):
        out = jnp.where(lane % EAST == g, lane_roll(v[g * 8 : g * 8 + 8, :], g - x), out)
    return out


def unpack_east(v, x):
    return jnp.concatenate([lane_roll(v, x - g) for g in range(8)], axis=0)


def pack_north(v, y):
    lane = iota((8, DEVS), 1)
    out = jnp.zeros((8, DEVS), F32)
    for g in range(8):
        out = jnp.where(lane // EAST == g, lane_roll(v[g * 8 : g * 8 + 8, :], (g - y) * EAST), out)
    return out


def unpack_north(v, y):
    return jnp.concatenate([lane_roll(v, (y - g) * EAST) for g in range(8)], axis=0)


def store_blade_edges(planes, rows, edges, at=0):
    even_y = lax.axis_index("gy") % 2 == 0
    first_y, second_y = edges
    count = rows.stop - rows.start
    for c in range(5):
        low, high = (plane[c, rows, :] for plane in planes)
        first_y[c, at : at + count, :] = jnp.where(even_y, high, low)
        second_y[c, at : at + count, :] = jnp.where(even_y, low, high)


def store_back_edges(back, edges, at):
    first_y, second_y, first_x, second_x = edges
    even_y = lax.axis_index("gy") % 2 == 0
    even_x = lax.axis_index("gx") % 2 == 0
    for c in range(5):
        high, low = pack_north(back[c], NORTH - 1), pack_north(back[c], 0)
        first_y[c, at : at + 8, :] = jnp.where(even_y, high, low)
        second_y[c, at : at + 8, :] = jnp.where(even_y, low, high)
        high, low = pack_east(back[c], EAST - 1), pack_east(back[c], 0)
        first_x[c] = jnp.where(even_x, high, low)
        second_x[c] = jnp.where(even_x, low, high)


def edge_shapes(rows):
    ends = jax.ShapeDtypeStruct((5, rows, CHORD), F32)
    sides = jax.ShapeDtypeStruct((5, 8, DEVS), F32)
    return [ends, ends, sides, sides]


def read_ends(first_y, second_y, rows):
    even_y = lax.axis_index("gy") % 2 == 0
    both = [(first_y[c, rows, :], second_y[c, rows, :]) for c in range(5)]
    return [jnp.where(even_y, b, a) for a, b in both], [jnp.where(even_y, a, b) for a, b in both]


def read_back(first_y, second_y, first_x, second_x, at):
    north = lax.axis_index("gy")
    even_x = lax.axis_index("gx") % 2 == 0
    keep_low = jnp.where(north > 0, 1.0, 0.0)
    keep_high = jnp.where(north < DEVS // 8 - 1, 1.0, 0.0)
    below, above = read_ends(first_y, second_y, slice(at, at + 8))
    both = [(first_x[c], second_x[c]) for c in range(5)]
    east = [unpack_east(jnp.where(even_x, a, b), EAST - 1) for a, b in both]
    west = [unpack_east(jnp.where(even_x, b, a), 0) for a, b in both]
    south = [unpack_north(v * keep_low, 0) for v in below]
    upper = [unpack_north(v * keep_high, NORTH - 1) for v in above]
    return [west, east, south, upper]


def exchange(edges):
    gx, gy = lax.axis_size("gx"), lax.axis_size("gy")

    def pairs(start, stop, count):
        there = [(i, (i + 1) % count) for i in range(start, stop, 2)]
        return there + [(b, a) for a, b in there]

    first_y, second_y, first_x, second_x = edges
    got_y = lax.ppermute(first_y, "gy", pairs(0, gy, gy))
    got_x = lax.ppermute(first_x, "gx", pairs(0, gx, gx))
    got_x2 = lax.ppermute(second_x, "gx", pairs(1, gx - 1, gx))
    got_y2 = lax.ppermute(second_y, "gy", pairs(1, gy, gy))
    return got_y, got_y2, got_x, got_x2


def regroup(pieces, width):
    count = DEVS // width
    shape = next(piece.shape for piece in pieces if piece is not None)
    block = iota(shape, 1) // width
    out = []
    for b in range(count):
        total = jnp.zeros(shape, F32)
        for a in range(count):
            if pieces[a] is not None:
                total = jnp.where(block == a, lane_roll(pieces[a], (a - b) * width), total)
        out.append(total)
    return out


def ranks_of(owner_ref, out_ref):
    count = owner_ref.shape[1]
    earlier = jnp.where(iota((256, 256), 0) < iota((256, 256), 1), 1.0, 0.0).astype(BF16)
    carry = jnp.zeros((DEVS, 1), F32)
    for start in range(0, count, 256):
        marks = one_hot(DEVS, owner_ref[:, start : start + 256])
        before = dot_nn(marks.astype(BF16), earlier) + carry
        out_ref[:, start : start + 256] = jnp.sum(marks * before, axis=0, keepdims=True).astype(
            jnp.int32
        )
        carry = carry + jnp.sum(marks, axis=1, keepdims=True)


def seat_terms(slots, index, values):
    here = iota((slots, index.shape[1]), 0).astype(jnp.int16) == index.astype(jnp.int16)
    zero = jnp.zeros((), BF16)
    parts = [[jnp.where(here, part, zero) for part in split(v)] for v in values]
    hi, lo = (jnp.concatenate([p[k] for p in parts], axis=0) for k in range(2))
    return jnp.concatenate([hi, lo], axis=1)


def send_rows(values, owner, rank, slots):
    marks = one_hot(DEVS, owner).astype(BF16)
    return dot_nt(seat_terms(slots, rank, values), jnp.concatenate([marks, marks], axis=1))


def hole_parts(cell):
    row = ((cell >> 6) & (NORTH - 1)) * EAST + (cell >> 9)
    return row, cell & (VERT - 1)


def hole_values(low_half, cell):
    row, vert = hole_parts(cell)
    seats = one_hot(HALF, vert)
    table = dot_nn(low_half, twice(one_hot(DEVS, row).astype(BF16)))
    return [
        jnp.sum(table[n : n + HALF] * seats, axis=0, keepdims=True)
        for n in range(0, table.shape[0], HALF)
    ]


def hole_mask(cell_ref):
    total = jnp.zeros((HALF, DEVS), F32)
    for start in range(0, HOLES, 512):
        row, vert = hole_parts(cell_ref[:, start : start + 512])
        total = total + dot_nt(one_hot(HALF, vert).astype(BF16), one_hot(DEVS, row).astype(BF16))
    return total


CHUNK = 512


def chunk_lanes(n):
    return pl.ds(pl.multiple_of(n * CHUNK, CHUNK), CHUNK)


def lanes_of(ref, n, k):
    count = CHUNK // DEVS
    return jnp.concatenate([ref[k, pl.ds(n * count + m, 1), :] for m in range(count)], axis=1)


def store_chunk(out, n, values):
    for c in range(5):
        for m in range(CHUNK // DEVS):
            row = pl.ds(n * (CHUNK // DEVS) + m, 1)
            out[c, row, :] = values[c][:, m * DEVS : (m + 1) * DEVS]


def outer_planes(ref):
    return ref.at[:, :WALL, :], ref.at[:, (WRAP - 1) * WALL :, :]


def edge_kernel(
    blade_low, blade_high, cot_low, cot_high, back_cot,
    cot_planes, first_y, second_y, first_x, second_x,
):
    cots = []
    for c in range(5):
        turned = to_planes(back_cot[c])
        cot_planes[c] = turned
        cots.append(turned)
    store_blade_edges((cot_low, cot_high), slice(0, WALL), (first_y, second_y))
    store_blade_edges((blade_low, blade_high), slice(0, WALL - 8), (first_y, second_y), WALL + 8)
    store_back_edges(cots, (first_y, second_y, first_x, second_x), WALL)


def start_kernel(
    blade, back, back_base, back_weight, blade_base, blade_weight,
    send, back_planes,
    blade_parts, back_parts, hole_vals, rim_vals,
):
    for c in range(5):
        store_parts(blade_parts, c * CHORD, CHORD, blade[c].T)
        field = to_planes(back[c])
        back_planes[c] = field
        store_parts(back_parts, c * HALF, HALF, field[HALF:, :])

    def blade_step(n, carry):
        lanes = chunk_lanes(n)
        rows, cols = blade_donors(blade_base[0:1, lanes], blade_weight[0, :, lanes])
        store_chunk(hole_vals, n, picked(blade_parts, rows, cols))
        return carry

    lax.fori_loop(0, 2 * HOLES // CHUNK, blade_step, 0, unroll=4)

    def back_step(n, carry):
        lanes = chunk_lanes(n)
        rows, cols = back_donors(back_base[0:1, lanes], back_weight[0, :, lanes])
        store_chunk(rim_vals, n, picked(back_parts, rows, cols))
        return carry

    lax.fori_loop(0, 2 * RIMS // CHUNK, back_step, 0)
    store_slots(hole_vals, rim_vals, send)


def store_slots(hole_vals, rim_vals, send):
    first = regroup([hole_vals[c] for c in range(4)], QH)
    fifth = hole_vals[4]
    tail = regroup([fifth, None, None, None], QH)
    for d in range(DEVS // QH):
        send[pl.ds(d, QH, stride=DEVS // QH), 0, :] = first[d]
        send[pl.ds(d, QH, stride=DEVS // QH), 1, :] = tail[d]
    rims = regroup([None, None] + [rim_vals[c] for c in range(5)] + [None], QR)
    lane = iota((QR, DEVS), 1)
    for d in range(DEVS // QR):
        rows = pl.ds(d, QR, stride=DEVS // QR)
        send[rows, 1, :] = jnp.where(lane < QH, send[rows, 1, :], rims[d])


def cot_kernel(
    matrices, cot, cot_planes, got_y, got_y2, got_x, got_x2, rim_owner, hole_owner, hole_cell,
    send, blade_fields, back_fields, rim_rank, hole_rank,
):
    blade_m, back_m = Matrices(matrices, 0), Matrices(matrices, 3)
    low, high = read_ends(got_y, got_y2, slice(0, WALL))
    halo = read_back(got_y, got_y2, got_x, got_x2, WALL)
    for j in range(WRAP):
        center, sides = blade_sides(cot, low, high, j)
        fields = linear_fields(blade_m, center, sides)
        for n in range(FIELDS):
            blade_fields[n, j * WALL : (j + 1) * WALL, :] = fields[n]
    center = [cot_planes[c] for c in range(5)]
    fields = linear_fields(back_m, center, back_sides(center, halo))
    for n in range(FIELDS):
        back_fields[n] = fields[n]
    for step in range(2):
        ranks_of(rim_owner.at[step], rim_rank.at[step])
        ranks_of(hole_owner.at[step], hole_rank.at[step])

    total = jnp.zeros((FIELDS * QR, DEVS), F32)
    for j in range(WRAP):
        lanes = slice(j * 256, j * 256 + 256)
        top = j * WALL + WALL - 2
        values = [
            jnp.concatenate(
                [blade_fields[n, top + k : top + k + 1, :] for k in range(2)], axis=1
            )
            for n in range(FIELDS)
        ]
        total = total + send_rows(values, rim_owner[1, :, lanes], rim_rank[1, :, lanes], QR)
    total = jnp.concatenate([total, jnp.zeros((112, DEVS), F32)], axis=0)
    for m in range(3):
        send[:, 5 + m, :] = total[m * DEVS : (m + 1) * DEVS].T
    total = jnp.zeros((FIELDS * QH, DEVS), F32)
    low_half = doubled(jnp.concatenate([back_fields[n, :HALF, :] for n in range(FIELDS)], axis=0))
    for start in range(0, HOLES, 512):
        lanes = slice(start, start + 512)
        values = hole_values(low_half, hole_cell[1:2, lanes])
        total = total + send_rows(values, hole_owner[1, :, lanes], hole_rank[1, :, lanes], QH)
    total = jnp.concatenate([total, jnp.zeros((96, DEVS), F32)], axis=0)
    for m in range(5):
        send[:, m, :] = total[m * DEVS : (m + 1) * DEVS].T


def fill_kernel(
    blade, back_planes, recv, rim_owner, hole_owner, rim_rank, hole_rank, hole_cell,
    blade_first, back_first, first_y, second_y, first_x, second_x,
):
    arrived = doubled(jnp.concatenate([recv[:, 0, :].T, recv[:, 1, :].T], axis=0))
    for c in range(5):
        for j in range(WRAP):
            rows = slice(j * WALL, (j + 1) * WALL)
            blade_first[c, rows, :] = blade[c, rows, :]
    base = 5 * QH
    for j in range(WRAP):
        lanes = slice(j * 256, j * 256 + 256)
        marks = one_hot(DEVS, rim_owner[0, :, lanes]).astype(BF16)
        seats = one_hot(QR, rim_rank[0, :, lanes])
        table = dot_nn(arrived[base : base + 5 * QR], twice(marks))
        for c in range(5):
            value = jnp.sum(table[c * QR : (c + 1) * QR] * seats, axis=0, keepdims=True)
            for k in range(2):
                row = j * WALL + WALL - 2 + k
                blade_first[c, row : row + 1, :] = value[:, k * CHORD : (k + 1) * CHORD]
    filled = jnp.zeros((6 * HALF, DEVS), F32)
    for start in range(0, HOLES, 512):
        lanes = slice(start, start + 512)
        marks = one_hot(DEVS, hole_owner[0, :, lanes]).astype(BF16)
        seats = one_hot(QH, hole_rank[0, :, lanes])
        row, vert = hole_parts(hole_cell[0:1, lanes])
        table = dot_nn(arrived[:base], twice(marks))
        values = [
            jnp.sum(table[c * QH : (c + 1) * QH] * seats, axis=0, keepdims=True) for c in range(5)
        ]
        terms = seat_terms(HALF, vert, values + [jnp.ones(vert.shape, F32)])
        row_marks = one_hot(DEVS, row).astype(BF16)
        filled = filled + dot_nt(terms, jnp.concatenate([row_marks, row_marks], axis=1))
    mask = filled[5 * HALF :]
    backs = []
    for c in range(5):
        top = jnp.where(mask > 0.5, filled[c * HALF : (c + 1) * HALF], back_planes[c, :HALF, :])
        field = jnp.concatenate([top, back_planes[c, HALF:, :]], axis=0)
        back_first[c] = field
        backs.append(field)
    store_blade_edges(outer_planes(blade_first), slice(WALL - 8, WALL), (first_y, second_y))
    store_back_edges(backs, (first_y, second_y, first_x, second_x), 8)


def residual_step(center, halo_flux):
    out = [center[c] * (1.0 - 6.0 * damping * time_step) for c in range(5)]
    for t in range(3):
        upper, lower = halo_flux(t)
        for c in range(5):
            out[c] = out[c] - upper[c] + lower[c]
    return out


def side_terms(m_ref, t, v):
    flux = flux_of(m_ref, t, v, [0.5 * time_step * v[c] for c in range(5)])
    damped = [damping * time_step * v[c] for c in range(5)]
    upper = [flux[c] - damped[c] for c in range(5)]
    lower = [flux[c] + damped[c] for c in range(5)]
    return upper, lower


def middle_kernel(
    matrices, blade_first, back_first, old_y, old_y2, got_y, got_y2, got_x, got_x2,
    blade_fields, back_fields, recv, back_base, back_weight, blade_base, blade_weight, hole_cell,
    blade_mid, back_mid, first_y, second_y, first_x, second_x,
    blade_next, back_next, blade_parts, back_parts, hole_lin, rim_lin, blade_acc, back_acc,
):
    blade_m, back_m = Matrices(matrices, 0), Matrices(matrices, 3)
    planes = zip(
        read_ends(old_y, old_y2, slice(WALL + 8, 2 * WALL)), read_ends(got_y, got_y2, slice(0, 8))
    )
    low, high = (
        [jnp.concatenate([a, b], axis=0) for a, b in zip(inner, outer)] for inner, outer in planes
    )
    halo = read_back(got_y, got_y2, got_x, got_x2, 8)

    sections = [low]
    for j in range(WRAP):
        sections.append([blade_first[c, j * WALL : (j + 1) * WALL, :] for c in range(5)])
    sections.append(high)
    turns = [side_terms(blade_m, 0, plane) for plane in sections]
    for j in range(WRAP):
        center = sections[j + 1]

        def around(t, j=j, center=center):
            if t == 0:
                return turns[j + 2][0], turns[j][1]
            upper, lower = side_terms(blade_m, t, center)
            if t == 1:
                return [wall_shift(v, True) for v in upper], [wall_shift(v, False) for v in lower]
            return (
                [lane_shift(v, True, 1, CHORD, 0.0) for v in upper],
                [lane_shift(v, False, 1, CHORD, 0.0) for v in lower],
            )

        out = residual_step(center, around)
        for c in range(5):
            blade_next[c, j * WALL : (j + 1) * WALL, :] = out[c]
    center = [back_first[c] for c in range(5)]

    def across(t):
        upper, lower = side_terms(back_m, t, center)
        if t == 2:
            return [wall_shift(v, True) for v in upper], [wall_shift(v, False) for v in lower]
        width, period = ((1, EAST), (EAST, NORTH))[t]
        below = side_terms(back_m, t, halo[2 * t])[1]
        above = side_terms(back_m, t, halo[2 * t + 1])[0]
        return (
            [lane_shift(upper[c], True, width, period, above[c]) for c in range(5)],
            [lane_shift(lower[c], False, width, period, below[c]) for c in range(5)],
        )

    out = residual_step(center, across)
    for c in range(5):
        back_next[c] = out[c]
        store_parts(back_parts, c * HALF, HALF, out[c][HALF:, :])
        store_parts(blade_parts, c * CHORD, CHORD, blade_next[c].T)

    for j in range(WRAP):
        rows = slice(j * WALL, (j + 1) * WALL)
        v = [blade_next[c, rows, :] for c in range(5)]
        own = apply_fields([blade_fields[n, rows, :] for n in range(FIELDS)], v)
        inside = iota((WALL, CHORD), 0) < WALL - 2
        for c in range(5):
            blade_mid[c, rows, :] = jnp.where(inside, own[c], 0.0)
    mask = hole_mask(hole_cell.at[1:2])
    own = apply_fields([back_fields[n] for n in range(FIELDS)], [back_next[c] for c in range(5)])
    for c in range(5):
        back_mid[c, :HALF, :] = jnp.where(mask > 0.5, 0.0, own[c][:HALF, :])
        back_mid[c, HALF:, :] = own[c][HALF:, :]

    for m in range(5):
        pieces = [recv[pl.ds(d, QH, stride=DEVS // QH), m, :] for d in range(DEVS // QH)]
        for b, piece in enumerate(regroup(pieces, QH)):
            if m * 4 + b < FIELDS:
                hole_lin[m * 4 + b] = piece
    for m in range(3):
        pieces = [recv[pl.ds(d, QR, stride=DEVS // QR), 5 + m, :] for d in range(DEVS // QR)]
        for b, piece in enumerate(regroup(pieces, QR)):
            if m * 8 + b < FIELDS:
                rim_lin[m * 8 + b] = piece

    blade_acc[...] = jnp.zeros(blade_acc.shape, F32)
    back_acc[...] = jnp.zeros(back_acc.shape, F32)

    def blade_step(n, carry):
        lanes = chunk_lanes(n)
        rows, cols = blade_donors(blade_base[1:2, lanes], blade_weight[1, :, lanes])
        value = picked(blade_parts, rows, cols)
        mu = apply_fields([lanes_of(hole_lin, n, k) for k in range(FIELDS)], value)
        blade_acc[...] += spread_terms(rows, cols, mu)
        return carry

    lax.fori_loop(0, 2 * HOLES // CHUNK, blade_step, 0, unroll=4)

    def back_step(n, carry):
        lanes = chunk_lanes(n)
        rows, cols = back_donors(back_base[1:2, lanes], back_weight[1, :, lanes])
        value = picked(back_parts, rows, cols)
        mu = apply_fields([lanes_of(rim_lin, n, k) for k in range(FIELDS)], value)
        back_acc[...] += spread_terms(rows, cols, mu)
        return carry

    lax.fori_loop(0, 2 * RIMS // CHUNK, back_step, 0)
    for c in range(5):
        blade_mid[c] = blade_mid[c] + blade_acc[c * CHORD : (c + 1) * CHORD, :].T
        back_mid[c, HALF:, :] = back_mid[c, HALF:, :] + back_acc[c * HALF : (c + 1) * HALF, :]
    store_blade_edges(outer_planes(blade_mid), slice(0, WALL), (first_y, second_y))
    store_back_edges(
        [back_mid[c] for c in range(5)], (first_y, second_y, first_x, second_x), WALL
    )


def inner_kernel(
    matrices, blade_first, back_first, blade_mid, back_mid, hole_cell, blade_part, back_part, mask
):
    blade_m, back_m = Matrices(matrices, 0), Matrices(matrices, 3)
    nothing = [jnp.zeros((WALL, CHORD), F32)] * 5
    for j in range(WRAP):
        rows = slice(j * WALL, (j + 1) * WALL)
        center, sides = blade_sides(blade_mid, nothing, nothing, j)
        out = adjoint_at(blade_m, [blade_first[c, rows, :] for c in range(5)], center, sides)
        for c in range(5):
            blade_part[c, rows, :] = out[c]
    nothing = [jnp.zeros((VERT, DEVS), F32)] * 5
    center = [back_mid[c] for c in range(5)]
    sides = back_sides(center, [nothing] * 4)
    out = adjoint_at(back_m, [back_first[c] for c in range(5)], center, sides)
    for c in range(5):
        back_part[c] = out[c]
    mask[...] = hole_mask(hole_cell.at[0:1])


def outside_terms(m_ref, t, v, beyond, sign):
    jump = [-sign * 0.5 * time_step * beyond[c] for c in range(5)]
    turned = turned_of(m_ref, t, jump)
    inner = v[0] * jump[0]
    for e in range(1, 5):
        inner = inner + v[e] * jump[e]
    out = []
    for c in range(5):
        total = turned[c] + v[1 + t] * jump[c]
        if c == 1 + t:
            total = total + inner
        out.append(damping * time_step * beyond[c] - total)
    return out


def last_kernel(
    matrices, blade_first, back_first, blade_part, back_part, mask,
    got_y, got_y2, got_x, got_x2,
    rim_owner, hole_owner, rim_rank, hole_rank, hole_cell,
    send, blade_kept, back_kept,
):
    blade_m, back_m = Matrices(matrices, 0), Matrices(matrices, 3)
    low, high = read_ends(got_y, got_y2, slice(0, WALL))
    halo = read_back(got_y, got_y2, got_x, got_x2, WALL)
    rims = jnp.zeros((5 * QR, DEVS), F32)
    for j in range(WRAP):
        rows = slice(j * WALL, (j + 1) * WALL)
        out = [blade_part[c, rows, :] for c in range(5)]
        if j in (0, WRAP - 1):
            v = [blade_first[c, rows, :] for c in range(5)]
            beyond, sign = (high, 1.0) if j else (low, -1.0)
            more = outside_terms(blade_m, 0, v, beyond, sign)
            out = [out[c] + more[c] for c in range(5)]
        inside = iota((WALL, CHORD), 0) < WALL - 2
        values = []
        for c in range(5):
            blade_kept[c, rows, :] = jnp.where(inside, out[c], 0.0)
            outer = [out[c][WALL - 2 + k : WALL - 1 + k, :] for k in range(2)]
            values.append(jnp.concatenate(outer, axis=1))
        lanes = slice(j * 256, j * 256 + 256)
        rims = rims + send_rows(values, rim_owner[0, :, lanes], rim_rank[0, :, lanes], QR)
    v = [back_first[c] for c in range(5)]
    out = [back_part[c] for c in range(5)]
    place = iota((VERT, DEVS), 1)
    east, north = place % EAST, place // EAST
    for t, beyond, sign, at in (
        (0, halo[0], -1.0, east == 0),
        (0, halo[1], 1.0, east == EAST - 1),
        (1, halo[2], -1.0, north == 0),
        (1, halo[3], 1.0, north == NORTH - 1),
    ):
        more = outside_terms(back_m, t, v, [jnp.where(at, x, 0.0) for x in beyond], sign)
        out = [out[c] + more[c] for c in range(5)]
    holes_here = mask[...] > 0.5
    for c in range(5):
        back_kept[c, :HALF, :] = jnp.where(holes_here, 0.0, out[c][:HALF, :])
        back_kept[c, HALF:, :] = out[c][HALF:, :]
    holes = jnp.zeros((5 * QH, DEVS), F32)
    low_half = doubled(jnp.concatenate([out[c][:HALF, :] for c in range(5)], axis=0))
    for start in range(0, HOLES, 512):
        lanes = slice(start, start + 512)
        values = hole_values(low_half, hole_cell[0:1, lanes])
        holes = holes + send_rows(values, hole_owner[0, :, lanes], hole_rank[0, :, lanes], QH)
    rest = jnp.zeros((2 * DEVS - 5 * QH - 5 * QR, DEVS), F32)
    total = jnp.concatenate([holes, rims, rest], axis=0)
    send[:, 0, :] = total[:DEVS].T
    send[:, 1, :] = total[DEVS:].T


def end_kernel(
    blade_kept, back_kept, recv, back_base, back_weight, blade_base, blade_weight,
    blade_out, back_out, hole_mu, rim_mu, blade_acc, back_acc,
):
    count = DEVS // QH
    pieces = [recv[pl.ds(d, QH, stride=count), 0, :] for d in range(count)]
    for c, piece in enumerate(regroup(pieces, QH)):
        hole_mu[c] = piece
    pieces = [recv[pl.ds(d, QH, stride=count), 1, :] for d in range(count)]
    hole_mu[4] = regroup(pieces, QH)[0]
    count = DEVS // QR
    pieces = [recv[pl.ds(d, QR, stride=count), 1, :] for d in range(count)]
    groups = regroup(pieces, QR)
    for c in range(5):
        rim_mu[c] = groups[QH // QR + c]
    blade_acc[...] = jnp.zeros(blade_acc.shape, F32)
    back_acc[...] = jnp.zeros(back_acc.shape, F32)

    def blade_step(n, carry):
        lanes = chunk_lanes(n)
        rows, cols = blade_donors(blade_base[0:1, lanes], blade_weight[0, :, lanes])
        blade_acc[...] += spread_terms(rows, cols, [lanes_of(hole_mu, n, c) for c in range(5)])
        return carry

    lax.fori_loop(0, 2 * HOLES // CHUNK, blade_step, 0, unroll=4)

    def back_step(n, carry):
        lanes = chunk_lanes(n)
        rows, cols = back_donors(back_base[0:1, lanes], back_weight[0, :, lanes])
        back_acc[...] += spread_terms(rows, cols, [lanes_of(rim_mu, n, c) for c in range(5)])
        return carry

    lax.fori_loop(0, 2 * RIMS // CHUNK, back_step, 0)
    for c in range(5):
        blade_out[c] = blade_kept[c] + blade_acc[c * CHORD : (c + 1) * CHORD, :].T
        top = back_kept[c, HALF:, :] + back_acc[c * HALF : (c + 1) * HALF, :]
        parts = from_planes(jnp.concatenate([back_kept[c, :HALF, :], top], axis=0))
        for y in range(0, NORTH, 2):
            back_out[c, :, y * VERT : (y + 2) * VERT] = jnp.concatenate(parts[y : y + 2], axis=1)


VMEM = pl.BlockSpec(memory_space=pltpu.VMEM)
SMEM = pl.BlockSpec(memory_space=pltpu.SMEM)
BLADE = jax.ShapeDtypeStruct((5, WRAP * WALL, CHORD), F32)
PLANES = jax.ShapeDtypeStruct((5, VERT, DEVS), F32)
DONOR_PARTS = [
    pltpu.VMEM((5 * CHORD, 3 * WRAP * WALL), BF16),
    pltpu.VMEM((5 * HALF, 3 * DEVS), BF16),
]
SUMS = [pltpu.VMEM((5 * CHORD, WRAP * WALL), F32), pltpu.VMEM((5 * HALF, DEVS), F32)]


def plane_block(j):
    return pl.BlockSpec((5, WALL, CHORD), lambda _: (0, j, 0))


def run(kernel, args, out_shape, scratch=(), scalars=0, flops=0, blocks=None):
    size = sum(4 * a.size for a in args) + sum(4 * o.size for o in out_shape)
    return pl.pallas_call(
        kernel,
        grid=(1,) if blocks else (),
        out_shape=list(out_shape),
        in_specs=blocks or [SMEM] * scalars + [VMEM] * (len(args) - scalars),
        out_specs=[VMEM] * len(out_shape),
        scratch_shapes=list(scratch),
        cost_estimate=pl.CostEstimate(flops=flops, bytes_accessed=size, transcendentals=0),
    )(*args)


def swap(rows):
    return lax.all_to_all(rows, ("gx", "gy"), split_axis=0, concat_axis=0, tiled=True)


def body(
    blade_state,
    back_state,
    blade_cotangent,
    back_cotangent,
    blade_flux,
    back_flux,
    blade_owner,
    back_donor_cell,
    back_donor_weight,
    hole_cell,
    hole_owner,
    blade_donor_cell,
    blade_donor_weight,
):
    shape = jax.ShapeDtypeStruct
    blade = blade_state.reshape(5, WRAP * WALL, CHORD)
    cot = blade_cotangent.reshape(5, WRAP * WALL, CHORD)
    matrices = jnp.concatenate([blade_flux, back_flux]).reshape(6, 25)
    owners = (blade_owner.reshape(2, 1, RIMS), hole_owner.reshape(2, 1, HOLES))
    tables = (back_donor_cell, back_donor_weight, blade_donor_cell, blade_donor_weight)

    cot_planes, *edges = run(
        edge_kernel,
        (blade, blade, cot, cot, back_cotangent),
        [PLANES] + edge_shapes(2 * WALL),
        blocks=[plane_block(0), plane_block(WRAP - 1)] * 2 + [VMEM],
    )
    cot_halo = exchange(edges)
    send, back_planes = run(
        start_kernel,
        (blade, back_state) + tables,
        [shape((DEVS, 2, DEVS), F32), PLANES],
        DONOR_PARTS + [pltpu.VMEM((5, QH, DEVS), F32), pltpu.VMEM((5, QR, DEVS), F32)],
        flops=5 * 10**9,
    )
    recv = swap(send)
    lin_send, blade_fields, back_fields, rim_rank, hole_rank = run(
        cot_kernel,
        (matrices, cot, cot_planes, *cot_halo, *owners, hole_cell),
        [
            shape((DEVS, 8, DEVS), F32),
            shape((FIELDS, WRAP * WALL, CHORD), F32),
            shape((FIELDS, VERT, DEVS), F32),
            shape((2, 1, RIMS), jnp.int32),
            shape((2, 1, HOLES), jnp.int32),
        ],
        scalars=1,
        flops=2 * 10**9,
    )
    lin_recv = swap(lin_send)
    slots = (*owners, rim_rank, hole_rank, hole_cell)
    blade_first, back_first, *edges = run(
        fill_kernel,
        (blade, back_planes, recv) + slots,
        [BLADE, PLANES] + edge_shapes(16),
        flops=10**9,
    )
    first_halo = exchange(edges)
    blade_mid, back_mid, *edges = run(
        middle_kernel,
        (matrices, blade_first, back_first, *cot_halo[:2], *first_halo, blade_fields, back_fields)
        + (lin_recv,)
        + tables
        + (hole_cell,),
        [BLADE, PLANES] + edge_shapes(WALL + 8),
        [pltpu.VMEM(BLADE.shape, F32), pltpu.VMEM(PLANES.shape, F32)]
        + DONOR_PARTS
        + [pltpu.VMEM((FIELDS, QH, DEVS), F32), pltpu.VMEM((FIELDS, QR, DEVS), F32)]
        + SUMS,
        scalars=1,
        flops=10**10,
    )
    mid_halo = exchange(edges)
    parts = run(
        inner_kernel,
        (matrices, blade_first, back_first, blade_mid, back_mid, hole_cell),
        [BLADE, PLANES, shape((HALF, DEVS), F32)],
        scalars=1,
        flops=10**9,
    )
    send, blade_kept, back_kept = run(
        last_kernel,
        (matrices, blade_first, back_first, *parts, *mid_halo) + slots,
        [shape((DEVS, 2, DEVS), F32), BLADE, PLANES],
        scalars=1,
        flops=10**9,
    )
    recv = swap(send)
    blade_last, back_last = run(
        end_kernel,
        (blade_kept, back_kept, recv) + tables,
        [BLADE, shape((5, EAST, NORTH * VERT), F32)],
        [pltpu.VMEM((5, QH, DEVS), F32), pltpu.VMEM((5, QR, DEVS), F32)] + SUMS,
        flops=5 * 10**9,
    )
    return (blade_last.reshape(blade_state.shape), back_last)


def solution(mesh):
    return jax.shard_map(
        body,
        mesh=mesh,
        in_specs=(
            P(None, "gx", "gy"),
            P(None, "gx", "gy"),
            P(None, "gx", "gy"),
            P(None, "gx", "gy"),
            P(),
            P(),
            P(None, ("gx", "gy"), None),
            P(None, ("gx", "gy")),
            P(None, None, ("gx", "gy")),
            P(None, ("gx", "gy")),
            P(None, ("gx", "gy"), None),
            P(None, ("gx", "gy")),
            P(None, None, ("gx", "gy")),
        ),
        out_specs=(P(None, "gx", "gy"), P(None, "gx", "gy")),
        check_vma=False,
    )
```

```python
import jax
import jax.numpy as jnp
from jax import lax
from jax.experimental import pallas as pl
from jax.experimental.pallas import tpu as pltpu
from jax.sharding import PartitionSpec as P


DEVS = 128
WRAP = 4
WALL = 64
CHORD = 128
EAST = 16
NORTH = 8
VERT = 64
HALF = VERT // 2
RIMS = 1024
HOLES = 2048
QR = 2 * RIMS // DEVS
QH = 2 * HOLES // DEVS
FIELDS = 17

time_step = 0.2
damping = 0.1

F32 = jnp.float32
BF16 = jnp.bfloat16


def split(x):
    hi = x.astype(BF16)
    return hi, (x - hi.astype(F32)).astype(BF16)


def dot_nn(a, b):
    return lax.dot_general(a, b, (((1,), (0,)), ((), ())), preferred_element_type=F32)


def dot_nt(a, b):
    return lax.dot_general(a, b, (((1,), (1,)), ((), ())), preferred_element_type=F32)


def iota(shape, dim):
    return lax.broadcasted_iota(jnp.int32, shape, dim)


def one_hot(rows, index):
    return jnp.where(iota((rows, index.shape[1]), 0) == index, 1.0, 0.0)


def pair_hot(rows, index, first, second):
    position = iota((rows, index.shape[1]), 0)
    return jnp.where(position == index, first, jnp.where(position == index + 1, second, 0.0))


def lane_roll(x, amount):
    amount = amount % x.shape[-1]
    return pltpu.roll(x, amount, x.ndim - 1) if amount else x


def to_planes(block):
    rows = [block[:, y * VERT : (y + 1) * VERT] for y in range(NORTH)]
    return jnp.concatenate(rows, axis=0).T


def from_planes(field):
    turned = field.T
    return [turned[y * EAST : (y + 1) * EAST, :] for y in range(NORTH)]


def donor_parts(weights):
    w = [weights[corner : corner + 1, :] for corner in range(8)]
    x0 = (w[0] + w[1]) + (w[2] + w[3])
    x1 = (w[4] + w[5]) + (w[6] + w[7])
    y0 = (w[0] + w[1]) + (w[4] + w[5])
    y1 = (w[2] + w[3]) + (w[6] + w[7])
    z0 = (w[0] + w[2]) + (w[4] + w[6])
    z1 = (w[1] + w[3]) + (w[5] + w[7])
    return x0, x1, y0, y1, z0, z1


def short_marks(size, index):
    position = iota((size, index.shape[1]), 0).astype(jnp.int16)
    return position == index.astype(jnp.int16), position == (index + 1).astype(jnp.int16)


def pair_split(marks, first, second):
    (first_hi, first_lo), (second_hi, second_lo) = split(first), split(second)
    zero = jnp.zeros((), BF16)

    def place(a, b):
        return jnp.where(marks[0], a, jnp.where(marks[1], b, zero))

    return place(first_hi, second_hi), place(first_lo, second_lo)


def donor_rows(outer, outer_index, outer_pair, inner, inner_index, inner_pair):
    hot = pair_hot(outer, outer_index, *outer_pair)
    marks = short_marks(inner, inner_index)
    parts = [
        pair_split(marks, hot[n : n + 1, :] * inner_pair[0], hot[n : n + 1, :] * inner_pair[1])
        for n in range(outer)
    ]
    return tuple(jnp.concatenate([p[k] for p in parts], axis=0) for k in range(2))


def blade_donors(base, weights):
    x0, x1, y0, y1, z0, z1 = donor_parts(weights)
    wall = (base >> 7) & (WALL - 1)
    rows = donor_rows(WRAP, base >> 13, (x0, x1), WALL, wall, (y0, y1))
    return rows, (CHORD, base & (CHORD - 1), z0, z1)


def back_donors(base, weights):
    x0, x1, y0, y1, z0, z1 = donor_parts(weights)
    north = (base >> 6) & (NORTH - 1)
    rows = donor_rows(NORTH, north, (y0, y1), EAST, base >> 9, (x0, x1))
    return rows, (HALF, (base & (VERT - 1)) - HALF, z0, z1)


def triple_rows(rows):
    hi, lo = rows
    return jnp.concatenate([hi, lo, hi], axis=0)


def triple_lanes(rows):
    hi, lo = rows
    return jnp.concatenate([hi, hi, lo], axis=1)


def store_parts(target, place, size, field):
    hi, lo = split(field)
    rows = slice(place, place + size)
    target[rows, :] = jnp.concatenate([hi, hi, lo], axis=1)


def picked(parts, rows, cols):
    size = cols[0]
    hot = pair_hot(*cols)
    table = dot_nn(parts[...], triple_rows(rows))
    return [
        jnp.sum(table[c * size : (c + 1) * size] * hot, axis=0, keepdims=True) for c in range(5)
    ]


def spread_terms(rows, cols, mu):
    size, index, first, second = cols
    pairs = [(first * mu[c], second * mu[c]) for c in range(5)]
    tiles = {c: [] for c in range(5)}
    for start in range(0, size, 16):
        marks = short_marks(16, index - start)
        for c in range(5):
            tiles[c].append(pair_split(marks, *pairs[c]))
    hi, lo = (
        jnp.concatenate([t[k] for c in range(5) for t in tiles[c]], axis=0) for k in range(2)
    )
    return dot_nt(jnp.concatenate([hi, lo, hi], axis=1), triple_lanes(rows))


def doubled(field):
    hi, lo = split(field)
    return jnp.concatenate([hi, lo], axis=1)


def twice(marks):
    return jnp.concatenate([marks, marks], axis=0)


def wall_shift(v, up):
    position = iota(v.shape, 0)
    if up:
        return jnp.where(position == v.shape[0] - 1, 0.0, pltpu.roll(v, v.shape[0] - 1, 0))
    return jnp.where(position == 0, 0.0, pltpu.roll(v, 1, 0))


def lane_shift(v, up, width, period, fill):
    place = (iota(v.shape, 1) // width) % period
    if up:
        return jnp.where(place == period - 1, fill, lane_roll(v, -width))
    return jnp.where(place == 0, fill, lane_roll(v, width))


class Matrices:
    def __init__(self, ref, start):
        self.ref, self.start = ref, start

    def __getitem__(self, place):
        return self.ref[self.start + place[0], place[1]]


def flux_of(m_ref, t, v, scaled):
    out = []
    for c in range(5):
        total = v[1 + t] * scaled[c]
        for e in range(5):
            total = total + m_ref[t, c * 5 + e] * scaled[e]
        out.append(total)
    return out


def turned_of(m_ref, t, w):
    out = []
    for c in range(5):
        total = m_ref[t, c] * w[0]
        for e in range(1, 5):
            total = total + m_ref[t, e * 5 + c] * w[e]
        out.append(total)
    return out


PAIRS = [(0, 1), (0, 2), (0, 3), (4, 1), (4, 2), (4, 3), (1, 1), (1, 2), (1, 3), (2, 2), (2, 3), (3, 3)]


def linear_fields(m_ref, center, sides):
    base = [center[c] * (1.0 - 6.0 * damping * time_step) for c in range(5)]
    jumps = []
    for t, (upper, lower) in enumerate(sides):
        jump = [0.5 * time_step * (lower[c] - upper[c]) for c in range(5)]
        turned = turned_of(m_ref, t, jump)
        for c in range(5):
            base[c] = base[c] - turned[c] + damping * time_step * (upper[c] + lower[c])
        jumps.append(jump)
    out = list(base)
    for a, b in PAIRS:
        if a in (0, 4):
            out.append(jumps[b - 1][a])
        else:
            out.append(jumps[a - 1][b] + jumps[b - 1][a])
    return out


def apply_fields(fields, v):
    out = []
    table = {pair: 5 + n for n, pair in enumerate(PAIRS)}
    for c in range(5):
        total = fields[c]
        for e in range(5):
            key = (c, e) if (c, e) in table else (e, c)
            if key in table:
                total = total - fields[table[key]] * v[e]
        out.append(total)
    return out


def adjoint_at(m_ref, v, center, sides):
    out = [center[c] * (1.0 - 6.0 * damping * time_step) for c in range(5)]
    for t, (upper, lower) in enumerate(sides):
        jump = [0.5 * time_step * (lower[c] - upper[c]) for c in range(5)]
        turned = turned_of(m_ref, t, jump)
        inner = v[0] * jump[0]
        for e in range(1, 5):
            inner = inner + v[e] * jump[e]
        for c in range(5):
            total = turned[c] + v[1 + t] * jump[c]
            if c == 1 + t:
                total = total + inner
            out[c] = out[c] - total + damping * time_step * (upper[c] + lower[c])
    return out


def blade_sides(ref, low, high, j):
    def plane(n):
        if n < 0 or n >= WRAP:
            return low if n < 0 else high
        return [ref[c, n * WALL : (n + 1) * WALL, :] for c in range(5)]

    center, above, below = plane(j), plane(j + 1), plane(j - 1)
    wall = ([wall_shift(v, True) for v in center], [wall_shift(v, False) for v in center])
    span = (
        [lane_shift(v, True, 1, CHORD, 0.0) for v in center],
        [lane_shift(v, False, 1, CHORD, 0.0) for v in center],
    )
    return center, [(above, below), wall, span]


def back_sides(center, halo):
    east = (
        [lane_shift(v, True, 1, EAST, halo[1][c]) for c, v in enumerate(center)],
        [lane_shift(v, False, 1, EAST, halo[0][c]) for c, v in enumerate(center)],
    )
    north = (
        [lane_shift(v, True, EAST, NORTH, halo[3][c]) for c, v in enumerate(center)],
        [lane_shift(v, False, EAST, NORTH, halo[2][c]) for c, v in enumerate(center)],
    )
    vert = ([wall_shift(v, True) for v in center], [wall_shift(v, False) for v in center])
    return [east, north, vert]


def pack_east(v, x):
    lane = iota((8, DEVS), 1)
    out = jnp.zeros((8, DEVS), F32)
    for g in range(8):
        out = jnp.where(lane % EAST == g, lane_roll(v[g * 8 : g * 8 + 8, :], g - x), out)
    return out


def unpack_east(v, x):
    return jnp.concatenate([lane_roll(v, x - g) for g in range(8)], axis=0)


def pack_north(v, y):
    lane = iota((8, DEVS), 1)
    out = jnp.zeros((8, DEVS), F32)
    for g in range(8):
        out = jnp.where(lane // EAST == g, lane_roll(v[g * 8 : g * 8 + 8, :], (g - y) * EAST), out)
    return out


def unpack_north(v, y):
    return jnp.concatenate([lane_roll(v, (y - g) * EAST) for g in range(8)], axis=0)


def store_blade_edges(planes, rows, edges, at=0):
    even_y = lax.axis_index("gy") % 2 == 0
    first_y, second_y = edges
    count = rows.stop - rows.start
    for c in range(5):
        low, high = (plane[c, rows, :] for plane in planes)
        first_y[c, at : at + count, :] = jnp.where(even_y, high, low)
        second_y[c, at : at + count, :] = jnp.where(even_y, low, high)


def store_back_edges(back, edges, at):
    first_y, second_y, first_x, second_x = edges
    even_y = lax.axis_index("gy") % 2 == 0
    even_x = lax.axis_index("gx") % 2 == 0
    for c in range(5):
        high, low = pack_north(back[c], NORTH - 1), pack_north(back[c], 0)
        first_y[c, at : at + 8, :] = jnp.where(even_y, high, low)
        second_y[c, at : at + 8, :] = jnp.where(even_y, low, high)
        high, low = pack_east(back[c], EAST - 1), pack_east(back[c], 0)
        first_x[c] = jnp.where(even_x, high, low)
        second_x[c] = jnp.where(even_x, low, high)


def edge_shapes(rows):
    ends = jax.ShapeDtypeStruct((5, rows, CHORD), F32)
    sides = jax.ShapeDtypeStruct((5, 8, DEVS), F32)
    return [ends, ends, sides, sides]


def read_ends(first_y, second_y, rows):
    even_y = lax.axis_index("gy") % 2 == 0
    both = [(first_y[c, rows, :], second_y[c, rows, :]) for c in range(5)]
    return [jnp.where(even_y, b, a) for a, b in both], [jnp.where(even_y, a, b) for a, b in both]


def read_back(first_y, second_y, first_x, second_x, at):
    north = lax.axis_index("gy")
    even_x = lax.axis_index("gx") % 2 == 0
    keep_low = jnp.where(north > 0, 1.0, 0.0)
    keep_high = jnp.where(north < DEVS // 8 - 1, 1.0, 0.0)
    below, above = read_ends(first_y, second_y, slice(at, at + 8))
    both = [(first_x[c], second_x[c]) for c in range(5)]
    east = [unpack_east(jnp.where(even_x, a, b), EAST - 1) for a, b in both]
    west = [unpack_east(jnp.where(even_x, b, a), 0) for a, b in both]
    south = [unpack_north(v * keep_low, 0) for v in below]
    upper = [unpack_north(v * keep_high, NORTH - 1) for v in above]
    return [west, east, south, upper]


def exchange(edges):
    gx, gy = lax.axis_size("gx"), lax.axis_size("gy")

    def pairs(start, stop, count):
        there = [(i, (i + 1) % count) for i in range(start, stop, 2)]
        return there + [(b, a) for a, b in there]

    first_y, second_y, first_x, second_x = edges
    got_y = lax.ppermute(first_y, "gy", pairs(0, gy, gy))
    got_x = lax.ppermute(first_x, "gx", pairs(0, gx, gx))
    got_x2 = lax.ppermute(second_x, "gx", pairs(1, gx - 1, gx))
    got_y2 = lax.ppermute(second_y, "gy", pairs(1, gy, gy))
    return got_y, got_y2, got_x, got_x2


def regroup(pieces, width):
    count = DEVS // width
    shape = next(piece.shape for piece in pieces if piece is not None)
    block = iota(shape, 1) // width
    out = []
    for b in range(count):
        total = jnp.zeros(shape, F32)
        for a in range(count):
            if pieces[a] is not None:
                total = jnp.where(block == a, lane_roll(pieces[a], (a - b) * width), total)
        out.append(total)
    return out


def ranks_of(owner_ref, out_ref):
    count = owner_ref.shape[1]
    earlier = jnp.where(iota((256, 256), 0) < iota((256, 256), 1), 1.0, 0.0).astype(BF16)
    carry = jnp.zeros((DEVS, 1), F32)
    for start in range(0, count, 256):
        marks = one_hot(DEVS, owner_ref[:, start : start + 256])
        before = dot_nn(marks.astype(BF16), earlier) + carry
        out_ref[:, start : start + 256] = jnp.sum(marks * before, axis=0, keepdims=True).astype(
            jnp.int32
        )
        carry = carry + jnp.sum(marks, axis=1, keepdims=True)


def seat_terms(slots, index, values):
    here = iota((slots, index.shape[1]), 0).astype(jnp.int16) == index.astype(jnp.int16)
    zero = jnp.zeros((), BF16)
    parts = [[jnp.where(here, part, zero) for part in split(v)] for v in values]
    hi, lo = (jnp.concatenate([p[k] for p in parts], axis=0) for k in range(2))
    return jnp.concatenate([hi, lo], axis=1)


def send_rows(values, owner, rank, slots):
    marks = one_hot(DEVS, owner).astype(BF16)
    return dot_nt(seat_terms(slots, rank, values), jnp.concatenate([marks, marks], axis=1))


def hole_parts(cell):
    row = ((cell >> 6) & (NORTH - 1)) * EAST + (cell >> 9)
    return row, cell & (VERT - 1)


def hole_values(low_half, cell):
    row, vert = hole_parts(cell)
    seats = one_hot(HALF, vert)
    table = dot_nn(low_half, twice(one_hot(DEVS, row).astype(BF16)))
    return [
        jnp.sum(table[n : n + HALF] * seats, axis=0, keepdims=True)
        for n in range(0, table.shape[0], HALF)
    ]


def hole_mask(cell_ref):
    total = jnp.zeros((HALF, DEVS), F32)
    for start in range(0, HOLES, 512):
        row, vert = hole_parts(cell_ref[:, start : start + 512])
        total = total + dot_nt(one_hot(HALF, vert).astype(BF16), one_hot(DEVS, row).astype(BF16))
    return total


CHUNK = 512


def chunk_lanes(n):
    return pl.ds(pl.multiple_of(n * CHUNK, CHUNK), CHUNK)


def lanes_of(ref, n, k):
    count = CHUNK // DEVS
    return jnp.concatenate([ref[k, pl.ds(n * count + m, 1), :] for m in range(count)], axis=1)


def store_chunk(out, n, values):
    for c in range(5):
        for m in range(CHUNK // DEVS):
            row = pl.ds(n * (CHUNK // DEVS) + m, 1)
            out[c, row, :] = values[c][:, m * DEVS : (m + 1) * DEVS]


def outer_planes(ref):
    return ref.at[:, :WALL, :], ref.at[:, (WRAP - 1) * WALL :, :]


def edge_kernel(
    blade_low, blade_high, cot_low, cot_high, back_cot,
    cot_planes, first_y, second_y, first_x, second_x,
):
    cots = []
    for c in range(5):
        turned = to_planes(back_cot[c])
        cot_planes[c] = turned
        cots.append(turned)
    store_blade_edges((cot_low, cot_high), slice(0, WALL), (first_y, second_y))
    store_blade_edges((blade_low, blade_high), slice(0, WALL - 8), (first_y, second_y), WALL + 8)
    store_back_edges(cots, (first_y, second_y, first_x, second_x), WALL)


def start_kernel(
    blade, back, back_base, back_weight, blade_base, blade_weight,
    send, back_planes,
    blade_parts, back_parts, hole_vals, rim_vals,
):
    for c in range(5):
        store_parts(blade_parts, c * CHORD, CHORD, blade[c].T)
        field = to_planes(back[c])
        back_planes[c] = field
        store_parts(back_parts, c * HALF, HALF, field[HALF:, :])

    def blade_step(n, carry):
        lanes = chunk_lanes(n)
        rows, cols = blade_donors(blade_base[0:1, lanes], blade_weight[0, :, lanes])
        store_chunk(hole_vals, n, picked(blade_parts, rows, cols))
        return carry

    lax.fori_loop(0, 2 * HOLES // CHUNK, blade_step, 0, unroll=4)

    def back_step(n, carry):
        lanes = chunk_lanes(n)
        rows, cols = back_donors(back_base[0:1, lanes], back_weight[0, :, lanes])
        store_chunk(rim_vals, n, picked(back_parts, rows, cols))
        return carry

    lax.fori_loop(0, 2 * RIMS // CHUNK, back_step, 0, unroll=2)
    store_slots(hole_vals, rim_vals, send)


def store_slots(hole_vals, rim_vals, send):
    first = regroup([hole_vals[c] for c in range(4)], QH)
    fifth = hole_vals[4]
    tail = regroup([fifth, None, None, None], QH)
    for d in range(DEVS // QH):
        send[pl.ds(d, QH, stride=DEVS // QH), 0, :] = first[d]
        send[pl.ds(d, QH, stride=DEVS // QH), 1, :] = tail[d]
    rims = regroup([None, None] + [rim_vals[c] for c in range(5)] + [None], QR)
    lane = iota((QR, DEVS), 1)
    for d in range(DEVS // QR):
        rows = pl.ds(d, QR, stride=DEVS // QR)
        send[rows, 1, :] = jnp.where(lane < QH, send[rows, 1, :], rims[d])


def cot_kernel(
    matrices, cot, cot_planes, got_y, got_y2, got_x, got_x2, rim_owner, hole_owner, hole_cell,
    send, blade_fields, back_fields, rim_rank, hole_rank,
):
    blade_m, back_m = Matrices(matrices, 0), Matrices(matrices, 3)
    low, high = read_ends(got_y, got_y2, slice(0, WALL))
    halo = read_back(got_y, got_y2, got_x, got_x2, WALL)
    for j in range(WRAP):
        center, sides = blade_sides(cot, low, high, j)
        fields = linear_fields(blade_m, center, sides)
        for n in range(FIELDS):
            blade_fields[n, j * WALL : (j + 1) * WALL, :] = fields[n]
    center = [cot_planes[c] for c in range(5)]
    fields = linear_fields(back_m, center, back_sides(center, halo))
    for n in range(FIELDS):
        back_fields[n] = fields[n]
    for step in range(2):
        ranks_of(rim_owner.at[step], rim_rank.at[step])
        ranks_of(hole_owner.at[step], hole_rank.at[step])

    total = jnp.zeros((FIELDS * QR, DEVS), F32)
    for j in range(WRAP):
        lanes = slice(j * 256, j * 256 + 256)
        top = j * WALL + WALL - 2
        values = [
            jnp.concatenate(
                [blade_fields[n, top + k : top + k + 1, :] for k in range(2)], axis=1
            )
            for n in range(FIELDS)
        ]
        total = total + send_rows(values, rim_owner[1, :, lanes], rim_rank[1, :, lanes], QR)
    total = jnp.concatenate([total, jnp.zeros((112, DEVS), F32)], axis=0)
    for m in range(3):
        send[:, 5 + m, :] = total[m * DEVS : (m + 1) * DEVS].T
    total = jnp.zeros((FIELDS * QH, DEVS), F32)
    low_half = doubled(jnp.concatenate([back_fields[n, :HALF, :] for n in range(FIELDS)], axis=0))
    for start in range(0, HOLES, 512):
        lanes = slice(start, start + 512)
        values = hole_values(low_half, hole_cell[1:2, lanes])
        total = total + send_rows(values, hole_owner[1, :, lanes], hole_rank[1, :, lanes], QH)
    total = jnp.concatenate([total, jnp.zeros((96, DEVS), F32)], axis=0)
    for m in range(5):
        send[:, m, :] = total[m * DEVS : (m + 1) * DEVS].T


def fill_kernel(
    blade, back_planes, recv, rim_owner, hole_owner, rim_rank, hole_rank, hole_cell,
    blade_first, back_first, first_y, second_y, first_x, second_x,
):
    arrived = doubled(jnp.concatenate([recv[:, 0, :].T, recv[:, 1, :].T], axis=0))
    for c in range(5):
        for j in range(WRAP):
            rows = slice(j * WALL, (j + 1) * WALL)
            blade_first[c, rows, :] = blade[c, rows, :]
    base = 5 * QH
    for j in range(WRAP):
        lanes = slice(j * 256, j * 256 + 256)
        marks = one_hot(DEVS, rim_owner[0, :, lanes]).astype(BF16)
        seats = one_hot(QR, rim_rank[0, :, lanes])
        table = dot_nn(arrived[base : base + 5 * QR], twice(marks))
        for c in range(5):
            value = jnp.sum(table[c * QR : (c + 1) * QR] * seats, axis=0, keepdims=True)
            for k in range(2):
                row = j * WALL + WALL - 2 + k
                blade_first[c, row : row + 1, :] = value[:, k * CHORD : (k + 1) * CHORD]
    filled = jnp.zeros((6 * HALF, DEVS), F32)
    for start in range(0, HOLES, 512):
        lanes = slice(start, start + 512)
        marks = one_hot(DEVS, hole_owner[0, :, lanes]).astype(BF16)
        seats = one_hot(QH, hole_rank[0, :, lanes])
        row, vert = hole_parts(hole_cell[0:1, lanes])
        table = dot_nn(arrived[:base], twice(marks))
        values = [
            jnp.sum(table[c * QH : (c + 1) * QH] * seats, axis=0, keepdims=True) for c in range(5)
        ]
        terms = seat_terms(HALF, vert, values + [jnp.ones(vert.shape, F32)])
        row_marks = one_hot(DEVS, row).astype(BF16)
        filled = filled + dot_nt(terms, jnp.concatenate([row_marks, row_marks], axis=1))
    mask = filled[5 * HALF :]
    backs = []
    for c in range(5):
        top = jnp.where(mask > 0.5, filled[c * HALF : (c + 1) * HALF], back_planes[c, :HALF, :])
        field = jnp.concatenate([top, back_planes[c, HALF:, :]], axis=0)
        back_first[c] = field
        backs.append(field)
    store_blade_edges(outer_planes(blade_first), slice(WALL - 8, WALL), (first_y, second_y))
    store_back_edges(backs, (first_y, second_y, first_x, second_x), 8)


def residual_step(center, halo_flux):
    out = [center[c] * (1.0 - 6.0 * damping * time_step) for c in range(5)]
    for t in range(3):
        upper, lower = halo_flux(t)
        for c in range(5):
            out[c] = out[c] - upper[c] + lower[c]
    return out


def side_terms(m_ref, t, v):
    flux = flux_of(m_ref, t, v, [0.5 * time_step * v[c] for c in range(5)])
    damped = [damping * time_step * v[c] for c in range(5)]
    upper = [flux[c] - damped[c] for c in range(5)]
    lower = [flux[c] + damped[c] for c in range(5)]
    return upper, lower


def middle_kernel(
    matrices, blade_first, back_first, old_y, old_y2, got_y, got_y2, got_x, got_x2,
    blade_fields, back_fields, recv, back_base, back_weight, blade_base, blade_weight, hole_cell,
    blade_mid, back_mid, first_y, second_y, first_x, second_x,
    blade_next, back_next, blade_parts, back_parts, hole_lin, rim_lin, blade_acc, back_acc,
):
    blade_m, back_m = Matrices(matrices, 0), Matrices(matrices, 3)
    planes = zip(
        read_ends(old_y, old_y2, slice(WALL + 8, 2 * WALL)), read_ends(got_y, got_y2, slice(0, 8))
    )
    low, high = (
        [jnp.concatenate([a, b], axis=0) for a, b in zip(inner, outer)] for inner, outer in planes
    )
    halo = read_back(got_y, got_y2, got_x, got_x2, 8)

    sections = [low]
    for j in range(WRAP):
        sections.append([blade_first[c, j * WALL : (j + 1) * WALL, :] for c in range(5)])
    sections.append(high)
    turns = [side_terms(blade_m, 0, plane) for plane in sections]
    for j in range(WRAP):
        center = sections[j + 1]

        def around(t, j=j, center=center):
            if t == 0:
                return turns[j + 2][0], turns[j][1]
            upper, lower = side_terms(blade_m, t, center)
            if t == 1:
                return [wall_shift(v, True) for v in upper], [wall_shift(v, False) for v in lower]
            return (
                [lane_shift(v, True, 1, CHORD, 0.0) for v in upper],
                [lane_shift(v, False, 1, CHORD, 0.0) for v in lower],
            )

        out = residual_step(center, around)
        for c in range(5):
            blade_next[c, j * WALL : (j + 1) * WALL, :] = out[c]
    center = [back_first[c] for c in range(5)]

    def across(t):
        upper, lower = side_terms(back_m, t, center)
        if t == 2:
            return [wall_shift(v, True) for v in upper], [wall_shift(v, False) for v in lower]
        width, period = ((1, EAST), (EAST, NORTH))[t]
        below = side_terms(back_m, t, halo[2 * t])[1]
        above = side_terms(back_m, t, halo[2 * t + 1])[0]
        return (
            [lane_shift(upper[c], True, width, period, above[c]) for c in range(5)],
            [lane_shift(lower[c], False, width, period, below[c]) for c in range(5)],
        )

    out = residual_step(center, across)
    for c in range(5):
        back_next[c] = out[c]
        store_parts(back_parts, c * HALF, HALF, out[c][HALF:, :])
        store_parts(blade_parts, c * CHORD, CHORD, blade_next[c].T)

    for j in range(WRAP):
        rows = slice(j * WALL, (j + 1) * WALL)
        v = [blade_next[c, rows, :] for c in range(5)]
        own = apply_fields([blade_fields[n, rows, :] for n in range(FIELDS)], v)
        inside = iota((WALL, CHORD), 0) < WALL - 2
        for c in range(5):
            blade_mid[c, rows, :] = jnp.where(inside, own[c], 0.0)
    mask = hole_mask(hole_cell.at[1:2])
    own = apply_fields([back_fields[n] for n in range(FIELDS)], [back_next[c] for c in range(5)])
    for c in range(5):
        back_mid[c, :HALF, :] = jnp.where(mask > 0.5, 0.0, own[c][:HALF, :])
        back_mid[c, HALF:, :] = own[c][HALF:, :]

    for m in range(5):
        pieces = [recv[pl.ds(d, QH, stride=DEVS // QH), m, :] for d in range(DEVS // QH)]
        for b, piece in enumerate(regroup(pieces, QH)):
            if m * 4 + b < FIELDS:
                hole_lin[m * 4 + b] = piece
    for m in range(3):
        pieces = [recv[pl.ds(d, QR, stride=DEVS // QR), 5 + m, :] for d in range(DEVS // QR)]
        for b, piece in enumerate(regroup(pieces, QR)):
            if m * 8 + b < FIELDS:
                rim_lin[m * 8 + b] = piece

    blade_acc[...] = jnp.zeros(blade_acc.shape, F32)
    back_acc[...] = jnp.zeros(back_acc.shape, F32)

    def blade_step(n, carry):
        lanes = chunk_lanes(n)
        rows, cols = blade_donors(blade_base[1:2, lanes], blade_weight[1, :, lanes])
        value = picked(blade_parts, rows, cols)
        mu = apply_fields([lanes_of(hole_lin, n, k) for k in range(FIELDS)], value)
        blade_acc[...] += spread_terms(rows, cols, mu)
        return carry

    lax.fori_loop(0, 2 * HOLES // CHUNK, blade_step, 0, unroll=4)

    def back_step(n, carry):
        lanes = chunk_lanes(n)
        rows, cols = back_donors(back_base[1:2, lanes], back_weight[1, :, lanes])
        value = picked(back_parts, rows, cols)
        mu = apply_fields([lanes_of(rim_lin, n, k) for k in range(FIELDS)], value)
        back_acc[...] += spread_terms(rows, cols, mu)
        return carry

    lax.fori_loop(0, 2 * RIMS // CHUNK, back_step, 0, unroll=2)
    for c in range(5):
        blade_mid[c] = blade_mid[c] + blade_acc[c * CHORD : (c + 1) * CHORD, :].T
        back_mid[c, HALF:, :] = back_mid[c, HALF:, :] + back_acc[c * HALF : (c + 1) * HALF, :]
    store_blade_edges(outer_planes(blade_mid), slice(0, WALL), (first_y, second_y))
    store_back_edges(
        [back_mid[c] for c in range(5)], (first_y, second_y, first_x, second_x), WALL
    )


def inner_kernel(
    matrices, blade_first, back_first, blade_mid, back_mid, hole_cell, blade_part, back_part, mask
):
    blade_m, back_m = Matrices(matrices, 0), Matrices(matrices, 3)
    nothing = [jnp.zeros((WALL, CHORD), F32)] * 5
    for j in range(WRAP):
        rows = slice(j * WALL, (j + 1) * WALL)
        center, sides = blade_sides(blade_mid, nothing, nothing, j)
        out = adjoint_at(blade_m, [blade_first[c, rows, :] for c in range(5)], center, sides)
        for c in range(5):
            blade_part[c, rows, :] = out[c]
    nothing = [jnp.zeros((VERT, DEVS), F32)] * 5
    center = [back_mid[c] for c in range(5)]
    sides = back_sides(center, [nothing] * 4)
    out = adjoint_at(back_m, [back_first[c] for c in range(5)], center, sides)
    for c in range(5):
        back_part[c] = out[c]
    mask[...] = hole_mask(hole_cell.at[0:1])


def outside_terms(m_ref, t, v, beyond, sign):
    jump = [-sign * 0.5 * time_step * beyond[c] for c in range(5)]
    turned = turned_of(m_ref, t, jump)
    inner = v[0] * jump[0]
    for e in range(1, 5):
        inner = inner + v[e] * jump[e]
    out = []
    for c in range(5):
        total = turned[c] + v[1 + t] * jump[c]
        if c == 1 + t:
            total = total + inner
        out.append(damping * time_step * beyond[c] - total)
    return out


def last_kernel(
    matrices, blade_first, back_first, blade_part, back_part, mask,
    got_y, got_y2, got_x, got_x2,
    rim_owner, hole_owner, rim_rank, hole_rank, hole_cell,
    send, blade_kept, back_kept,
):
    blade_m, back_m = Matrices(matrices, 0), Matrices(matrices, 3)
    low, high = read_ends(got_y, got_y2, slice(0, WALL))
    halo = read_back(got_y, got_y2, got_x, got_x2, WALL)
    rims = jnp.zeros((5 * QR, DEVS), F32)
    for j in range(WRAP):
        rows = slice(j * WALL, (j + 1) * WALL)
        out = [blade_part[c, rows, :] for c in range(5)]
        if j in (0, WRAP - 1):
            v = [blade_first[c, rows, :] for c in range(5)]
            beyond, sign = (high, 1.0) if j else (low, -1.0)
            more = outside_terms(blade_m, 0, v, beyond, sign)
            out = [out[c] + more[c] for c in range(5)]
        inside = iota((WALL, CHORD), 0) < WALL - 2
        values = []
        for c in range(5):
            blade_kept[c, rows, :] = jnp.where(inside, out[c], 0.0)
            outer = [out[c][WALL - 2 + k : WALL - 1 + k, :] for k in range(2)]
            values.append(jnp.concatenate(outer, axis=1))
        lanes = slice(j * 256, j * 256 + 256)
        rims = rims + send_rows(values, rim_owner[0, :, lanes], rim_rank[0, :, lanes], QR)
    v = [back_first[c] for c in range(5)]
    out = [back_part[c] for c in range(5)]
    place = iota((VERT, DEVS), 1)
    east, north = place % EAST, place // EAST
    for t, beyond, sign, at in (
        (0, halo[0], -1.0, east == 0),
        (0, halo[1], 1.0, east == EAST - 1),
        (1, halo[2], -1.0, north == 0),
        (1, halo[3], 1.0, north == NORTH - 1),
    ):
        more = outside_terms(back_m, t, v, [jnp.where(at, x, 0.0) for x in beyond], sign)
        out = [out[c] + more[c] for c in range(5)]
    holes_here = mask[...] > 0.5
    for c in range(5):
        back_kept[c, :HALF, :] = jnp.where(holes_here, 0.0, out[c][:HALF, :])
        back_kept[c, HALF:, :] = out[c][HALF:, :]
    holes = jnp.zeros((5 * QH, DEVS), F32)
    low_half = doubled(jnp.concatenate([out[c][:HALF, :] for c in range(5)], axis=0))
    for start in range(0, HOLES, 512):
        lanes = slice(start, start + 512)
        values = hole_values(low_half, hole_cell[0:1, lanes])
        holes = holes + send_rows(values, hole_owner[0, :, lanes], hole_rank[0, :, lanes], QH)
    rest = jnp.zeros((2 * DEVS - 5 * QH - 5 * QR, DEVS), F32)
    total = jnp.concatenate([holes, rims, rest], axis=0)
    send[:, 0, :] = total[:DEVS].T
    send[:, 1, :] = total[DEVS:].T


def end_kernel(
    blade_kept, back_kept, recv, back_base, back_weight, blade_base, blade_weight,
    blade_out, back_out, hole_mu, rim_mu, blade_acc, back_acc,
):
    count = DEVS // QH
    pieces = [recv[pl.ds(d, QH, stride=count), 0, :] for d in range(count)]
    for c, piece in enumerate(regroup(pieces, QH)):
        hole_mu[c] = piece
    pieces = [recv[pl.ds(d, QH, stride=count), 1, :] for d in range(count)]
    hole_mu[4] = regroup(pieces, QH)[0]
    count = DEVS // QR
    pieces = [recv[pl.ds(d, QR, stride=count), 1, :] for d in range(count)]
    groups = regroup(pieces, QR)
    for c in range(5):
        rim_mu[c] = groups[QH // QR + c]
    blade_acc[...] = jnp.zeros(blade_acc.shape, F32)
    back_acc[...] = jnp.zeros(back_acc.shape, F32)

    def blade_step(n, carry):
        lanes = chunk_lanes(n)
        rows, cols = blade_donors(blade_base[0:1, lanes], blade_weight[0, :, lanes])
        blade_acc[...] += spread_terms(rows, cols, [lanes_of(hole_mu, n, c) for c in range(5)])
        return carry

    lax.fori_loop(0, 2 * HOLES // CHUNK, blade_step, 0, unroll=4)

    def back_step(n, carry):
        lanes = chunk_lanes(n)
        rows, cols = back_donors(back_base[0:1, lanes], back_weight[0, :, lanes])
        back_acc[...] += spread_terms(rows, cols, [lanes_of(rim_mu, n, c) for c in range(5)])
        return carry

    lax.fori_loop(0, 2 * RIMS // CHUNK, back_step, 0, unroll=2)
    for c in range(5):
        blade_out[c] = blade_kept[c] + blade_acc[c * CHORD : (c + 1) * CHORD, :].T
        top = back_kept[c, HALF:, :] + back_acc[c * HALF : (c + 1) * HALF, :]
        parts = from_planes(jnp.concatenate([back_kept[c, :HALF, :], top], axis=0))
        for y in range(0, NORTH, 2):
            back_out[c, :, y * VERT : (y + 2) * VERT] = jnp.concatenate(parts[y : y + 2], axis=1)


VMEM = pl.BlockSpec(memory_space=pltpu.VMEM)
SMEM = pl.BlockSpec(memory_space=pltpu.SMEM)
BLADE = jax.ShapeDtypeStruct((5, WRAP * WALL, CHORD), F32)
PLANES = jax.ShapeDtypeStruct((5, VERT, DEVS), F32)
DONOR_PARTS = [
    pltpu.VMEM((5 * CHORD, 3 * WRAP * WALL), BF16),
    pltpu.VMEM((5 * HALF, 3 * DEVS), BF16),
]
SUMS = [pltpu.VMEM((5 * CHORD, WRAP * WALL), F32), pltpu.VMEM((5 * HALF, DEVS), F32)]


def plane_block(j):
    return pl.BlockSpec((5, WALL, CHORD), lambda _: (0, j, 0))


def run(kernel, args, out_shape, scratch=(), scalars=0, flops=0, blocks=None):
    size = sum(4 * a.size for a in args) + sum(4 * o.size for o in out_shape)
    return pl.pallas_call(
        kernel,
        grid=(1,) if blocks else (),
        out_shape=list(out_shape),
        in_specs=blocks or [SMEM] * scalars + [VMEM] * (len(args) - scalars),
        out_specs=[VMEM] * len(out_shape),
        scratch_shapes=list(scratch),
        cost_estimate=pl.CostEstimate(flops=flops, bytes_accessed=size, transcendentals=0),
    )(*args)


def swap(rows):
    return lax.all_to_all(rows, ("gx", "gy"), split_axis=0, concat_axis=0, tiled=True)


def body(
    blade_state,
    back_state,
    blade_cotangent,
    back_cotangent,
    blade_flux,
    back_flux,
    blade_owner,
    back_donor_cell,
    back_donor_weight,
    hole_cell,
    hole_owner,
    blade_donor_cell,
    blade_donor_weight,
):
    shape = jax.ShapeDtypeStruct
    blade = blade_state.reshape(5, WRAP * WALL, CHORD)
    cot = blade_cotangent.reshape(5, WRAP * WALL, CHORD)
    matrices = jnp.concatenate([blade_flux, back_flux]).reshape(6, 25)
    owners = (blade_owner.reshape(2, 1, RIMS), hole_owner.reshape(2, 1, HOLES))
    tables = (back_donor_cell, back_donor_weight, blade_donor_cell, blade_donor_weight)

    cot_planes, *edges = run(
        edge_kernel,
        (blade, blade, cot, cot, back_cotangent),
        [PLANES] + edge_shapes(2 * WALL),
        blocks=[plane_block(0), plane_block(WRAP - 1)] * 2 + [VMEM],
    )
    cot_halo = exchange(edges)
    send, back_planes = run(
        start_kernel,
        (blade, back_state) + tables,
        [shape((DEVS, 2, DEVS), F32), PLANES],
        DONOR_PARTS + [pltpu.VMEM((5, QH, DEVS), F32), pltpu.VMEM((5, QR, DEVS), F32)],
        flops=5 * 10**9,
    )
    recv = swap(send)
    lin_send, blade_fields, back_fields, rim_rank, hole_rank = run(
        cot_kernel,
        (matrices, cot, cot_planes, *cot_halo, *owners, hole_cell),
        [
            shape((DEVS, 8, DEVS), F32),
            shape((FIELDS, WRAP * WALL, CHORD), F32),
            shape((FIELDS, VERT, DEVS), F32),
            shape((2, 1, RIMS), jnp.int32),
            shape((2, 1, HOLES), jnp.int32),
        ],
        scalars=1,
        flops=2 * 10**9,
    )
    lin_recv = swap(lin_send)
    slots = (*owners, rim_rank, hole_rank, hole_cell)
    blade_first, back_first, *edges = run(
        fill_kernel,
        (blade, back_planes, recv) + slots,
        [BLADE, PLANES] + edge_shapes(16),
        flops=10**9,
    )
    first_halo = exchange(edges)
    blade_mid, back_mid, *edges = run(
        middle_kernel,
        (matrices, blade_first, back_first, *cot_halo[:2], *first_halo, blade_fields, back_fields)
        + (lin_recv,)
        + tables
        + (hole_cell,),
        [BLADE, PLANES] + edge_shapes(WALL + 8),
        [pltpu.VMEM(BLADE.shape, F32), pltpu.VMEM(PLANES.shape, F32)]
        + DONOR_PARTS
        + [pltpu.VMEM((FIELDS, QH, DEVS), F32), pltpu.VMEM((FIELDS, QR, DEVS), F32)]
        + SUMS,
        scalars=1,
        flops=10**10,
    )
    mid_halo = exchange(edges)
    parts = run(
        inner_kernel,
        (matrices, blade_first, back_first, blade_mid, back_mid, hole_cell),
        [BLADE, PLANES, shape((HALF, DEVS), F32)],
        scalars=1,
        flops=10**9,
    )
    send, blade_kept, back_kept = run(
        last_kernel,
        (matrices, blade_first, back_first, *parts, *mid_halo) + slots,
        [shape((DEVS, 2, DEVS), F32), BLADE, PLANES],
        scalars=1,
        flops=10**9,
    )
    recv = swap(send)
    blade_last, back_last = run(
        end_kernel,
        (blade_kept, back_kept, recv) + tables,
        [BLADE, shape((5, EAST, NORTH * VERT), F32)],
        [pltpu.VMEM((5, QH, DEVS), F32), pltpu.VMEM((5, QR, DEVS), F32)] + SUMS,
        flops=5 * 10**9,
    )
    return (blade_last.reshape(blade_state.shape), back_last)


def solution(mesh):
    return jax.shard_map(
        body,
        mesh=mesh,
        in_specs=(
            P(None, "gx", "gy"),
            P(None, "gx", "gy"),
            P(None, "gx", "gy"),
            P(None, "gx", "gy"),
            P(),
            P(),
            P(None, ("gx", "gy"), None),
            P(None, ("gx", "gy")),
            P(None, None, ("gx", "gy")),
            P(None, ("gx", "gy")),
            P(None, ("gx", "gy"), None),
            P(None, ("gx", "gy")),
            P(None, None, ("gx", "gy")),
        ),
        out_specs=(P(None, "gx", "gy"), P(None, "gx", "gy")),
        check_vma=False,
    )
```
